256 devices in a mesh: dp: 32 (over y, z_lo, core), tm: 8 (over x, z_hi).
Axes of the slice: x: 4, y: 4, z: 8 (z_hi: 2, z_lo: 4; z = z_hi * 4 + z_lo), core: 2. Of those that a mesh axis runs over, the one named last changes fastest.
Arguments:
- frames_in: bfloat16 [32, 16, 10, 16, 512], P('dp', 'tm'), may hold values from -6 to 6
- cotangent: bfloat16 [32, 32, 10, 16, 512], P('dp', 'tm'), may hold values from -6 to 6
- w_spatial: bfloat16 [9, 512, 512], P(None, 'dp'), may hold values from -0.09375 to 0.09375
- w_temporal: bfloat16 [3, 512, 512], P(None, 'dp'), may hold values from -0.15625 to 0.15625
Outputs:
- decoded: bfloat16 [32, 32, 10, 16, 512], P('dp', 'tm')
- grad_input: bfloat16 [32, 16, 10, 16, 512], P('dp', 'tm')
- grad_spatial: float32 [9, 512, 512], P(None, 'dp')
- grad_temporal: float32 [3, 512, 512], P(None, 'dp')
The draws below stay inside these ranges and needn't reach their ends.
All inputs are finite; a program needn't handle non-finite values.
Results may differ from the reference program's by a relative error of at most 0.0051.
Values may be sent and summed in bfloat16 or wider, within the bound.
No kernel may reach another device: no remote copies, remote signals or barrier semaphores. Data moves between devices by JAX's collectives and lax.ppermute only.
A program may use at most 192 MiB of HBM per device.

```python
import math
import jax
import jax.numpy as jnp
from jax import lax

C = 512
ROWS = 10
COLS = 16
CLIPS = 32
FRAMES = 16
OUT_FRAMES = 32


def level_of(stream_key, extent, pieces, smallest, top_value):
    gain = 1.0
    for dim, shards_of in pieces:
        steps = jax.random.uniform(jax.random.fold_in(jax.random.fold_in(stream_key, 6), dim), (shards_of,), jnp.float32, smallest / len(pieces), top_value / len(pieces))
        gain = gain * jnp.repeat(jnp.exp(steps), extent[dim] // shards_of).reshape((-1,) + (1,) * (len(extent) - 1 - dim))
    return gain


def centred(key, dims, scale, bound, cuts=(), held_as=jnp.bfloat16):
    entries = scale * jax.random.normal(key, dims, jnp.float32)
    if cuts:
        entries = entries * level_of(key, dims, cuts, -0.22, 0.18)
    return jnp.clip(entries, -bound, bound).astype(held_as)


def setup_inputs(seed: int = 0) -> dict:
    streams_of = jax.random.split(jax.random.key(seed), 5)
    frames_in = centred(streams_of[0], (CLIPS, FRAMES, ROWS, COLS, C), 1.0, 6.0, ((0, 32), (1, 8)))
    cotangent = centred(streams_of[1], (CLIPS, OUT_FRAMES, ROWS, COLS, C), 1.0, 6.0, ((0, 32), (1, 8)))
    w_spatial = centred(streams_of[2], (9, C, C), (9 * C) ** -0.5, 0.09375, ((1, 32),))
    w_temporal = centred(streams_of[3], (3, C, C), (3 * C) ** -0.5, 0.15625, ((1, 32),))
    return dict(frames_in=frames_in, cotangent=cotangent, w_spatial=w_spatial, w_temporal=w_temporal)


spatial_taps = [(row_shift, col_shift) for row_shift in range(3) for col_shift in range(3)]

def contract_rows(left, right):
    return lax.dot_general(left, right, (((0,), (0,)), ((), ())), preferred_element_type=jnp.float32)

def contract_cols(left, right):
    return lax.dot_general(left, right, (((1,), (1,)), ((), ())), preferred_element_type=jnp.float32)

def silu_slope(value):
    sigmoid = jax.nn.sigmoid(value)
    return sigmoid * (1.0 + value * (1.0 - sigmoid))

def spatial_forward(padded_act, weight):
    height = padded_act.shape[1] - 2
    width = padded_act.shape[2] - 2
    total = jnp.float32(0.0)
    for position, (row_shift, col_shift) in enumerate(spatial_taps):
        window = padded_act[:, row_shift:row_shift + height, col_shift:col_shift + width].reshape(-1, padded_act.shape[3])
        total = total + jnp.dot(window, weight[position], preferred_element_type=jnp.float32)
    return total

def spatial_transpose(grad_flat, weight, frames, height, width):
    result = jnp.zeros((frames, height + 2, width + 2, weight.shape[1]), jnp.float32)
    for position, (row_shift, col_shift) in enumerate(spatial_taps):
        part = contract_cols(grad_flat, weight[position]).reshape(frames, height, width, weight.shape[1])
        result = result.at[:, row_shift:row_shift + height, col_shift:col_shift + width].add(part)
    return result[:, 1:-1, 1:-1]

def temporal_forward(stacked, weight, frames):
    total = jnp.float32(0.0)
    for lag_step in range(3):
        window = stacked[lag_step:lag_step + frames].reshape(-1, stacked.shape[3])
        total = total + jnp.dot(window, weight[lag_step], preferred_element_type=jnp.float32)
    return total

def temporal_transpose(grad_flat, weight, frames, height, width):
    total = jnp.zeros((frames + 2, height, width, weight.shape[1]), jnp.float32)
    for lag_step in range(3):
        part = contract_cols(grad_flat, weight[lag_step]).reshape(frames, height, width, weight.shape[1])
        total = total + jnp.pad(part, ((lag_step, 2 - lag_step), (0, 0), (0, 0), (0, 0)))
    return total

def clip_pass(source, upstream, w_spatial, w_temporal):
    frames = 2 * source.shape[0]
    height, width, channels = (source.shape[1], source.shape[2], source.shape[3])
    upsampled = jnp.repeat(source, 2, axis=0)
    up_float = upsampled.astype(jnp.float32)
    activated = jax.nn.silu(up_float).astype(jnp.bfloat16)
    padded_act = jnp.pad(activated, ((0, 0), (1, 1), (1, 1), (0, 0)))
    spatial_out = spatial_forward(padded_act, w_spatial).reshape(frames, height, width, channels).astype(jnp.bfloat16)
    stacked = jnp.concatenate([spatial_out[:1], spatial_out[:1], spatial_out], axis=0)
    temporal_sum = temporal_forward(stacked, w_temporal, frames).reshape(frames, height, width, channels)
    decoded = (up_float + temporal_sum).astype(jnp.bfloat16)
    upstream_flat = upstream.reshape(-1, channels)
    pad_grad = temporal_transpose(upstream_flat, w_temporal, frames, height, width)
    inner = pad_grad[2:].at[0].add(pad_grad[0] + pad_grad[1])
    spatial_grad = inner.reshape(-1, channels).astype(jnp.bfloat16)
    grad_temporal = jnp.stack([contract_rows(stacked[lag_step:lag_step + frames].reshape(-1, channels), upstream_flat) for lag_step in range(3)])
    windows = []
    for row_shift, col_shift in spatial_taps:
        window = padded_act[:, row_shift:row_shift + height, col_shift:col_shift + width].reshape(-1, channels)
        windows.append(contract_rows(window, spatial_grad))
    grad_spatial = jnp.stack(windows)
    act_grad = spatial_transpose(spatial_grad, w_spatial, frames, height, width)
    up_grad = upstream.astype(jnp.float32) + act_grad * silu_slope(up_float)
    grad_input = up_grad.reshape(frames // 2, 2, height, width, channels).sum(axis=1).astype(jnp.bfloat16)
    return (decoded, grad_input, grad_spatial, grad_temporal)

def reference(frames_in, cotangent, w_spatial, w_temporal):

    def step(carry, item):
        decoded, grad_input, grad_s, grad_t = clip_pass(item[0], item[1], w_spatial, w_temporal)
        return ((carry[0] + grad_s, carry[1] + grad_t), (decoded, grad_input))
    start_sums = (jnp.zeros((9, C, C), jnp.float32), jnp.zeros((3, C, C), jnp.float32))
    sums, outputs = lax.scan(step, start_sums, (frames_in, cotangent))
    inverse = 1.0 / math.sqrt(CLIPS * OUT_FRAMES * ROWS * COLS)
    return (outputs[0], outputs[1], sums[0] * inverse, sums[1] * inverse)
```

```python
import math

import jax
import jax.numpy as jnp
from jax import lax
from jax.experimental import pallas as pl
from jax.experimental.pallas import tpu as pltpu
from jax.sharding import Mesh, PartitionSpec as P

f32 = jnp.float32
bf16 = jnp.bfloat16
VMEM_LIMIT = 56 * 1024 * 1024

AXES = ("y", "zl", "core", "x", "zh")
SIZES = (4, 4, 2, 4, 2)
RING = (1, 3, 2)
REL = (0, 1, 3, 2)
Y, ZL, CORE, X, FIRST = range(5)


def along(value, axis, offset):
    return lax.ppermute(value, axis, [(i, (i + offset) % 4) for i in range(4)])


def along_z(value, offset):
    steps = offset if offset < 3 else 7
    place = lambda z: z % 4 * 2 + z // 4
    return lax.ppermute(value, ("zl", "zh"), [(place(z), place((z + steps) % 8)) for z in range(8)])


def to_sibling(value):
    return lax.ppermute(value, "core", [(0, 1), (1, 0)])


def staggered_y(value):
    pairs = [(4 * y + x, (y + REL[x]) % 4 * 4 + x) for x in range(4) for y in range(4)]
    return lax.ppermute(value, ("y", "x"), pairs)


def call(kernel, outs, scratch, *args, any_from=None):
    count = len(args)
    any_from = count if any_from is None else any_from
    specs = [pl.BlockSpec(memory_space=pltpu.SMEM)]
    specs += [
        pl.BlockSpec(memory_space=pltpu.VMEM if i < any_from else pl.ANY) for i in range(1, count)
    ]
    return pl.pallas_call(
        kernel,
        out_shape=[jax.ShapeDtypeStruct(s, d) for s, d in outs],
        in_specs=specs,
        out_specs=[pl.BlockSpec(memory_space=pltpu.VMEM) for _ in outs],
        scratch_shapes=scratch,
        compiler_params=pltpu.CompilerParams(vmem_limit_bytes=VMEM_LIMIT),
        name=kernel.__name__,
    )(*args)


def mod4(value):
    return lax.rem(value + 4, 4)


def rel(q):
    return jnp.where(q < 2, q, 5 - q)


def dot(left, right):
    return jnp.dot(left, right, preferred_element_type=f32)


def dot_nt(left, right):
    return lax.dot_general(left, right, (((1,), (1,)), ((), ())), preferred_element_type=f32)


def placements(pos, pieces, weights, first_tap, taps, source_y, sems, base):
    copies = []
    for a, piece in enumerate(pieces):
        core = pos[CORE] if a < 4 else 1 - pos[CORE]
        for j in range(4):
            block = (source_y[a % 4] * 4 + mod4(pos[ZL] - REL[j])) * 2 + core
            copies.append(
                pltpu.make_async_copy(
                    piece.at[j],
                    weights.at[pl.ds(first_tap, taps), pl.ds(pl.multiple_of(block * 16, 16), 16), :],
                    sems.at[base + 4 * a + j],
                )
            )
    return copies


def column_shifts(value):
    rows = value.shape[0]
    column = lax.broadcasted_iota(jnp.int32, value.shape, 0) % 16
    before = jnp.where(column == 0, 0.0, pltpu.roll(value, 1, 0))
    after = jnp.where(column == 15, 0.0, pltpu.roll(value, rows - 1, 0))
    return before, value, after


def temporal_grad_kernel(pos, c, ch, *refs):
    pieces, (sg, mine, theirs, wt), (acc, sems) = refs[:8], refs[8:12], refs[12:]
    source_y = [mod4(pos[Y] - o) for o in REL]
    copies = placements(pos, pieces, wt, 0, 3, source_y, sems, 0)
    for copy in copies:
        copy.start()
    pair = []
    frames = [c[0], c[1], c[2], c[3], ch[0], ch[1]]
    for k in range(5):
        pair.append((frames[k].astype(f32) + frames[k + 1].astype(f32)).astype(bf16))
    lower = pos[CORE] == 0
    for k, value in enumerate((pair[0], pair[1], pair[2], frames[0], frames[3])):
        lo, hi = value[:, :256], value[:, 256:]
        mine[2 + k] = jnp.where(lower, lo, hi)
        theirs[2 + k] = jnp.where(lower, hi, lo)
    for copy in copies:
        copy.wait()
    total = dot_nt(jnp.concatenate([pair[2], pair[4]], 0), wt[0])
    total += dot_nt(jnp.concatenate([pair[1], pair[3]], 0), wt[1])
    total += dot_nt(jnp.concatenate([pair[0], pair[2]], 0), wt[2])
    acc[...] = total

    @pl.when(pos[FIRST] == 1)
    def _():
        acc[:160] += dot_nt(pair[0], wt[0]) + dot_nt(frames[0], wt[1])

    for f in range(2):
        value = acc[160 * f : 160 * f + 160].astype(bf16)
        sg[f] = value
        lo, hi = value[:, :256], value[:, 256:]
        mine[f] = jnp.where(lower, lo, hi)
        theirs[f] = jnp.where(lower, hi, lo)


def silu16(value):
    return jax.nn.silu(value.astype(f32))


def fill_shifts(buffer, slot, value, reverse):
    before, centre, after = column_shifts(value)
    order = (after, centre, before) if reverse else (before, centre, after)
    zeros = jnp.zeros((16, value.shape[1]), bf16)
    for s in range(3):
        buffer[s, slot, :16] = zeros
        buffer[s, slot, 176:] = zeros
        buffer[s, slot, 16:176] = order[s].astype(bf16)


def spatial_weight_grad_kernel(pos, src, sib, mine, theirs, *refs):
    ownx, sx1, sx2, sx3, owny, sy1, sy2, sy3, last, act_t, shifted, gx, gy, gxb, gyb = refs
    rows = [silu16(src[0]), silu16(src[1]), silu16(sib[0]), silu16(sib[1])]
    act_t[...] = jnp.concatenate(rows, 0).T.astype(bf16)
    for k, half in enumerate((mine, mine, theirs, theirs)):
        fill_shifts(shifted, k, half[k % 2].astype(f32), True)
    for tap in range(9):
        r, s = divmod(tap, 3)
        window = shifted[s, :, (2 - r) * 16 : (2 - r) * 16 + 160].reshape(640, 256)
        value = dot(act_t[...], window)
        if tap < 4:
            gx[tap] = value
            gxb[tap] = value.astype(bf16)
        elif tap < 8:
            gy[tap - 4] = value
            gyb[tap - 4] = value.astype(bf16)
        else:
            last[...] = value
    x, y = pos[X], pos[Y]
    ownx[...] = gx[x]
    owny[...] = gy[:, pl.ds(pl.multiple_of(y * 128, 128), 128)]
    for offset, outx, outy in zip(RING, (sx1, sx2, sx3), (sy1, sy2, sy3)):
        outx[...] = gxb[mod4(x + offset)]
        outy[...] = gyb[:, pl.ds(pl.multiple_of(mod4(y + offset) * 128, 128), 128)]


def spatial_conv_kernel(pos, src, prev, *refs):
    near, far, (out, ws), (shifted, sems) = refs[:8], refs[8:16], refs[16:18], refs[18:]
    near_y = [mod4(pos[Y] - o) for o in REL]
    far_y = [mod4(pos[Y] - rel(mod4(pos[X] - o))) for o in REL]
    copies = placements(pos, near, ws, 0, 4, near_y, sems, 0)
    copies += placements(pos, far, ws, 4, 5, far_y, sems, 32)
    for copy in copies:
        copy.start()
    before = jnp.where(pos[FIRST] == 1, src[0].astype(f32), prev[...].astype(f32))
    for slot, value in enumerate((before, src[0].astype(f32), src[1].astype(f32))):
        fill_shifts(shifted, slot, jax.nn.silu(value), False)
    for copy in copies:
        copy.wait()
    total = jnp.zeros((480, 512), f32)
    for tap in range(9):
        r, s = divmod(tap, 3)
        total += dot(shifted[s, :, r * 16 : r * 16 + 160].reshape(480, 512), ws[tap])
    for f in range(3):
        out[f] = total[160 * f : 160 * f + 160].astype(bf16)


def outputs_kernel(pos, src, c, sp, sg, wt, ws, decoded, grad_input, shifted):
    p0 = dot(sp[0:2].reshape(320, 512), wt[0])
    p1 = dot(sp[...].reshape(480, 512), wt[1])
    p2 = dot(sp[1:3].reshape(320, 512), wt[2])
    for g in range(2):
        u = src[g].astype(f32)
        both = p0[160 * g : 160 * g + 160] + p2[160 * g : 160 * g + 160]
        decoded[2 * g] = (u + (both + p1[160 * g : 160 * g + 160])).astype(bf16)
        decoded[2 * g + 1] = (u + (both + p1[160 * g + 160 : 160 * g + 320])).astype(bf16)
    for f in range(2):
        fill_shifts(shifted, f, sg[f].astype(f32), True)
    total = jnp.zeros((320, 512), f32)
    for tap in range(9):
        r, s = divmod(tap, 3)
        window = shifted[s, :, (2 - r) * 16 : (2 - r) * 16 + 160].reshape(320, 512)
        total += dot_nt(window, ws[tap])
    for g in range(2):
        u = src[g].astype(f32)
        sigma = jax.nn.sigmoid(u)
        slope = sigma * (1.0 + u * (1.0 - sigma))
        cotangents = c[2 * g].astype(f32) + c[2 * g + 1].astype(f32)
        grad_input[g] = (cotangents + total[160 * g : 160 * g + 160] * slope).astype(bf16)


def temporal_weight_grad_kernel(pos, sp, sps, mine, theirs, last, *refs):
    ownx, sx1, sx2, sx3, owny, sy1, sy2, sy3, early, late, gx, gy, gxb, gyb = refs
    early[...] = (
        jnp.concatenate([sp[0], sp[1], sps[0], sps[1]], 0).astype(f32).T.astype(bf16)
    )
    late[...] = jnp.concatenate([sp[1], sp[2], sps[1], sps[2]], 0).astype(f32).T.astype(bf16)
    outer = jnp.concatenate([mine[2], mine[4], theirs[2], theirs[4]], 0)
    inner = jnp.concatenate([mine[5], mine[3], theirs[5], theirs[3]], 0)
    zeros = jnp.zeros((160, 256), bf16)
    end = jnp.concatenate([zeros, mine[6], zeros, theirs[6]], 0)
    values = (
        last[...],
        dot(early[...], outer),
        dot(early[...], inner) + dot(late[...], end),
        dot(late[...], outer),
    )
    for q, value in enumerate(values):
        gx[q] = value[:, :128]
        gxb[q] = value[:, :128].astype(bf16)
        gy[q] = value[:, 128:]
        gyb[q] = value[:, 128:].astype(bf16)
    x, y = pos[X], pos[Y]
    ownx[...] = gx[x]
    owny[...] = gy[:, pl.ds(pl.multiple_of(y * 128, 128), 128)]
    for offset, outx, outy in zip(RING, (sx1, sx2, sx3), (sy1, sy2, sy3)):
        outx[...] = gxb[mod4(x + offset)]
        outy[...] = gyb[:, pl.ds(pl.multiple_of(mod4(y + offset) * 128, 128), 128)]


def second_exchange_kernel(pos, ax, ax1, ax2, ax3, ay, ay1, ay2, ay3, *outs):
    ownx, bx1, bx2, bx3, owny, by1, by2, by3 = outs
    x, y = pos[X], pos[Y]
    for offset, outx, outy in zip((0,) + RING, (ownx, bx1, bx2, bx3), (owny, by1, by2, by3)):
        rows = pl.ds(pl.multiple_of(mod4(y + offset) * 128, 128), 128)
        tap = mod4(x + offset)
        sumx = ax[rows] + ax1[rows].astype(f32) + ax2[rows].astype(f32) + ax3[rows].astype(f32)
        sumy = ay[tap] + ay1[tap].astype(f32) + ay2[tap].astype(f32) + ay3[tap].astype(f32)
        outx[...] = sumx.astype(outx.dtype)
        outy[...] = sumy.astype(outy.dtype)


def third_exchange_kernel(pos, *refs):
    groups, (own, z1, z2, z3), (total,) = refs[:16], refs[16:20], refs[20:]

    def summed(k):
        a, b, c, d = groups[4 * k : 4 * k + 4]
        return a[...] + b[...].astype(f32) + c[...].astype(f32) + d[...].astype(f32)

    total[0] = summed(0)
    total[1] = summed(1)
    total[2, :, :128] = summed(2)
    total[2, :, 128:] = summed(3)
    for offset, out in zip((0,) + RING, (own, z1, z2, z3)):
        rows = pl.ds(pl.multiple_of(mod4(pos[ZL] + offset) * 32, 32), 32)
        out[...] = total[:, rows]


def core_rows_kernel(pos, own, z1, z2, z3, mine, theirs):
    total = own[...] + z1[...] + z2[...] + z3[...]
    lower = pos[CORE] == 0
    mine[...] = jnp.where(lower, total[:, :16], total[:, 16:])
    theirs[...] = jnp.where(lower, total[:, 16:], total[:, :16])


def halves_kernel(inverse):
    def halves(pos, mine, other_zh, sibling, both, out):
        own = (mine[...] + other_zh[...]) * inverse
        rest = (sibling[...] + both[...]) * inverse
        lower = pos[CORE] == 0
        out[:, :, :256] = jnp.where(lower, own, rest)
        out[:, :, 256:] = jnp.where(lower, rest, own)

    return halves


def final_taps_kernel(pos, g0, g1, g2, g3, spatial, temporal, taps):
    for offset, piece in zip(REL, (g0, g1, g2, g3)):
        q = mod4(pos[X] - offset)
        for g in range(3):
            taps[4 * g + q] = piece[g]
    spatial[...] = taps[0:9]
    temporal[...] = taps[9:12]


def exchange(axis_send, values):
    return [axis_send(v, o) for v, o in zip(values, RING)]


def per_device(frames_in, cotangent, w_spatial, w_temporal):
    src = frames_in[0].reshape(2, 160, 512)
    c = cotangent[0].reshape(4, 160, 512)
    tm_index = lax.axis_index("x") * 2 + lax.axis_index("zh")
    pos = jnp.stack(
        [
            lax.axis_index("y"),
            lax.axis_index("zl"),
            lax.axis_index("core"),
            lax.axis_index("x"),
            (tm_index == 0).astype(jnp.int32),
        ]
    ).astype(jnp.int32)
    send_x = lambda v, o: along(v, "x", o)
    send_y = lambda v, o: along(v, "y", o)

    gathered_t = [w_temporal] + [along_z(w_temporal, o) for o in RING]
    after = lax.ppermute(c[:2], ("x", "zh"), [(i, i - 1) for i in range(1, 8)])
    sib_src = to_sibling(src)
    before = lax.ppermute(src[1], ("x", "zh"), [(i, i + 1) for i in range(7)])
    stack_t = jnp.stack(gathered_t)
    pieces_t = [stack_t] + [send_y(stack_t, o) for o in RING]
    pieces_t += [to_sibling(p) for p in pieces_t]

    gathered_s = [w_spatial] + [along_z(w_spatial, o) for o in RING]
    near = jnp.stack([g[:4] for g in gathered_s])
    far = jnp.stack([g[4:] for g in gathered_s])
    far = staggered_y(far)
    far_pieces = [far] + [send_x(far, o) for o in RING]
    near_pieces = [near] + [send_y(near, o) for o in RING]
    near_pieces += [to_sibling(p) for p in near_pieces]
    far_pieces += [to_sibling(p) for p in far_pieces]

    sg, mine, theirs, wt = call(
        temporal_grad_kernel,
        [((2, 160, 512), bf16), ((7, 160, 256), bf16), ((7, 160, 256), bf16), ((3, 512, 512), bf16)],
        [pltpu.VMEM((320, 512), f32), pltpu.SemaphoreType.DMA((32,))],
        pos, c, after, *pieces_t, any_from=3,
    )
    theirs = to_sibling(theirs)

    first = call(
        spatial_weight_grad_kernel,
        [((512, 256), f32)] + [((512, 256), bf16)] * 3
        + [((4, 128, 256), f32)] + [((4, 128, 256), bf16)] * 3 + [((512, 256), f32)],
        [
            pltpu.VMEM((512, 640), bf16), pltpu.VMEM((3, 4, 192, 256), bf16),
            pltpu.VMEM((4, 512, 256), f32), pltpu.VMEM((4, 512, 256), f32),
            pltpu.VMEM((4, 512, 256), bf16), pltpu.VMEM((4, 512, 256), bf16),
        ],
        pos, src, sib_src, mine, theirs,
    )
    last = first[8]
    rx = exchange(send_x, first[1:4])
    ry = exchange(send_y, first[5:8])
    part = ((128, 256), f32), ((128, 256), bf16), ((128, 256), bf16), ((128, 256), bf16)
    second = call(
        second_exchange_kernel, list(part) * 2, [],
        pos, first[0], *rx, first[4], *ry,
    )
    bx = exchange(send_y, second[1:4])
    by = exchange(send_x, second[5:8])

    sp, ws = call(
        spatial_conv_kernel,
        [((3, 160, 512), bf16), ((9, 512, 512), bf16)],
        [pltpu.VMEM((3, 3, 192, 512), bf16), pltpu.SemaphoreType.DMA((64,))],
        pos, src, before, *near_pieces, *far_pieces, any_from=3,
    )
    sib_sp = to_sibling(sp)
    decoded, grad_input = call(
        outputs_kernel,
        [((4, 160, 512), bf16), ((2, 160, 512), bf16)],
        [pltpu.VMEM((3, 2, 192, 512), bf16)],
        pos, src, c, sp, sg, wt, ws,
    )
    late = call(
        temporal_weight_grad_kernel,
        [((512, 128), f32)] + [((512, 128), bf16)] * 3
        + [((4, 128, 128), f32)] + [((4, 128, 128), bf16)] * 3,
        [
            pltpu.VMEM((512, 640), bf16), pltpu.VMEM((512, 640), bf16),
            pltpu.VMEM((4, 512, 128), f32), pltpu.VMEM((4, 512, 128), f32),
            pltpu.VMEM((4, 512, 128), bf16), pltpu.VMEM((4, 512, 128), bf16),
        ],
        pos, sp, sib_sp, mine, theirs, last,
    )
    lx = exchange(send_x, late[1:4])
    ly = exchange(send_y, late[5:8])
    part = ((128, 128), f32), ((128, 128), bf16), ((128, 128), bf16), ((128, 128), bf16)
    fourth = call(
        second_exchange_kernel, list(part) * 2, [],
        pos, late[0], *lx, late[4], *ly,
    )
    mx = exchange(send_y, fourth[1:4])
    my = exchange(send_x, fourth[5:8])

    zs = call(
        third_exchange_kernel,
        [((3, 32, 256), f32)] * 4,
        [pltpu.VMEM((3, 128, 256), f32)],
        pos, second[0], *bx, second[4], *by, fourth[0], *mx, fourth[4], *my,
    )
    rz = exchange(along_z, zs[1:4])
    rows_mine, rows_theirs = call(
        core_rows_kernel, [((3, 16, 256), f32)] * 2, [], pos, zs[0], *rz
    )
    other_zh = lax.ppermute(rows_mine, "zh", [(0, 1), (1, 0)])
    sibling = to_sibling(rows_theirs)
    both = lax.ppermute(rows_theirs, ("core", "zh"), [(i, 3 - i) for i in range(4)])
    inverse = 1.0 / math.sqrt(256 * 640)
    (taps,) = call(
        halves_kernel(inverse), [((3, 16, 512), f32)], [],
        pos, rows_mine, other_zh, sibling, both,
    )
    pieces = [taps] + [send_x(taps, o) for o in RING]
    grad_s, grad_t = call(
        final_taps_kernel,
        [((9, 16, 512), f32), ((3, 16, 512), f32)],
        [pltpu.VMEM((12, 16, 512), f32)],
        pos, *pieces,
    )
    return (
        decoded.reshape(1, 4, 10, 16, 512),
        grad_input.reshape(1, 2, 10, 16, 512),
        grad_s,
        grad_t,
    )


def solution(mesh):
    physical = Mesh(mesh.devices.reshape(SIZES), AXES)
    dp, tm = ("y", "zl", "core"), ("x", "zh")
    values, weights = P(dp, tm, None, None, None), P(None, dp, None)
    return jax.shard_map(
        per_device,
        mesh=physical,
        in_specs=(values, values, weights, weights),
        out_specs=(values, values, weights, weights),
        check_vma=False,
    )
```

```python
import math

import jax
import jax.numpy as jnp
from jax import lax
from jax.experimental import pallas as pl
from jax.experimental.pallas import tpu as pltpu
from jax.sharding import Mesh, PartitionSpec as P

f32 = jnp.float32
bf16 = jnp.bfloat16
VMEM_LIMIT = 56 * 1024 * 1024

AXES = ("y", "zl", "core", "x", "zh")
SIZES = (4, 4, 2, 4, 2)
RING = (1, 3, 2)
REL = (0, 1, 3, 2)
Y, ZL, CORE, X, FIRST = range(5)


def along(value, axis, offset):
    return lax.ppermute(value, axis, [(i, (i + offset) % 4) for i in range(4)])


def along_z(value, offset):
    steps = offset if offset < 3 else 7
    place = lambda z: z % 4 * 2 + z // 4
    return lax.ppermute(value, ("zl", "zh"), [(place(z), place((z + steps) % 8)) for z in range(8)])


def to_sibling(value):
    return lax.ppermute(value, "core", [(0, 1), (1, 0)])


def call(kernel, outs, scratch, *args, any_from=None):
    count = len(args)
    any_from = count if any_from is None else any_from
    specs = [pl.BlockSpec(memory_space=pltpu.SMEM)]
    specs += [
        pl.BlockSpec(memory_space=pltpu.VMEM if i < any_from else pl.ANY) for i in range(1, count)
    ]
    return pl.pallas_call(
        kernel,
        out_shape=[jax.ShapeDtypeStruct(s, d) for s, d in outs],
        in_specs=specs,
        out_specs=[pl.BlockSpec(memory_space=pltpu.VMEM) for _ in outs],
        scratch_shapes=scratch,
        compiler_params=pltpu.CompilerParams(vmem_limit_bytes=VMEM_LIMIT),
        name=kernel.__name__,
    )(*args)


def mod4(value):
    return lax.rem(value + 4, 4)


def dot(left, right):
    return jnp.dot(left, right, preferred_element_type=f32)


def dot_nt(left, right):
    return lax.dot_general(left, right, (((1,), (1,)), ((), ())), preferred_element_type=f32)


def placements(pos, own, sibling, weights, zl_of, sems):
    copies = []
    for a, piece in enumerate((own, sibling)):
        core = pos[CORE] if a == 0 else 1 - pos[CORE]
        for y in range(4):
            for k in range(4):
                block = (y * 4 + zl_of(k)) * 2 + core
                copies.append(
                    pltpu.make_async_copy(
                        piece.at[y, k],
                        weights.at[:, pl.ds(pl.multiple_of(block * 16, 16), 16), :],
                        sems.at[16 * a + 4 * y + k],
                    )
                )
    return copies


def column_shifts(value):
    rows = value.shape[0]
    column = lax.broadcasted_iota(jnp.int32, value.shape, 0) % 16
    before = jnp.where(column == 0, 0.0, pltpu.roll(value, 1, 0))
    after = jnp.where(column == 15, 0.0, pltpu.roll(value, rows - 1, 0))
    return before, value, after


def fill_shifts(buffer, slot, value, reverse):
    before, centre, after = column_shifts(value)
    width = value.shape[1]
    buffer[slot, :16] = jnp.zeros((16, 3 * width), bf16)
    buffer[slot, 176:] = jnp.zeros((16, 3 * width), bf16)
    for s, shifted in enumerate((after, centre, before) if reverse else (before, centre, after)):
        buffer[slot, 16:176, s * width : (s + 1) * width] = shifted.astype(bf16)


def strip_rows(start):
    return pl.ds(pl.multiple_of(start * 16, 16), 160)


def temporal_grad_kernel(pos, c, own, sibling, grads, mine, theirs, wt, sems):
    copies = placements(pos, own, sibling, wt, lambda k: k, sems)
    for copy in copies:
        copy.start()
    lower = pos[CORE] == 0

    def split(k, value):
        lo, hi = value[:, :256], value[:, 256:]
        mine[k] = jnp.where(lower, lo, hi)
        theirs[k] = jnp.where(lower, hi, lo)

    frames = [c[k] for k in range(4)]
    pair = [(frames[k].astype(f32) + frames[k + 1].astype(f32)).astype(bf16) for k in range(3)]
    for k, value in enumerate((pair[0], pair[1], pair[2], frames[0], frames[3])):
        split(3 + k, value)
    for copy in copies:
        copy.wait()
    ends = jnp.concatenate([pair[0], pair[2]], 0)
    p0 = dot_nt(ends, wt[0])
    p1 = dot_nt(jnp.concatenate([frames[0], pair[1], frames[3]], 0), wt[1])
    p2 = dot_nt(ends, wt[2])
    values = (p0[:160] + p1[:160], p0[160:] + p1[160:320] + p2[:160], p1[320:] + p2[160:])
    for k, value in enumerate(values):
        value = value.astype(bf16)
        grads[k] = value
        split(k, value)


def spatial_weight_grad_kernel(pos, frames, sib, mine, theirs, *refs):
    own, s1, s2, s3, last, act_t, shifted, g, gb = refs
    rows = [jax.nn.silu(ref[k].astype(f32)) for ref in (frames, sib) for k in range(3)]
    act_t[...] = jnp.concatenate(rows, 0).T.astype(bf16)
    for k in range(6):
        fill_shifts(shifted, k, (mine, theirs)[k // 3][k % 3].astype(f32), True)

    def step(r, _):
        window = shifted[:, strip_rows(2 - r)].reshape(960, 768)
        value = dot(act_t[...], window)
        for s in range(3):
            part = value[:, 256 * s : 256 * s + 256]
            g[3 * r + s] = part
            gb[3 * r + s] = part.astype(bf16)
        return 0

    lax.fori_loop(0, 3, step, 0)
    x = pos[X]
    own[...] = g[pl.ds(2 * x, 2)]
    last[...] = g[8]
    for offset, out in zip(RING, (s1, s2, s3)):
        out[...] = gb[pl.ds(2 * mod4(x + offset), 2)]


def spatial_conv_kernel(pos, frames, own, sibling, out, ws, shifted, acc, sems):
    copies = placements(pos, own, sibling, ws, lambda k: mod4(pos[ZL] - REL[k]), sems)
    for copy in copies:
        copy.start()
    for k in range(3):
        fill_shifts(shifted, k, jax.nn.silu(frames[k].astype(f32)), False)
    for copy in copies:
        copy.wait()
    acc[...] = jnp.zeros((480, 512), f32)

    def step(r, _):
        window = shifted[:, strip_rows(r)].reshape(480, 1536)
        acc[...] += dot(window, ws[pl.ds(3 * r, 3)].reshape(1536, 512))
        return 0

    lax.fori_loop(0, 3, step, 0)
    for k in range(3):
        out[k] = acc[160 * k : 160 * k + 160].astype(bf16)


def outputs_kernel(pos, frames, c, sp, grads, after, wt, ws, decoded, grad_input, shifted, acc):
    p0 = dot(sp[0:2].reshape(320, 512), wt[0])
    p1 = dot(sp[...].reshape(480, 512), wt[1])
    p2 = dot(sp[1:3].reshape(320, 512), wt[2])
    for g in range(2):
        u = frames[1 + g].astype(f32)
        both = p0[160 * g : 160 * g + 160] + p2[160 * g : 160 * g + 160]
        decoded[2 * g] = (u + (both + p1[160 * g : 160 * g + 160])).astype(bf16)
        decoded[2 * g + 1] = (u + (both + p1[160 * g + 160 : 160 * g + 320])).astype(bf16)
    edge = jnp.where(pos[FIRST] == 1, grads[0].astype(f32), 0.0)
    fill_shifts(shifted, 0, grads[1].astype(f32) + edge, True)
    fill_shifts(shifted, 1, grads[2].astype(f32) + after[...].astype(f32), True)
    acc[...] = jnp.zeros((320, 512), f32)

    def step(r, _):
        for s in range(3):
            window = shifted[:, strip_rows(2 - r), 512 * s : 512 * s + 512].reshape(320, 512)
            acc[...] += dot_nt(window, ws[3 * r + s])
        return 0

    lax.fori_loop(0, 3, step, 0)
    for g in range(2):
        u = frames[1 + g].astype(f32)
        sigma = jax.nn.sigmoid(u)
        slope = sigma * (1.0 + u * (1.0 - sigma))
        cotangents = c[2 * g].astype(f32) + c[2 * g + 1].astype(f32)
        grad_input[g] = (cotangents + acc[160 * g : 160 * g + 160] * slope).astype(bf16)


def temporal_weight_grad_kernel(pos, sp, sps, mine, theirs, last, *refs):
    own, s1, s2, s3, early, late, g, gb = refs
    early[...] = (
        jnp.concatenate([sp[0], sp[1], sps[0], sps[1]], 0).astype(f32).T.astype(bf16)
    )
    late[...] = jnp.concatenate([sp[1], sp[2], sps[1], sps[2]], 0).astype(f32).T.astype(bf16)
    outer = jnp.concatenate([mine[3], mine[5], theirs[3], theirs[5]], 0)
    inner = jnp.concatenate([mine[6], mine[4], theirs[6], theirs[4]], 0)
    zeros = jnp.zeros((160, 256), bf16)
    end = jnp.concatenate([zeros, mine[7], zeros, theirs[7]], 0)
    values = (
        last[...],
        dot(early[...], outer),
        dot(early[...], inner) + dot(late[...], end),
        dot(late[...], outer),
    )
    for q, value in enumerate(values):
        g[q] = value
        gb[q] = value.astype(bf16)
    x = pos[X]
    own[...] = g[pl.ds(x, 1)]
    for offset, out in zip(RING, (s1, s2, s3)):
        out[...] = gb[pl.ds(mod4(x + offset), 1)]


def rows_kernel(pos, own, r1, r2, r3, *outs):
    for offset, out in zip((0,) + RING, outs):
        rows = pl.ds(pl.multiple_of(mod4(pos[Y] + offset) * 128, 128), 128)
        total = own[:, rows] + r1[:, rows].astype(f32) + r2[:, rows].astype(f32)
        out[...] = (total + r3[:, rows].astype(f32)).astype(out.dtype)


def third_exchange_kernel(pos, *refs):
    groups, outs, (total,) = refs[:8], refs[8:12], refs[12:]
    for k, start in enumerate((0, 2)):
        a, b, c, d = groups[4 * k : 4 * k + 4]
        value = a[...] + b[...].astype(f32) + c[...].astype(f32) + d[...].astype(f32)
        total[start : start + a.shape[0]] = value
    for offset, out in zip((0,) + RING, outs):
        rows = pl.ds(pl.multiple_of(mod4(pos[ZL] + offset) * 32, 32), 32)
        out[...] = total[:, rows]


def core_rows_kernel(pos, own, z1, z2, z3, mine, theirs):
    total = own[...] + z1[...] + z2[...] + z3[...]
    lower = pos[CORE] == 0
    mine[...] = jnp.where(lower, total[:, :16], total[:, 16:])
    theirs[...] = jnp.where(lower, total[:, 16:], total[:, :16])


def halves_kernel(inverse):
    def halves(pos, mine, other_zh, sibling, both, out):
        own = (mine[...] + other_zh[...]) * inverse
        rest = (sibling[...] + both[...]) * inverse
        lower = pos[CORE] == 0
        out[:, :, :256] = jnp.where(lower, own, rest)
        out[:, :, 256:] = jnp.where(lower, rest, own)

    return halves


def final_taps_kernel(pos, parts, spatial, temporal):
    for q in range(4):
        spatial[2 * q] = parts[q, 0]
        spatial[2 * q + 1] = parts[q, 1]
    spatial[8] = parts[0, 2]
    for q in range(1, 4):
        temporal[q - 1] = parts[q, 2]


def exchange(axis_send, values):
    return [axis_send(v, o) for v, o in zip(values, RING)]


def per_device(frames_in, cotangent, w_spatial, w_temporal):
    src = frames_in[0].reshape(2, 160, 512)
    c = cotangent[0].reshape(4, 160, 512)
    first = lax.axis_index("x") * 2 + lax.axis_index("zh") == 0
    pos = jnp.stack(
        [
            lax.axis_index("y"),
            lax.axis_index("zl"),
            lax.axis_index("core"),
            lax.axis_index("x"),
            first.astype(jnp.int32),
        ]
    ).astype(jnp.int32)
    send_x = lambda v, o: along(v, "x", o)
    send_y = lambda v, o: along(v, "y", o)

    gathered_t = lax.all_gather(w_temporal, "zl")
    before = lax.ppermute(src[1], ("x", "zh"), [(i, i + 1) for i in range(7)])
    gathered_s = jnp.stack([w_spatial] + [along_z(w_spatial, o) for o in RING])
    gathered_t = lax.all_gather(gathered_t, "y")
    sibling_t = to_sibling(gathered_t)
    frames = jnp.concatenate([jnp.where(first, src[:1], before[None]), src], 0)
    sib_frames = to_sibling(frames)
    gathered_s = lax.all_gather(gathered_s, "y")
    sibling_s = to_sibling(gathered_s)

    grads, mine, theirs, wt = call(
        temporal_grad_kernel,
        [((3, 160, 512), bf16), ((8, 160, 256), bf16), ((8, 160, 256), bf16), ((3, 512, 512), bf16)],
        [pltpu.SemaphoreType.DMA((32,))],
        pos, c, gathered_t, sibling_t, any_from=2,
    )
    theirs = to_sibling(theirs)
    after = lax.ppermute(grads[0], ("x", "zh"), [(i, i - 1) for i in range(1, 8)])

    one = call(
        spatial_weight_grad_kernel,
        [((2, 512, 256), f32)] + [((2, 512, 256), bf16)] * 3 + [((512, 256), f32)],
        [
            pltpu.VMEM((512, 960), bf16), pltpu.VMEM((6, 192, 768), bf16),
            pltpu.VMEM((9, 512, 256), f32), pltpu.VMEM((9, 512, 256), bf16),
        ],
        pos, frames, sib_frames, mine, theirs,
    )
    last = one[4]
    two = call(
        rows_kernel, [((2, 128, 256), f32)] + [((2, 128, 256), bf16)] * 3, [],
        pos, one[0], *exchange(send_x, one[1:4]),
    )
    two_received = exchange(send_y, two[1:4])

    sp, ws = call(
        spatial_conv_kernel,
        [((3, 160, 512), bf16), ((9, 512, 512), bf16)],
        [pltpu.VMEM((3, 192, 1536), bf16), pltpu.VMEM((480, 512), f32), pltpu.SemaphoreType.DMA((32,))],
        pos, frames, gathered_s, sibling_s, any_from=2,
    )
    sib_sp = to_sibling(sp)
    late = call(
        temporal_weight_grad_kernel,
        [((1, 512, 256), f32)] + [((1, 512, 256), bf16)] * 3,
        [
            pltpu.VMEM((512, 640), bf16), pltpu.VMEM((512, 640), bf16),
            pltpu.VMEM((4, 512, 256), f32), pltpu.VMEM((4, 512, 256), bf16),
        ],
        pos, sp, sib_sp, mine, theirs, last,
    )
    late_received = exchange(send_x, late[1:4])
    sp, late_own = lax.optimization_barrier((sp, late[0]))
    decoded, grad_input = call(
        outputs_kernel,
        [((4, 160, 512), bf16), ((2, 160, 512), bf16)],
        [pltpu.VMEM((2, 192, 1536), bf16), pltpu.VMEM((320, 512), f32)],
        pos, frames, c, sp, grads, after, wt, ws,
    )
    *late_received, decoded = lax.optimization_barrier((*late_received, decoded))
    four = call(
        rows_kernel, [((1, 128, 256), f32)] + [((1, 128, 256), bf16)] * 3, [],
        pos, late_own, *late_received,
    )
    zs = call(
        third_exchange_kernel,
        [((3, 32, 256), f32)] * 4,
        [pltpu.VMEM((3, 128, 256), f32)],
        pos, two[0], *two_received, four[0], *exchange(send_y, four[1:4]),
    )
    rz = exchange(along_z, zs[1:4])
    rows_mine, rows_theirs = call(
        core_rows_kernel, [((3, 16, 256), f32)] * 2, [], pos, zs[0], *rz
    )
    other_zh = lax.ppermute(rows_mine, "zh", [(0, 1), (1, 0)])
    sibling = to_sibling(rows_theirs)
    both = lax.ppermute(rows_theirs, ("core", "zh"), [(i, 3 - i) for i in range(4)])
    inverse = 1.0 / math.sqrt(256 * 640)
    (taps,) = call(
        halves_kernel(inverse), [((3, 16, 512), f32)], [],
        pos, rows_mine, other_zh, sibling, both,
    )
    grad_s, grad_t = call(
        final_taps_kernel,
        [((9, 16, 512), f32), ((3, 16, 512), f32)], [],
        pos, lax.all_gather(taps, "x"),
    )
    return (
        decoded.reshape(1, 4, 10, 16, 512),
        grad_input.reshape(1, 2, 10, 16, 512),
        grad_s,
        grad_t,
    )


def solution(mesh):
    physical = Mesh(mesh.devices.reshape(SIZES), AXES)
    dp, tm = ("y", "zl", "core"), ("x", "zh")
    values, weights = P(dp, tm, None, None, None), P(None, dp, None)
    return jax.shard_map(
        per_device,
        mesh=physical,
        in_specs=(values, values, weights, weights),
        out_specs=(values, values, weights, weights),
        check_vma=False,
    )
```

```python
import math

import jax
import jax.numpy as jnp
from jax import lax
from jax.experimental import pallas as pl
from jax.experimental.pallas import tpu as pltpu
from jax.sharding import Mesh, PartitionSpec as P

f32 = jnp.float32
bf16 = jnp.bfloat16
VMEM_LIMIT = 56 * 1024 * 1024
COST = 1000000

AXES = ("y", "zl", "core", "x", "zh")
SIZES = (4, 4, 2, 4, 2)
RING = (1, 3, 2)
REL = (0, 1, 3, 2)
Y, ZL, CORE, X, FIRST = range(5)


def along(value, axis, offset):
    return lax.ppermute(value, axis, [(i, (i + offset) % 4) for i in range(4)])


def along_z(value, offset):
    steps = offset if offset < 3 else 7
    place = lambda z: z % 4 * 2 + z // 4
    return lax.ppermute(value, ("zl", "zh"), [(place(z), place((z + steps) % 8)) for z in range(8)])


def to_sibling(value):
    return lax.ppermute(value, "core", [(0, 1), (1, 0)])


def call(kernel, outs, scratch, *args, any_from=None):
    count = len(args)
    any_from = count if any_from is None else any_from
    specs = [pl.BlockSpec(memory_space=pltpu.SMEM)]
    specs += [
        pl.BlockSpec(memory_space=pltpu.VMEM if i < any_from else pl.ANY) for i in range(1, count)
    ]
    return pl.pallas_call(
        kernel,
        out_shape=[jax.ShapeDtypeStruct(s, d) for s, d in outs],
        in_specs=specs,
        out_specs=[pl.BlockSpec(memory_space=pltpu.VMEM) for _ in outs],
        scratch_shapes=scratch,
        compiler_params=pltpu.CompilerParams(vmem_limit_bytes=VMEM_LIMIT),
        cost_estimate=pl.CostEstimate(flops=COST, bytes_accessed=0, transcendentals=0),
        name=kernel.__name__,
    )(*args)


def mod4(value):
    return lax.rem(value + 4, 4)


def dot(left, right):
    return jnp.dot(left, right, preferred_element_type=f32)


def dot_nt(left, right):
    return lax.dot_general(left, right, (((1,), (1,)), ((), ())), preferred_element_type=f32)


def placements(pos, own, sibling, weights, zl_of, sems):
    copies = []
    for a, piece in enumerate((own, sibling)):
        core = pos[CORE] if a == 0 else 1 - pos[CORE]
        for y in range(4):
            for k in range(4):
                block = (y * 4 + zl_of(k)) * 2 + core
                copies.append(
                    pltpu.make_async_copy(
                        piece.at[y, k],
                        weights.at[:, pl.ds(pl.multiple_of(block * 16, 16), 16), :],
                        sems.at[16 * a + 4 * y + k],
                    )
                )
    return copies


def column_shifts(value):
    rows = value.shape[0]
    column = lax.broadcasted_iota(jnp.int32, value.shape, 0) % 16
    before = jnp.where(column == 0, 0.0, pltpu.roll(value, 1, 0))
    after = jnp.where(column == 15, 0.0, pltpu.roll(value, rows - 1, 0))
    return before, value, after


def fill_shifts(buffer, slot, value, reverse):
    before, centre, after = column_shifts(value)
    width = value.shape[1]
    buffer[slot, :16] = jnp.zeros((16, 3 * width), bf16)
    buffer[slot, 176:] = jnp.zeros((16, 3 * width), bf16)
    for s, shifted in enumerate((after, centre, before) if reverse else (before, centre, after)):
        buffer[slot, 16:176, s * width : (s + 1) * width] = shifted.astype(bf16)


def strip_rows(start):
    return pl.ds(pl.multiple_of(start * 16, 16), 160)


def temporal_grad_kernel(pos, c, own, sibling, terms, wt, sems):
    copies = placements(pos, own, sibling, wt, lambda k: mod4(pos[ZL] - REL[k]), sems)
    for copy in copies:
        copy.start()
    frames = [c[k] for k in range(4)]
    pair = [(frames[k].astype(f32) + frames[k + 1].astype(f32)).astype(bf16) for k in range(3)]
    for k, value in enumerate((pair[0], pair[1], pair[2], frames[0], frames[3])):
        terms[3 + k] = value
    for copy in copies:
        copy.wait()
    ends = jnp.concatenate([pair[0], pair[2]], 0)
    p0 = dot_nt(ends, wt[0])
    p1 = dot_nt(jnp.concatenate([frames[0], pair[1], frames[3]], 0), wt[1])
    p2 = dot_nt(ends, wt[2])
    values = (p0[:160] + p1[:160], p0[160:] + p1[160:320] + p2[:160], p1[320:] + p2[160:])
    for k, value in enumerate(values):
        terms[k] = value.astype(bf16)


def core_channels(pos, frames):
    flat = jnp.concatenate(frames, 0)
    parts = flat.T.astype(bf16).reshape(16, 2, 16, flat.shape[0])
    return jnp.where(pos[CORE] == 0, parts[:, 0], parts[:, 1]).reshape(256, flat.shape[0])


def spatial_weight_grad_kernel(pos, frames, sib, terms, sib_terms, g, act_t, shifted):
    act_t[...] = core_channels(
        pos, [jax.nn.silu(ref[k].astype(f32)) for ref in (frames, sib) for k in range(3)]
    )
    for k in range(6):
        fill_shifts(shifted, k, (terms, sib_terms)[k // 3][k % 3].astype(f32), True)

    def step(r, _):
        window = shifted[:, strip_rows(2 - r)].reshape(960, 1536)
        value = dot(act_t[...], window)
        for s in range(3):
            g[3 * r + s] = value[:, 512 * s : 512 * s + 512]
        return 0

    lax.fori_loop(0, 3, step, 0)


def spatial_conv_kernel(pos, frames, own, sibling, out, ws, shifted, acc, sems):
    copies = placements(pos, own, sibling, ws, lambda k: mod4(pos[ZL] - REL[k]), sems)
    for copy in copies:
        copy.start()
    for k in range(3):
        fill_shifts(shifted, k, jax.nn.silu(frames[k].astype(f32)), False)
    for copy in copies:
        copy.wait()
    acc[...] = jnp.zeros((480, 512), f32)

    def step(r, _):
        window = shifted[:, strip_rows(r)].reshape(480, 1536)
        acc[...] += dot(window, ws[pl.ds(3 * r, 3)].reshape(1536, 512))
        return 0

    lax.fori_loop(0, 3, step, 0)
    for k in range(3):
        out[k] = acc[160 * k : 160 * k + 160].astype(bf16)


def outputs_kernel(pos, frames, c, sp, terms, after, wt, ws, decoded, grad_input, shifted, acc):
    p0 = dot(sp[0:2].reshape(320, 512), wt[0])
    p1 = dot(sp[...].reshape(480, 512), wt[1])
    p2 = dot(sp[1:3].reshape(320, 512), wt[2])
    for g in range(2):
        u = frames[1 + g].astype(f32)
        both = p0[160 * g : 160 * g + 160] + p2[160 * g : 160 * g + 160]
        decoded[2 * g] = (u + (both + p1[160 * g : 160 * g + 160])).astype(bf16)
        decoded[2 * g + 1] = (u + (both + p1[160 * g + 160 : 160 * g + 320])).astype(bf16)
    edge = jnp.where(pos[FIRST] == 1, terms[0].astype(f32), 0.0)
    fill_shifts(shifted, 0, terms[1].astype(f32) + edge, True)
    fill_shifts(shifted, 1, terms[2].astype(f32) + after[...].astype(f32), True)
    acc[...] = jnp.zeros((320, 512), f32)

    def step(r, _):
        for s in range(3):
            window = shifted[:, strip_rows(2 - r), 512 * s : 512 * s + 512].reshape(320, 512)
            acc[...] += dot_nt(window, ws[3 * r + s])
        return 0

    lax.fori_loop(0, 3, step, 0)
    for g in range(2):
        u = frames[1 + g].astype(f32)
        sigma = jax.nn.sigmoid(u)
        slope = sigma * (1.0 + u * (1.0 - sigma))
        cotangents = c[2 * g].astype(f32) + c[2 * g + 1].astype(f32)
        grad_input[g] = (cotangents + acc[160 * g : 160 * g + 160] * slope).astype(bf16)


def temporal_weight_grad_kernel(pos, sp, sps, terms, sib_terms, spatial, *refs):
    xs, ys, (early, late, g) = refs[:4], refs[4:8], refs[8:]
    early[...] = core_channels(pos, [ref[k].astype(f32) for ref in (sp, sps) for k in (0, 1)])
    late[...] = core_channels(pos, [ref[k].astype(f32) for ref in (sp, sps) for k in (1, 2)])
    outer = jnp.concatenate([terms[3], terms[5], sib_terms[3], sib_terms[5]], 0)
    inner = jnp.concatenate([terms[6], terms[4], sib_terms[6], sib_terms[4]], 0)
    zeros = jnp.zeros((160, 512), bf16)
    end = jnp.concatenate([zeros, terms[7], zeros, sib_terms[7]], 0)
    g[0:9] = spatial[...]
    g[9] = dot(early[...], outer)
    g[10] = dot(early[...], inner) + dot(late[...], end)
    g[11] = dot(late[...], outer)
    for offset, outx, outy in zip((0,) + RING, xs, ys):
        rows = pl.ds(pl.multiple_of(mod4(pos[Y] + offset) * 64, 64), 64)
        outx[...] = g[pl.ds(3 * mod4(pos[X] + offset), 3), :, :256].astype(outx.dtype)
        outy[...] = g[:, rows, 256:].astype(outy.dtype)


def second_exchange_kernel(pos, *refs):
    (ax, *bx), (ay, *by), xs, ys = refs[:4], refs[4:8], refs[8:12], refs[12:]
    for offset, outx, outy in zip((0,) + RING, xs, ys):
        rows = pl.ds(pl.multiple_of(mod4(pos[Y] + offset) * 64, 64), 64)
        taps = pl.ds(3 * mod4(pos[X] + offset), 3)
        totalx, totaly = ax[:, rows], ay[taps]
        for b in bx:
            totalx += b[:, rows].astype(f32)
        for b in by:
            totaly += b[taps].astype(f32)
        outx[...] = totalx.astype(outx.dtype)
        outy[...] = totaly.astype(outy.dtype)


def third_exchange_kernel(pos, *refs):
    groups, outs = refs[:8], refs[8:]
    for offset, out in zip((0,) + RING, outs):
        rows = pl.ds(pl.multiple_of(mod4(pos[ZL] + offset) * 16, 16), 16)
        for half in range(2):
            a, *others = groups[4 * half : 4 * half + 4]
            total = a[:, rows]
            for b in others:
                total += b[:, rows].astype(f32)
            out[:, :, 256 * half : 256 * half + 256] = total


def final_taps_kernel(pos, g0, g1, g2, g3, spatial, temporal, taps):
    for offset, piece in zip(REL, (g0, g1, g2, g3)):
        taps[pl.ds(3 * mod4(pos[X] - offset), 3)] = piece[...]
    spatial[...] = taps[0:9]
    temporal[...] = taps[9:12]


def exchange(axis_send, values):
    return [axis_send(v, o) for v, o in zip(values, RING)]


def per_device(frames_in, cotangent, w_spatial, w_temporal):
    src = frames_in[0].reshape(2, 160, 512)
    c = cotangent[0].reshape(4, 160, 512)
    first = lax.axis_index("x") * 2 + lax.axis_index("zh") == 0
    pos = jnp.stack(
        [
            lax.axis_index("y"),
            lax.axis_index("zl"),
            lax.axis_index("core"),
            lax.axis_index("x"),
            first.astype(jnp.int32),
        ]
    ).astype(jnp.int32)
    send_x = lambda v, o: along(v, "x", o)
    send_y = lambda v, o: along(v, "y", o)

    gathered_t = jnp.stack([w_temporal] + [along_z(w_temporal, o) for o in RING])
    before = lax.ppermute(src[1], ("x", "zh"), [(i, i + 1) for i in range(7)])
    pieces_s = [w_spatial] + [along_z(w_spatial, o) for o in RING]
    gathered_t = lax.all_gather(gathered_t, "y")
    gathered_t, before, *pieces_s = lax.optimization_barrier((gathered_t, before, *pieces_s))
    gathered_s = lax.all_gather(jnp.stack(pieces_s), "y")
    sibling_t = to_sibling(gathered_t)
    frames = jnp.concatenate([jnp.where(first, src[:1], before[None]), src], 0)
    sib_frames = to_sibling(frames)

    terms, wt = call(
        temporal_grad_kernel,
        [((8, 160, 512), bf16), ((3, 512, 512), bf16)],
        [pltpu.SemaphoreType.DMA((32,))],
        pos, c, gathered_t, sibling_t, any_from=2,
    )
    sib_terms = to_sibling(terms)
    after = lax.ppermute(terms[0], ("x", "zh"), [(i, i - 1) for i in range(1, 8)])

    (one,) = call(
        spatial_weight_grad_kernel,
        [((9, 256, 512), f32)],
        [pltpu.VMEM((256, 960), bf16), pltpu.VMEM((6, 192, 1536), bf16)],
        pos, frames, sib_frames, terms, sib_terms,
    )
    one, gathered_s, after = lax.optimization_barrier((one, gathered_s, after))
    sibling_s = to_sibling(gathered_s)

    sp, ws = call(
        spatial_conv_kernel,
        [((3, 160, 512), bf16), ((9, 512, 512), bf16)],
        [pltpu.VMEM((3, 192, 1536), bf16), pltpu.VMEM((480, 512), f32), pltpu.SemaphoreType.DMA((32,))],
        pos, frames, gathered_s, sibling_s, any_from=2,
    )
    sib_sp = to_sibling(sp)
    part = [((3, 256, 256), f32)] + [((3, 256, 256), bf16)] * 3
    part += [((12, 64, 256), f32)] + [((12, 64, 256), bf16)] * 3
    grads = call(
        temporal_weight_grad_kernel, part,
        [pltpu.VMEM((256, 640), bf16), pltpu.VMEM((256, 640), bf16), pltpu.VMEM((12, 256, 512), f32)],
        pos, sp, sib_sp, terms, sib_terms, one,
    )
    rx, ry = exchange(send_x, grads[1:4]), exchange(send_y, grads[5:8])
    sp, _ = lax.optimization_barrier((sp, grads[0]))
    decoded, grad_input = call(
        outputs_kernel,
        [((4, 160, 512), bf16), ((2, 160, 512), bf16)],
        [pltpu.VMEM((2, 192, 1536), bf16), pltpu.VMEM((320, 512), f32)],
        pos, frames, c, sp, terms, after, wt, ws,
    )
    *rx, decoded = lax.optimization_barrier((*rx, decoded))
    part = [((3, 64, 256), f32)] + [((3, 64, 256), bf16)] * 3
    two = call(second_exchange_kernel, part * 2, [], pos, grads[0], *rx, grads[4], *ry)
    rx, ry = exchange(send_y, two[1:4]), exchange(send_x, two[5:8])
    zs = call(
        third_exchange_kernel, [((3, 16, 512), f32)] * 4, [],
        pos, two[0], *rx, two[4], *ry,
    )
    z1, z2, z3 = exchange(along_z, zs[1:4])
    total = zs[0] + z1 + z2 + z3
    total = total + lax.ppermute(total, "zh", [(0, 1), (1, 0)])
    taps = total * (1.0 / math.sqrt(256 * 640))
    grad_s, grad_t = call(
        final_taps_kernel,
        [((9, 16, 512), f32), ((3, 16, 512), f32)],
        [pltpu.VMEM((12, 16, 512), f32)],
        pos, taps, *[send_x(taps, o) for o in RING],
    )
    return (
        decoded.reshape(1, 4, 10, 16, 512),
        grad_input.reshape(1, 2, 10, 16, 512),
        grad_s,
        grad_t,
    )


def solution(mesh):
    physical = Mesh(mesh.devices.reshape(SIZES), AXES)
    dp, tm = ("y", "zl", "core"), ("x", "zh")
    values, weights = P(dp, tm, None, None, None), P(None, dp, None)
    return jax.shard_map(
        per_device,
        mesh=physical,
        in_specs=(values, values, weights, weights),
        out_specs=(values, values, weights, weights),
        check_vma=False,
    )
```

```python
import math

import jax
import jax.numpy as jnp
from jax import lax
from jax.experimental import pallas as pl
from jax.experimental.pallas import tpu as pltpu
from jax.sharding import Mesh, PartitionSpec as P

f32 = jnp.float32
bf16 = jnp.bfloat16
COST = 1000000
NEAR = 4

AXES = ("y", "zl", "core", "x", "zh")
SIZES = (4, 4, 2, 4, 2)
RING = (1, 3, 2)
REL = (0, 1, 3, 2)
Y, ZL, CORE, X, FIRST = range(5)


def along(value, axis, offset):
    return lax.ppermute(value, axis, [(i, (i + offset) % 4) for i in range(4)])


def along_z(value, offset):
    steps = offset if offset < 3 else 7
    place = lambda z: z % 4 * 2 + z // 4
    return lax.ppermute(value, ("zl", "zh"), [(place(z), place((z + steps) % 8)) for z in range(8)])


def to_sibling(value):
    return lax.ppermute(value, "core", [(0, 1), (1, 0)])


def call(kernel, mib, outs, scratch, *args, any_from=None):
    count = len(args)
    any_from = count if any_from is None else any_from
    specs = [pl.BlockSpec(memory_space=pltpu.SMEM)]
    specs += [
        pl.BlockSpec(memory_space=pltpu.VMEM if i < any_from else pl.ANY) for i in range(1, count)
    ]
    return pl.pallas_call(
        kernel,
        out_shape=[jax.ShapeDtypeStruct(s, d) for s, d in outs],
        in_specs=specs,
        out_specs=[pl.BlockSpec(memory_space=pltpu.VMEM) for _ in outs],
        scratch_shapes=scratch,
        compiler_params=pltpu.CompilerParams(vmem_limit_bytes=mib * 1024 * 1024),
        cost_estimate=pl.CostEstimate(flops=COST, bytes_accessed=0, transcendentals=0),
        name=kernel.__name__,
    )(*args)


def mod4(value):
    return lax.rem(value + 4, 4)


def dot(left, right):
    return jnp.dot(left, right, preferred_element_type=f32)


def dot_nt(left, right):
    return lax.dot_general(left, right, (((1,), (1,)), ((), ())), preferred_element_type=f32)


def placements(pos, pieces, weights, first_tap, last, sems, base):
    copies = []
    for a, piece in enumerate(pieces):
        core = pos[CORE] if a < 4 else 1 - pos[CORE]
        for k in range(4):
            outer, inner = REL[a % 4], REL[k]
            y, zl = (outer, inner) if last == "y" else (inner, outer)
            block = (mod4(pos[Y] - y) * 4 + mod4(pos[ZL] - zl)) * 2 + core
            copies.append(
                pltpu.make_async_copy(
                    piece.at[k],
                    weights.at[
                        pl.ds(first_tap, piece.shape[1]), pl.ds(pl.multiple_of(block * 16, 16), 16), :
                    ],
                    sems.at[base + 4 * a + k],
                )
            )
    return copies


def column_shifts(value):
    rows = value.shape[0]
    column = lax.broadcasted_iota(jnp.int32, value.shape, 0) % 16
    before = jnp.where(column == 0, 0.0, pltpu.roll(value, 1, 0))
    after = jnp.where(column == 15, 0.0, pltpu.roll(value, rows - 1, 0))
    return before, value, after


def fill_shifts(buffer, slot, value, reverse):
    before, centre, after = column_shifts(value)
    width = value.shape[1]
    buffer[slot, :16] = jnp.zeros((16, 3 * width), bf16)
    buffer[slot, 176:] = jnp.zeros((16, 3 * width), bf16)
    for s, shifted in enumerate((after, centre, before) if reverse else (before, centre, after)):
        buffer[slot, 16:176, s * width : (s + 1) * width] = shifted.astype(bf16)


def strip_rows(start):
    return pl.ds(pl.multiple_of(start * 16, 16), 160)


def temporal_grad_kernel(pos, c, *refs):
    pieces, (terms, edge, wt, parts, sems) = refs[:8], refs[8:]
    copies = placements(pos, pieces, wt, 0, "y", sems, 0)
    for copy in copies:
        copy.start()
    frames = [c[k] for k in range(4)]
    for k in range(3):
        terms[3 + k] = (frames[k].astype(f32) + frames[k + 1].astype(f32)).astype(bf16)
    terms[6] = frames[0]
    terms[7] = frames[3]
    for copy in copies:
        copy.wait()

    def step(k, _):
        parts[k] = dot_nt(c[...].reshape(640, 512), wt[k]).reshape(4, 160, 512)
        return 0

    lax.fori_loop(0, 3, step, 0)
    p, q, r = (parts.at[k] for k in range(3))
    edge_value = (p[0] + p[1] + q[0]).astype(bf16)
    edge[...] = edge_value
    terms[0] = edge_value
    terms[1] = (p[2] + p[3] + q[1] + q[2] + r[0] + r[1]).astype(bf16)
    terms[2] = (q[3] + r[2] + r[3]).astype(bf16)


def loop(count, step):
    lax.fori_loop(0, count, lambda k, _: (step(k), 0)[1], 0)


def three_frames(pos, src, before, out):
    first = pos[FIRST] == 1
    out[0] = jnp.where(first, src[0].astype(f32), before[...].astype(f32))
    out[1] = src[0].astype(f32)
    out[2] = src[1].astype(f32)


def core_channels(pos, frames):
    flat = jnp.concatenate(frames, 0)
    parts = flat.T.astype(bf16).reshape(16, 2, 16, flat.shape[0])
    return jnp.where(pos[CORE] == 0, parts[:, 0], parts[:, 1]).reshape(256, flat.shape[0])


def spatial_weight_grad_kernel(
    pos, src, before, sib, sib_before, terms, sib_terms, g, act, act_t, shifted
):
    three_frames(pos, src, before, act.at[0:3])
    three_frames(pos, sib, sib_before, act.at[3:6])

    def silu(k):
        act[k] = jax.nn.silu(act[k])

    loop(6, silu)
    act_t[...] = core_channels(pos, [act[...].reshape(960, 512)])

    def shifts(k):
        fill_shifts(shifted, k, terms[k].astype(f32), True)
        fill_shifts(shifted, 3 + k, sib_terms[k].astype(f32), True)

    loop(3, shifts)

    def step(r, _):
        window = shifted[:, strip_rows(2 - r)].reshape(960, 1536)
        value = dot(act_t[...], window)
        for s in range(3):
            g[3 * r + s] = value[:, 512 * s : 512 * s + 512]
        return 0

    lax.fori_loop(0, 3, step, 0)


def spatial_conv_kernel(pos, src, before, *refs):
    near, far, (out, ws, act, shifted, acc, sems) = refs[:8], refs[8:16], refs[16:]
    copies = placements(pos, near, ws, 0, "y", sems, 0)
    copies += placements(pos, far, ws, NEAR, "z", sems, 32)
    for copy in copies:
        copy.start()
    three_frames(pos, src, before, act)
    loop(3, lambda k: fill_shifts(shifted, k, jax.nn.silu(act[k]), False))
    for copy in copies:
        copy.wait()
    acc[...] = jnp.zeros((480, 512), f32)

    def step(r, _):
        window = shifted[:, strip_rows(r)].reshape(480, 1536)
        acc[...] += dot(window, ws[pl.ds(3 * r, 3)].reshape(1536, 512))
        return 0

    lax.fori_loop(0, 3, step, 0)
    for k in range(3):
        out[k] = acc[160 * k : 160 * k + 160].astype(bf16)


def outputs_kernel(pos, src, c, sp, terms, after, wt, ws, decoded, grad_input, shifted, acc, parts):

    def forward(k, _):
        parts[k] = dot(sp[...].reshape(480, 512), wt[k]).reshape(3, 160, 512)
        return 0

    lax.fori_loop(0, 3, forward, 0)

    def decode(g):
        u = src[g].astype(f32)
        both = parts[0, g] + parts[2, g + 1]
        decoded[2 * g] = (u + (both + parts[1, g])).astype(bf16)
        decoded[2 * g + 1] = (u + (both + parts[1, g + 1])).astype(bf16)

    loop(2, decode)
    edge = jnp.where(pos[FIRST] == 1, terms[0].astype(f32), 0.0)
    fill_shifts(shifted, 0, terms[1].astype(f32) + edge, True)
    fill_shifts(shifted, 1, terms[2].astype(f32) + after[...].astype(f32), True)
    acc[...] = jnp.zeros((320, 512), f32)

    def step(r, _):
        for s in range(3):
            window = shifted[:, strip_rows(2 - r), 512 * s : 512 * s + 512].reshape(320, 512)
            acc[...] += dot_nt(window, ws[3 * r + s])
        return 0

    lax.fori_loop(0, 3, step, 0)

    def finish(g):
        u = src[g].astype(f32)
        sigma = jax.nn.sigmoid(u)
        slope = sigma * (1.0 + u * (1.0 - sigma))
        cotangents = c[2 * g].astype(f32) + c[2 * g + 1].astype(f32)
        rows = pl.ds(pl.multiple_of(160 * g, 160), 160)
        grad_input[g] = (cotangents + acc[rows] * slope).astype(bf16)

    loop(2, finish)


def temporal_weight_grad_kernel(pos, sp, sps, terms, sib_terms, spatial, *refs):
    xs, ys, (early, late, g) = refs[:4], refs[4:8], refs[8:]
    early[...] = core_channels(pos, [ref[k].astype(f32) for ref in (sp, sps) for k in (0, 1)])
    late[...] = core_channels(pos, [ref[k].astype(f32) for ref in (sp, sps) for k in (1, 2)])
    outer = jnp.concatenate([terms[3], terms[5], sib_terms[3], sib_terms[5]], 0)
    inner = jnp.concatenate([terms[6], terms[4], sib_terms[6], sib_terms[4]], 0)
    zeros = jnp.zeros((160, 512), bf16)
    end = jnp.concatenate([zeros, terms[7], zeros, sib_terms[7]], 0)
    g[0] = spatial[8]
    g[1] = dot(early[...], outer)
    g[2] = dot(early[...], inner) + dot(late[...], end)
    g[3] = dot(late[...], outer)
    for offset, outx, outy in zip((0,) + RING, xs, ys):
        rows = pl.ds(pl.multiple_of(mod4(pos[Y] + offset) * 64, 64), 64)
        x = mod4(pos[X] + offset)
        outx[0:2] = spatial[pl.ds(2 * x, 2), :, :256].astype(outx.dtype)
        outx[2] = g[x, :, :256].astype(outx.dtype)
        outy[0:9] = spatial[:, rows, 256:].astype(outy.dtype)
        outy[9:12] = g[1:4, rows, 256:].astype(outy.dtype)


def second_exchange_kernel(pos, *refs):
    (ax, *bx), (ay, *by), xs, ys = refs[:4], refs[4:8], refs[8:12], refs[12:]
    for offset, outx, outy in zip((0,) + RING, xs, ys):
        rows = pl.ds(pl.multiple_of(mod4(pos[Y] + offset) * 64, 64), 64)
        x = mod4(pos[X] + offset)
        total = ax[:, rows]
        for b in bx:
            total += b[:, rows].astype(f32)
        outx[...] = total.astype(outx.dtype)
        for out, taps in ((outy.at[0:2], pl.ds(2 * x, 2)), (outy.at[2:3], pl.ds(8 + x, 1))):
            total = ay[taps]
            for b in by:
                total += b[taps].astype(f32)
            out[...] = total.astype(outy.dtype)


def third_exchange_kernel(pos, *refs):
    groups, outs = refs[:8], refs[8:]
    for offset, out in zip((0,) + RING, outs):
        rows = pl.ds(pl.multiple_of(mod4(pos[ZL] + offset) * 16, 16), 16)
        for half in range(2):
            a, *others = groups[4 * half : 4 * half + 4]
            total = a[:, rows]
            for b in others:
                total += b[:, rows].astype(f32)
            out[:, :, 256 * half : 256 * half + 256] = total.astype(out.dtype)


def final_taps_kernel(pos, g0, g1, g2, g3, spatial, temporal, taps):
    for offset, piece in zip(REL, (g0, g1, g2, g3)):
        x = mod4(pos[X] - offset)
        taps[pl.ds(2 * x, 2)] = piece[0:2].astype(f32)
        taps[8 + x] = piece[2].astype(f32)
    spatial[...] = taps[0:9]
    temporal[...] = taps[9:12]


def exchange(axis_send, values):
    return [axis_send(v, o) for v, o in zip(values, RING)]


def per_device(frames_in, cotangent, w_spatial, w_temporal):
    src = frames_in[0].reshape(2, 160, 512)
    c = cotangent[0].reshape(4, 160, 512)
    first = lax.axis_index("x") * 2 + lax.axis_index("zh") == 0
    pos = jnp.stack(
        [
            lax.axis_index("y"),
            lax.axis_index("zl"),
            lax.axis_index("core"),
            lax.axis_index("x"),
            first.astype(jnp.int32),
        ]
    ).astype(jnp.int32)
    send_x = lambda v, o: along(v, "x", o)
    send_y = lambda v, o: along(v, "y", o)

    mixed = jnp.concatenate([w_temporal, w_spatial[:NEAR]], 0)
    mixed = [mixed] + [along_z(mixed, o) for o in RING]
    far = w_spatial[NEAR:]
    far = jnp.stack([far] + [send_y(far, o) for o in RING])
    temporal = jnp.stack([piece[:3] for piece in mixed])
    near = jnp.stack([piece[3:] for piece in mixed])
    before = lax.ppermute(src[1], ("x", "zh"), [(i, i + 1) for i in range(7)])
    temporal = [temporal] + [send_y(temporal, o) for o in RING]
    temporal += [to_sibling(piece) for piece in temporal]
    near = [near] + [send_y(near, o) for o in RING]
    far = [far] + [along_z(far, o) for o in RING]
    sib_src = to_sibling(src)
    sib_before = to_sibling(before)

    terms, edge, wt = call(
        temporal_grad_kernel, 18,
        [((8, 160, 512), bf16), ((160, 512), bf16), ((3, 512, 512), bf16)],
        [pltpu.VMEM((3, 4, 160, 512), f32), pltpu.SemaphoreType.DMA((32,))],
        pos, c, *temporal, any_from=2,
    )
    sib_terms = to_sibling(terms)
    after = lax.ppermute(edge, ("x", "zh"), [(i, i - 1) for i in range(1, 8)])
    (one,) = call(
        spatial_weight_grad_kernel, 28,
        [((9, 256, 512), f32)],
        [pltpu.VMEM((6, 160, 512), f32), pltpu.VMEM((256, 960), bf16), pltpu.VMEM((6, 192, 1536), bf16)],
        pos, src, before, sib_src, sib_before, terms, sib_terms,
    )
    near += [to_sibling(piece) for piece in near]
    far += [to_sibling(piece) for piece in far]
    one, after, near[0] = lax.optimization_barrier((one, after, near[0]))

    sp, ws = call(
        spatial_conv_kernel, 20,
        [((3, 160, 512), bf16), ((9, 512, 512), bf16)],
        [
            pltpu.VMEM((3, 160, 512), f32), pltpu.VMEM((3, 192, 1536), bf16),
            pltpu.VMEM((480, 512), f32), pltpu.SemaphoreType.DMA((64,)),
        ],
        pos, src, before, *near, *far, any_from=3,
    )
    sib_sp = to_sibling(sp)
    part = [((3, 256, 256), f32)] + [((3, 256, 256), bf16)] * 3
    part += [((12, 64, 256), f32)] + [((12, 64, 256), bf16)] * 3
    grads = call(
        temporal_weight_grad_kernel, 28, part,
        [pltpu.VMEM((256, 640), bf16), pltpu.VMEM((256, 640), bf16), pltpu.VMEM((4, 256, 512), f32)],
        pos, sp, sib_sp, terms, sib_terms, one,
    )
    rx, ry = exchange(send_x, grads[1:4]), exchange(send_y, grads[5:8])
    sp, _ = lax.optimization_barrier((sp, grads[0]))
    decoded, grad_input = call(
        outputs_kernel, 26,
        [((4, 160, 512), bf16), ((2, 160, 512), bf16)],
        [pltpu.VMEM((2, 192, 1536), bf16), pltpu.VMEM((320, 512), f32), pltpu.VMEM((3, 3, 160, 512), f32)],
        pos, src, c, sp, terms, after, wt, ws,
    )
    *rx, decoded = lax.optimization_barrier((*rx, decoded))
    part = [((3, 64, 256), f32)] + [((3, 64, 256), bf16)] * 3
    two = call(second_exchange_kernel, 10, part * 2, [], pos, grads[0], *rx, grads[4], *ry)
    rx, ry = exchange(send_y, two[1:4]), exchange(send_x, two[5:8])
    zs = call(
        third_exchange_kernel, 8, [((3, 16, 512), f32)] + [((3, 16, 512), bf16)] * 3, [],
        pos, two[0], *rx, two[4], *ry,
    )
    total = zs[0] + sum(part.astype(f32) for part in exchange(along_z, zs[1:4]))
    other = lax.ppermute(total.astype(bf16), "zh", [(0, 1), (1, 0)])
    taps = (total + other.astype(f32)) * (1.0 / math.sqrt(256 * 640))
    grad_s, grad_t = call(
        final_taps_kernel, 4,
        [((9, 16, 512), f32), ((3, 16, 512), f32)],
        [pltpu.VMEM((12, 16, 512), f32)],
        pos, taps, *[send_x(taps, o) for o in RING],
    )
    return (
        decoded.reshape(1, 4, 10, 16, 512),
        grad_input.reshape(1, 2, 10, 16, 512),
        grad_s,
        grad_t,
    )


def solution(mesh):
    physical = Mesh(mesh.devices.reshape(SIZES), AXES)
    dp, tm = ("y", "zl", "core"), ("x", "zh")
    values, weights = P(dp, tm, None, None, None), P(None, dp, None)
    return jax.shard_map(
        per_device,
        mesh=physical,
        in_specs=(values, values, weights, weights),
        out_specs=(values, values, weights, weights),
        check_vma=False,
    )
```

```python
import math

import jax
import jax.numpy as jnp
from jax import lax
from jax.experimental import pallas as pl
from jax.experimental.pallas import tpu as pltpu
from jax.sharding import Mesh, PartitionSpec as P

f32 = jnp.float32
bf16 = jnp.bfloat16
COST = 1000000
FAR = 2

AXES = ("y", "zl", "core", "x", "zh")
SIZES = (4, 4, 2, 4, 2)
RING = (2, 1, 3)
REL = (0, 2, 1, 3)
Y, ZL, CORE, X, FIRST = range(5)


def along(value, axis, offset):
    return lax.ppermute(value, axis, [(i, (i + offset) % 4) for i in range(4)])


def along_z(value, offset):
    steps = 7 if offset == 3 else offset
    place = lambda z: z % 4 * 2 + z // 4
    return lax.ppermute(value, ("zl", "zh"), [(place(z), place((z + steps) % 8)) for z in range(8)])


def to_sibling(value):
    return lax.ppermute(value, "core", [(0, 1), (1, 0)])


def call(kernel, mib, outs, scratch, *args, any_from=None):
    count = len(args)
    any_from = count if any_from is None else any_from
    specs = [pl.BlockSpec(memory_space=pltpu.SMEM)]
    specs += [
        pl.BlockSpec(memory_space=pltpu.VMEM if i < any_from else pl.ANY) for i in range(1, count)
    ]
    return pl.pallas_call(
        kernel,
        out_shape=[jax.ShapeDtypeStruct(s, d) for s, d in outs],
        in_specs=specs,
        out_specs=[pl.BlockSpec(memory_space=pltpu.VMEM) for _ in outs],
        scratch_shapes=scratch,
        compiler_params=pltpu.CompilerParams(vmem_limit_bytes=mib * 1024 * 1024),
        cost_estimate=pl.CostEstimate(flops=COST, bytes_accessed=0, transcendentals=0),
        name=kernel.__name__,
    )(*args)


def mod4(value):
    return lax.rem(value + 4, 4)


def dot(left, right):
    return jnp.dot(left, right, preferred_element_type=f32)


def dot_nt(left, right):
    return lax.dot_general(left, right, (((1,), (1,)), ((), ())), preferred_element_type=f32)


def placements(pos, pieces, taps, weights, first_tap, last, sems, base):
    copies = []
    for a, piece in enumerate(pieces):
        core = pos[CORE] if a < 4 else 1 - pos[CORE]
        for k in range(4):
            outer, inner = REL[a % 4], REL[k]
            y, zl = (outer, inner) if last == "y" else (inner, outer)
            block = (mod4(pos[Y] - y) * 4 + mod4(pos[ZL] - zl)) * 2 + core
            copies.append(
                pltpu.make_async_copy(
                    piece.at[k, taps],
                    weights.at[
                        first_tap : first_tap + taps.stop - taps.start,
                        pl.ds(pl.multiple_of(block * 16, 16), 16),
                        :,
                    ],
                    sems.at[base + 4 * a + k],
                )
            )
    return copies


def column_shifts(value):
    rows = value.shape[0]
    column = lax.broadcasted_iota(jnp.int32, value.shape, 0) % 16
    before = jnp.where(column == 0, 0.0, pltpu.roll(value, 1, 0))
    after = jnp.where(column == 15, 0.0, pltpu.roll(value, rows - 1, 0))
    return before, value, after


def fill_shifts(buffer, slot, value, reverse):
    before, centre, after = column_shifts(value)
    width = value.shape[1]
    buffer[slot, :16] = jnp.zeros((16, 3 * width), bf16)
    buffer[slot, 176:] = jnp.zeros((16, 3 * width), bf16)
    for s, shifted in enumerate((after, centre, before) if reverse else (before, centre, after)):
        buffer[slot, 16:176, s * width : (s + 1) * width] = shifted.astype(bf16)


def strip_rows(start):
    return pl.ds(pl.multiple_of(start * 16, 16), 160)


def loop(count, step):
    lax.fori_loop(0, count, lambda k, _: (step(k), 0)[1], 0)


def temporal_grad_kernel(pos, c, *refs):
    far, (terms, edge, wt, parts, sems) = refs[:8], refs[8:]
    copies = placements(pos, far, slice(0, 3), wt, 0, "z", sems, 0)
    for copy in copies:
        copy.start()
    frames = [c[k] for k in range(4)]
    for k in range(3):
        terms[3 + k] = (frames[k].astype(f32) + frames[k + 1].astype(f32)).astype(bf16)
    terms[6] = frames[0]
    terms[7] = frames[3]
    for copy in copies:
        copy.wait()

    def step(k, _):
        parts[k] = dot_nt(c[...].reshape(640, 512), wt[k]).reshape(4, 160, 512)
        return 0

    lax.fori_loop(0, 3, step, 0)
    p, q, r = (parts.at[k] for k in range(3))
    edge_value = (p[0] + p[1] + q[0]).astype(bf16)
    edge[...] = edge_value
    terms[0] = edge_value
    terms[1] = (p[2] + p[3] + q[1] + q[2] + r[0] + r[1]).astype(bf16)
    terms[2] = (q[3] + r[2] + r[3]).astype(bf16)


def loop(count, step):
    lax.fori_loop(0, count, lambda k, _: (step(k), 0)[1], 0)


def core_channels(pos, frames):
    flat = jnp.concatenate(frames, 0)
    parts = flat.T.astype(bf16).reshape(16, 2, 16, flat.shape[0])
    return jnp.where(pos[CORE] == 0, parts[:, 0], parts[:, 1]).reshape(256, flat.shape[0])


def spatial_weight_grad_kernel(
    pos, frames, sib_frames, terms, sib_terms, g, act, act_t, shifted
):

    def silu(k):
        act[k] = jax.nn.silu(frames[k].astype(f32))
        act[3 + k] = jax.nn.silu(sib_frames[k].astype(f32))

    loop(3, silu)
    act_t[...] = core_channels(pos, [act[...].reshape(960, 512)])

    def shifts(k):
        fill_shifts(shifted, k, terms[k].astype(f32), True)
        fill_shifts(shifted, 3 + k, sib_terms[k].astype(f32), True)

    loop(3, shifts)

    def step(r, _):
        window = shifted[:, strip_rows(2 - r)].reshape(960, 1536)
        value = dot(act_t[...], window)
        for s in range(3):
            g[3 * r + s] = value[:, 512 * s : 512 * s + 512]
        return 0

    lax.fori_loop(0, 3, step, 0)


def spatial_conv_kernel(pos, frames, *refs):
    far, near, (out, ws, shifted, acc, sems) = refs[:8], refs[8:16], refs[16:]
    copies = placements(pos, far, slice(3, 3 + FAR), ws, 0, "z", sems, 0)
    copies += placements(pos, near, slice(0, 9 - FAR), ws, FAR, "y", sems, 32)
    for copy in copies:
        copy.start()
    loop(3, lambda k: fill_shifts(shifted, k, jax.nn.silu(frames[k].astype(f32)), False))
    for copy in copies:
        copy.wait()
    acc[...] = jnp.zeros((480, 512), f32)

    def step(r, _):
        window = shifted[:, strip_rows(r)].reshape(480, 1536)
        acc[...] += dot(window, ws[pl.ds(3 * r, 3)].reshape(1536, 512))
        return 0

    lax.fori_loop(0, 3, step, 0)
    for k in range(3):
        out[k] = acc[160 * k : 160 * k + 160].astype(bf16)


def outputs_kernel(pos, src, c, sp, terms, after, wt, ws, decoded, grad_input, shifted, acc, parts):

    def forward(k, _):
        parts[k] = dot(sp[...].reshape(480, 512), wt[k]).reshape(3, 160, 512)
        return 0

    lax.fori_loop(0, 3, forward, 0)

    def decode(g):
        u = src[g].astype(f32)
        both = parts[0, g] + parts[2, g + 1]
        decoded[2 * g] = (u + (both + parts[1, g])).astype(bf16)
        decoded[2 * g + 1] = (u + (both + parts[1, g + 1])).astype(bf16)

    loop(2, decode)
    edge = jnp.where(pos[FIRST] == 1, terms[0].astype(f32), 0.0)
    fill_shifts(shifted, 0, terms[1].astype(f32) + edge, True)
    fill_shifts(shifted, 1, terms[2].astype(f32) + after[...].astype(f32), True)
    acc[...] = jnp.zeros((320, 512), f32)

    def step(r, _):
        for s in range(3):
            window = shifted[:, strip_rows(2 - r), 512 * s : 512 * s + 512].reshape(320, 512)
            acc[...] += dot_nt(window, ws[3 * r + s])
        return 0

    lax.fori_loop(0, 3, step, 0)

    def finish(g):
        u = src[g].astype(f32)
        sigma = jax.nn.sigmoid(u)
        slope = sigma * (1.0 + u * (1.0 - sigma))
        cotangents = c[2 * g].astype(f32) + c[2 * g + 1].astype(f32)
        rows = pl.ds(pl.multiple_of(160 * g, 160), 160)
        grad_input[g] = (cotangents + acc[rows] * slope).astype(bf16)

    loop(2, finish)


def temporal_weight_grad_kernel(pos, sp, sps, terms, sib_terms, spatial, *refs):
    xs, ys, (early, late, g) = refs[:4], refs[4:8], refs[8:]
    early[...] = core_channels(pos, [ref[k].astype(f32) for ref in (sp, sps) for k in (0, 1)])
    late[...] = core_channels(pos, [ref[k].astype(f32) for ref in (sp, sps) for k in (1, 2)])
    outer = jnp.concatenate([terms[3], terms[5], sib_terms[3], sib_terms[5]], 0)
    inner = jnp.concatenate([terms[6], terms[4], sib_terms[6], sib_terms[4]], 0)
    zeros = jnp.zeros((160, 512), bf16)
    end = jnp.concatenate([zeros, terms[7], zeros, sib_terms[7]], 0)
    g[0] = spatial[8]
    g[1] = dot(early[...], outer)
    g[2] = dot(early[...], inner) + dot(late[...], end)
    g[3] = dot(late[...], outer)
    for offset, outx, outy in zip((0,) + RING, xs, ys):
        rows = pl.ds(pl.multiple_of(mod4(pos[Y] + offset) * 64, 64), 64)
        x = mod4(pos[X] + offset)
        outx[0:2] = spatial[pl.ds(2 * x, 2), :, :256].astype(outx.dtype)
        outx[2] = g[x, :, :256].astype(outx.dtype)
        outy[0:9] = spatial[:, rows, 256:].astype(outy.dtype)
        outy[9:12] = g[1:4, rows, 256:].astype(outy.dtype)


def second_exchange_kernel(pos, *refs):
    (ax, *bx), (ay, *by), xs, ys = refs[:4], refs[4:8], refs[8:12], refs[12:]
    for offset, outx, outy in zip((0,) + RING, xs, ys):
        rows = pl.ds(pl.multiple_of(mod4(pos[Y] + offset) * 64, 64), 64)
        x = mod4(pos[X] + offset)
        total = ax[:, rows]
        for b in bx:
            total += b[:, rows].astype(f32)
        outx[...] = total.astype(outx.dtype)
        for out, taps in ((outy.at[0:2], pl.ds(2 * x, 2)), (outy.at[2:3], pl.ds(8 + x, 1))):
            total = ay[taps]
            for b in by:
                total += b[taps].astype(f32)
            out[...] = total.astype(outy.dtype)


def third_exchange_kernel(pos, *refs):
    groups, outs = refs[:8], refs[8:]
    for offset, out in zip((0,) + RING, outs):
        rows = pl.ds(pl.multiple_of(mod4(pos[ZL] + offset) * 16, 16), 16)
        for half in range(2):
            a, *others = groups[4 * half : 4 * half + 4]
            total = a[:, rows]
            for b in others:
                total += b[:, rows].astype(f32)
            out[:, :, 256 * half : 256 * half + 256] = total.astype(out.dtype)


def final_taps_kernel(pos, g0, g1, g2, g3, spatial, temporal, taps):
    for offset, piece in zip(REL, (g0, g1, g2, g3)):
        x = mod4(pos[X] - offset)
        taps[pl.ds(2 * x, 2)] = piece[0:2].astype(f32)
        taps[8 + x] = piece[2].astype(f32)
    spatial[...] = taps[0:9]
    temporal[...] = taps[9:12]


def exchange(axis_send, values):
    return [axis_send(v, o) for v, o in zip(values, RING)]


def per_device(frames_in, cotangent, w_spatial, w_temporal):
    src = frames_in[0].reshape(2, 160, 512)
    c = cotangent[0].reshape(4, 160, 512)
    first = lax.axis_index("x") * 2 + lax.axis_index("zh") == 0
    pos = jnp.stack(
        [
            lax.axis_index("y"),
            lax.axis_index("zl"),
            lax.axis_index("core"),
            lax.axis_index("x"),
            first.astype(jnp.int32),
        ]
    ).astype(jnp.int32)
    send_x = lambda v, o: along(v, "x", o)
    send_y = lambda v, o: along(v, "y", o)

    near = w_spatial[FAR:]
    far = jnp.concatenate([w_temporal, w_spatial[:FAR]], 0)
    near = jnp.stack([near] + [along_z(near, o) for o in RING])
    far = jnp.stack([far] + [send_y(far, o) for o in RING])
    far, near = lax.optimization_barrier((far, near))
    near = [near] + [send_y(near, o) for o in RING]
    far = [far] + [along_z(far, o) for o in RING]
    before = lax.ppermute(src[1], ("x", "zh"), [(i, i + 1) for i in range(7)])
    c_late, before, *_ = lax.optimization_barrier((c, before, *near[1:], *far[1:]))
    near += [to_sibling(piece) for piece in near]
    far += [to_sibling(piece) for piece in far]
    frames = jnp.concatenate([jnp.where(first, src[0], before)[None], src], 0)
    sib_frames = to_sibling(frames)

    terms, edge, wt = call(
        temporal_grad_kernel, 18,
        [((8, 160, 512), bf16), ((160, 512), bf16), ((3, 512, 512), bf16)],
        [pltpu.VMEM((3, 4, 160, 512), f32), pltpu.SemaphoreType.DMA((32,))],
        pos, c_late, *far, any_from=2,
    )
    after = lax.ppermute(edge, ("x", "zh"), [(i, i - 1) for i in range(1, 8)])
    sib_terms = to_sibling(terms)
    (one,) = call(
        spatial_weight_grad_kernel, 28,
        [((9, 256, 512), f32)],
        [pltpu.VMEM((6, 160, 512), f32), pltpu.VMEM((256, 960), bf16), pltpu.VMEM((6, 192, 1536), bf16)],
        pos, frames, sib_frames, terms, sib_terms,
    )
    sp, ws = call(
        spatial_conv_kernel, 20,
        [((3, 160, 512), bf16), ((9, 512, 512), bf16)],
        [pltpu.VMEM((3, 192, 1536), bf16), pltpu.VMEM((480, 512), f32), pltpu.SemaphoreType.DMA((64,))],
        pos, frames, *far, *near, any_from=2,
    )
    sib_sp = to_sibling(sp)
    one, after = lax.optimization_barrier((one, after))
    part = [((3, 256, 256), f32)] + [((3, 256, 256), bf16)] * 3
    part += [((12, 64, 256), f32)] + [((12, 64, 256), bf16)] * 3
    grads = call(
        temporal_weight_grad_kernel, 28, part,
        [pltpu.VMEM((256, 640), bf16), pltpu.VMEM((256, 640), bf16), pltpu.VMEM((4, 256, 512), f32)],
        pos, sp, sib_sp, terms, sib_terms, one,
    )
    rx, ry = exchange(send_x, grads[1:4]), exchange(send_y, grads[5:8])
    sp, _ = lax.optimization_barrier((sp, grads[0]))
    decoded, grad_input = call(
        outputs_kernel, 26,
        [((4, 160, 512), bf16), ((2, 160, 512), bf16)],
        [pltpu.VMEM((2, 192, 1536), bf16), pltpu.VMEM((320, 512), f32), pltpu.VMEM((3, 3, 160, 512), f32)],
        pos, src, c, sp, terms, after, wt, ws,
    )
    *rx, decoded = lax.optimization_barrier((*rx, decoded))
    part = [((3, 64, 256), f32)] + [((3, 64, 256), bf16)] * 3
    two = call(second_exchange_kernel, 10, part * 2, [], pos, grads[0], *rx, grads[4], *ry)
    rx, ry = exchange(send_y, two[1:4]), exchange(send_x, two[5:8])
    zs = call(
        third_exchange_kernel, 8, [((3, 16, 512), f32)] + [((3, 16, 512), bf16)] * 3, [],
        pos, two[0], *rx, two[4], *ry,
    )
    total = zs[0] + sum(part.astype(f32) for part in exchange(along_z, zs[1:4]))
    other = lax.ppermute(total.astype(bf16), "zh", [(0, 1), (1, 0)])
    taps = (total + other.astype(f32)) * (1.0 / math.sqrt(256 * 640))
    grad_s, grad_t = call(
        final_taps_kernel, 4,
        [((9, 16, 512), f32), ((3, 16, 512), f32)],
        [pltpu.VMEM((12, 16, 512), f32)],
        pos, taps, *[send_x(taps, o) for o in RING],
    )
    return (
        decoded.reshape(1, 4, 10, 16, 512),
        grad_input.reshape(1, 2, 10, 16, 512),
        grad_s,
        grad_t,
    )


def solution(mesh):
    physical = Mesh(mesh.devices.reshape(SIZES), AXES)
    dp, tm = ("y", "zl", "core"), ("x", "zh")
    values, weights = P(dp, tm, None, None, None), P(None, dp, None)
    return jax.shard_map(
        per_device,
        mesh=physical,
        in_specs=(values, values, weights, weights),
        out_specs=(values, values, weights, weights),
        check_vma=False,
    )
```

```python
import math

import jax
import jax.numpy as jnp
from jax import lax
from jax.experimental import pallas as pl
from jax.experimental.pallas import tpu as pltpu
from jax.sharding import Mesh, PartitionSpec as P

f32 = jnp.float32
bf16 = jnp.bfloat16
RATE = 1000000000
FAR = 2

AXES = ("y", "zl", "core", "x", "zh")
SIZES = (4, 4, 2, 4, 2)
RING = (2, 1, 3)
REL = (0, 2, 1, 3)
Y, ZL, CORE, X, FIRST = range(5)


def along(value, axis, offset):
    return lax.ppermute(value, axis, [(i, (i + offset) % 4) for i in range(4)])


def along_z(value, offset):
    steps = 7 if offset == 3 else offset
    place = lambda z: z % 4 * 2 + z // 4
    return lax.ppermute(value, ("zl", "zh"), [(place(z), place((z + steps) % 8)) for z in range(8)])


def to_sibling(value):
    return lax.ppermute(value, "core", [(0, 1), (1, 0)])


def call(kernel, mib, micros, outs, scratch, *args, any_from=None):
    count = len(args)
    any_from = count if any_from is None else any_from
    specs = [pl.BlockSpec(memory_space=pltpu.SMEM)]
    specs += [
        pl.BlockSpec(memory_space=pltpu.VMEM if i < any_from else pl.ANY) for i in range(1, count)
    ]
    return pl.pallas_call(
        kernel,
        out_shape=[jax.ShapeDtypeStruct(s, d) for s, d in outs],
        in_specs=specs,
        out_specs=[pl.BlockSpec(memory_space=pltpu.VMEM) for _ in outs],
        scratch_shapes=scratch,
        compiler_params=pltpu.CompilerParams(vmem_limit_bytes=mib * 1024 * 1024),
        cost_estimate=pl.CostEstimate(flops=micros * RATE, bytes_accessed=0, transcendentals=0),
        name=kernel.__name__,
    )(*args)


def mod4(value):
    return lax.rem(value + 4, 4)


def dot(left, right):
    return jnp.dot(left, right, preferred_element_type=f32)


def dot_nt(left, right):
    return lax.dot_general(left, right, (((1,), (1,)), ((), ())), preferred_element_type=f32)


def placements(pos, pieces, taps, weights, first_tap, last, sems, base):
    copies = []
    for a, piece in enumerate(pieces):
        core = pos[CORE] if a < 4 else 1 - pos[CORE]
        for k in range(4):
            outer, inner = REL[a % 4], REL[k]
            y, zl = (outer, inner) if last == "y" else (inner, outer)
            block = (mod4(pos[Y] - y) * 4 + mod4(pos[ZL] - zl)) * 2 + core
            copies.append(
                pltpu.make_async_copy(
                    piece.at[k, taps],
                    weights.at[
                        first_tap : first_tap + taps.stop - taps.start,
                        pl.ds(pl.multiple_of(block * 16, 16), 16),
                        :,
                    ],
                    sems.at[base + 4 * a + k],
                )
            )
    return copies


def column_shifts(value):
    rows = value.shape[0]
    column = lax.broadcasted_iota(jnp.int32, value.shape, 0) % 16
    before = jnp.where(column == 0, 0.0, pltpu.roll(value, 1, 0))
    after = jnp.where(column == 15, 0.0, pltpu.roll(value, rows - 1, 0))
    return before, value, after


def fill_shifts(buffer, slot, value, reverse):
    before, centre, after = column_shifts(value)
    width = value.shape[1]
    buffer[slot, :16] = jnp.zeros((16, 3 * width), bf16)
    buffer[slot, 176:] = jnp.zeros((16, 3 * width), bf16)
    for s, shifted in enumerate((after, centre, before) if reverse else (before, centre, after)):
        buffer[slot, 16:176, s * width : (s + 1) * width] = shifted.astype(bf16)


def strip_rows(start):
    return pl.ds(pl.multiple_of(start * 16, 16), 160)


def loop(count, step):
    lax.fori_loop(0, count, lambda k, _: (step(k), 0)[1], 0)


def temporal_grad_kernel(pos, c, *refs):
    far, (terms, edge, wt, parts, sems) = refs[:8], refs[8:]
    copies = placements(pos, far, slice(0, 3), wt, 0, "z", sems, 0)
    for copy in copies:
        copy.start()
    frames = [c[k] for k in range(4)]
    for k in range(3):
        terms[3 + k] = (frames[k].astype(f32) + frames[k + 1].astype(f32)).astype(bf16)
    terms[6] = frames[0]
    terms[7] = frames[3]
    for copy in copies:
        copy.wait()

    def step(k, _):
        parts[k] = dot_nt(c[...].reshape(640, 512), wt[k]).reshape(4, 160, 512)
        return 0

    lax.fori_loop(0, 3, step, 0)
    p, q, r = (parts.at[k] for k in range(3))
    edge_value = (p[0] + p[1] + q[0]).astype(bf16)
    edge[...] = edge_value
    terms[0] = edge_value
    terms[1] = (p[2] + p[3] + q[1] + q[2] + r[0] + r[1]).astype(bf16)
    terms[2] = (q[3] + r[2] + r[3]).astype(bf16)


def loop(count, step):
    lax.fori_loop(0, count, lambda k, _: (step(k), 0)[1], 0)


def core_channels(pos, frames):
    flat = jnp.concatenate(frames, 0)
    parts = flat.T.astype(bf16).reshape(16, 2, 16, flat.shape[0])
    return jnp.where(pos[CORE] == 0, parts[:, 0], parts[:, 1]).reshape(256, flat.shape[0])


def spatial_weight_grad_kernel(
    pos, frames, sib_frames, terms, sib_terms, g, act, act_t, shifted
):

    def silu(k):
        act[k] = jax.nn.silu(frames[k].astype(f32))
        act[3 + k] = jax.nn.silu(sib_frames[k].astype(f32))

    loop(3, silu)
    act_t[...] = core_channels(pos, [act[...].reshape(960, 512)])

    def shifts(k):
        fill_shifts(shifted, k, terms[k].astype(f32), True)
        fill_shifts(shifted, 3 + k, sib_terms[k].astype(f32), True)

    loop(3, shifts)

    def step(r, _):
        window = shifted[:, strip_rows(2 - r)].reshape(960, 1536)
        value = dot(act_t[...], window)
        for s in range(3):
            g[3 * r + s] = value[:, 512 * s : 512 * s + 512]
        return 0

    lax.fori_loop(0, 3, step, 0)


def spatial_conv_kernel(pos, frames, *refs):
    far, near, (out, ws, shifted, acc, sems) = refs[:8], refs[8:16], refs[16:]
    copies = placements(pos, far, slice(3, 3 + FAR), ws, 0, "z", sems, 0)
    copies += placements(pos, near, slice(0, 9 - FAR), ws, FAR, "y", sems, 32)
    for copy in copies:
        copy.start()
    loop(3, lambda k: fill_shifts(shifted, k, jax.nn.silu(frames[k].astype(f32)), False))
    for copy in copies:
        copy.wait()
    acc[...] = jnp.zeros((480, 512), f32)

    def step(r, _):
        window = shifted[:, strip_rows(r)].reshape(480, 1536)
        acc[...] += dot(window, ws[pl.ds(3 * r, 3)].reshape(1536, 512))
        return 0

    lax.fori_loop(0, 3, step, 0)
    for k in range(3):
        out[k] = acc[160 * k : 160 * k + 160].astype(bf16)


def outputs_kernel(pos, src, c, sp, terms, after, wt, ws, decoded, grad_input, shifted, acc, parts):

    def forward(k, _):
        parts[k] = dot(sp[...].reshape(480, 512), wt[k]).reshape(3, 160, 512)
        return 0

    lax.fori_loop(0, 3, forward, 0)

    def decode(g):
        u = src[g].astype(f32)
        both = parts[0, g] + parts[2, g + 1]
        decoded[2 * g] = (u + (both + parts[1, g])).astype(bf16)
        decoded[2 * g + 1] = (u + (both + parts[1, g + 1])).astype(bf16)

    loop(2, decode)
    edge = jnp.where(pos[FIRST] == 1, terms[0].astype(f32), 0.0)
    fill_shifts(shifted, 0, terms[1].astype(f32) + edge, True)
    fill_shifts(shifted, 1, terms[2].astype(f32) + after[...].astype(f32), True)
    acc[...] = jnp.zeros((320, 512), f32)

    def step(r, _):
        for s in range(3):
            window = shifted[:, strip_rows(2 - r), 512 * s : 512 * s + 512].reshape(320, 512)
            acc[...] += dot_nt(window, ws[3 * r + s])
        return 0

    lax.fori_loop(0, 3, step, 0)

    def finish(g):
        u = src[g].astype(f32)
        sigma = jax.nn.sigmoid(u)
        slope = sigma * (1.0 + u * (1.0 - sigma))
        cotangents = c[2 * g].astype(f32) + c[2 * g + 1].astype(f32)
        rows = pl.ds(pl.multiple_of(160 * g, 160), 160)
        grad_input[g] = (cotangents + acc[rows] * slope).astype(bf16)

    loop(2, finish)


def temporal_weight_grad_kernel(pos, sp, sps, terms, sib_terms, spatial, *refs):
    xs, ys, (early, late, g) = refs[:4], refs[4:8], refs[8:]
    early[...] = core_channels(pos, [ref[k].astype(f32) for ref in (sp, sps) for k in (0, 1)])
    late[...] = core_channels(pos, [ref[k].astype(f32) for ref in (sp, sps) for k in (1, 2)])
    outer = jnp.concatenate([terms[3], terms[5], sib_terms[3], sib_terms[5]], 0)
    inner = jnp.concatenate([terms[6], terms[4], sib_terms[6], sib_terms[4]], 0)
    zeros = jnp.zeros((160, 512), bf16)
    end = jnp.concatenate([zeros, terms[7], zeros, sib_terms[7]], 0)
    g[0] = spatial[8]
    g[1] = dot(early[...], outer)
    g[2] = dot(early[...], inner) + dot(late[...], end)
    g[3] = dot(late[...], outer)
    for offset, outx, outy in zip((0,) + RING, xs, ys):
        rows = pl.ds(pl.multiple_of(mod4(pos[Y] + offset) * 64, 64), 64)
        x = mod4(pos[X] + offset)
        outx[0:2] = spatial[pl.ds(2 * x, 2), :, :256].astype(outx.dtype)
        outx[2] = g[x, :, :256].astype(outx.dtype)
        outy[0:9] = spatial[:, rows, 256:].astype(outy.dtype)
        outy[9:12] = g[1:4, rows, 256:].astype(outy.dtype)


def second_exchange_kernel(pos, *refs):
    (ax, *bx), (ay, *by), xs, ys = refs[:4], refs[4:8], refs[8:12], refs[12:]
    for offset, outx, outy in zip((0,) + RING, xs, ys):
        rows = pl.ds(pl.multiple_of(mod4(pos[Y] + offset) * 64, 64), 64)
        x = mod4(pos[X] + offset)
        total = ax[:, rows]
        for b in bx:
            total += b[:, rows].astype(f32)
        outx[...] = total.astype(outx.dtype)
        for out, taps in ((outy.at[0:2], pl.ds(2 * x, 2)), (outy.at[2:3], pl.ds(8 + x, 1))):
            total = ay[taps]
            for b in by:
                total += b[taps].astype(f32)
            out[...] = total.astype(outy.dtype)


def third_exchange_kernel(pos, *refs):
    groups, outs = refs[:8], refs[8:]
    for offset, out in zip((0,) + RING, outs):
        rows = pl.ds(pl.multiple_of(mod4(pos[ZL] + offset) * 16, 16), 16)
        for half in range(2):
            a, *others = groups[4 * half : 4 * half + 4]
            total = a[:, rows]
            for b in others:
                total += b[:, rows].astype(f32)
            out[:, :, 256 * half : 256 * half + 256] = total.astype(out.dtype)


def final_taps_kernel(pos, g0, g1, g2, g3, spatial, temporal, taps):
    for offset, piece in zip(REL, (g0, g1, g2, g3)):
        x = mod4(pos[X] - offset)
        taps[pl.ds(2 * x, 2)] = piece[0:2].astype(f32)
        taps[8 + x] = piece[2].astype(f32)
    spatial[...] = taps[0:9]
    temporal[...] = taps[9:12]


def exchange(axis_send, values):
    return [axis_send(v, o) for v, o in zip(values, RING)]


def per_device(frames_in, cotangent, w_spatial, w_temporal):
    src = frames_in[0].reshape(2, 160, 512)
    c = cotangent[0].reshape(4, 160, 512)
    first = lax.axis_index("x") * 2 + lax.axis_index("zh") == 0
    pos = jnp.stack(
        [
            lax.axis_index("y"),
            lax.axis_index("zl"),
            lax.axis_index("core"),
            lax.axis_index("x"),
            first.astype(jnp.int32),
        ]
    ).astype(jnp.int32)
    send_x = lambda v, o: along(v, "x", o)
    send_y = lambda v, o: along(v, "y", o)

    near = w_spatial[FAR:]
    near = jnp.stack([near] + [along_z(near, o) for o in RING])
    far = jnp.concatenate([w_temporal, w_spatial[:FAR]], 0)
    far = jnp.stack([far] + [send_y(far, o) for o in RING])
    far, near = lax.optimization_barrier((far, near))
    near = [near] + [send_y(near, o) for o in RING]
    far = [far] + [along_z(far, o) for o in RING]
    last_frame, _ = lax.optimization_barrier((src[1], far[2]))
    before = lax.ppermute(last_frame, ("x", "zh"), [(i, i + 1) for i in range(7)])
    c_late, before, *_ = lax.optimization_barrier((c, before, *near[1:], *far[1:]))
    near += [to_sibling(piece) for piece in near]
    far += [to_sibling(piece) for piece in far]
    frames = jnp.concatenate([jnp.where(first, src[0], before)[None], src], 0)
    sib_frames = to_sibling(frames)

    terms, edge, wt = call(
        temporal_grad_kernel, 18, 4,
        [((8, 160, 512), bf16), ((160, 512), bf16), ((3, 512, 512), bf16)],
        [pltpu.VMEM((3, 4, 160, 512), f32), pltpu.SemaphoreType.DMA((32,))],
        pos, c_late, *far, any_from=2,
    )
    after = lax.ppermute(edge, ("x", "zh"), [(i, i - 1) for i in range(1, 8)])
    sib_terms = to_sibling(terms)
    sib_frames, after = lax.optimization_barrier((sib_frames, after))
    (one,) = call(
        spatial_weight_grad_kernel, 28, 5,
        [((9, 256, 512), f32)],
        [pltpu.VMEM((6, 160, 512), f32), pltpu.VMEM((256, 960), bf16), pltpu.VMEM((6, 192, 1536), bf16)],
        pos, frames, sib_frames, terms, sib_terms,
    )
    sp, ws = call(
        spatial_conv_kernel, 20, 6,
        [((3, 160, 512), bf16), ((9, 512, 512), bf16)],
        [pltpu.VMEM((3, 192, 1536), bf16), pltpu.VMEM((480, 512), f32), pltpu.SemaphoreType.DMA((64,))],
        pos, frames, *far, *near, any_from=2,
    )
    sib_sp = to_sibling(sp)
    part = [((3, 256, 256), f32)] + [((3, 256, 256), bf16)] * 3
    part += [((12, 64, 256), f32)] + [((12, 64, 256), bf16)] * 3
    grads = call(
        temporal_weight_grad_kernel, 28, 2, part,
        [pltpu.VMEM((256, 640), bf16), pltpu.VMEM((256, 640), bf16), pltpu.VMEM((4, 256, 512), f32)],
        pos, sp, sib_sp, terms, sib_terms, one,
    )
    rx, ry = exchange(send_x, grads[1:4]), exchange(send_y, grads[5:8])
    sp, _ = lax.optimization_barrier((sp, grads[0]))
    decoded, grad_input = call(
        outputs_kernel, 26, 6,
        [((4, 160, 512), bf16), ((2, 160, 512), bf16)],
        [pltpu.VMEM((2, 192, 1536), bf16), pltpu.VMEM((320, 512), f32), pltpu.VMEM((3, 3, 160, 512), f32)],
        pos, src, c, sp, terms, after, wt, ws,
    )
    *rx, decoded = lax.optimization_barrier((*rx, decoded))
    part = [((3, 64, 256), f32)] + [((3, 64, 256), bf16)] * 3
    two = call(second_exchange_kernel, 10, 1, part * 2, [], pos, grads[0], *rx, grads[4], *ry)
    rx, ry = exchange(send_y, two[1:4]), exchange(send_x, two[5:8])
    zs = call(
        third_exchange_kernel, 8, 1, [((3, 16, 512), f32)] + [((3, 16, 512), bf16)] * 3, [],
        pos, two[0], *rx, two[4], *ry,
    )
    total = zs[0] + sum(part.astype(f32) for part in exchange(along_z, zs[1:4]))
    total = total.astype(bf16)
    other = lax.ppermute(total, "zh", [(0, 1), (1, 0)])
    taps = (total.astype(f32) + other.astype(f32)) * (1.0 / math.sqrt(256 * 640))
    taps = taps.astype(bf16)
    grad_s, grad_t = call(
        final_taps_kernel, 4, 1,
        [((9, 16, 512), f32), ((3, 16, 512), f32)],
        [pltpu.VMEM((12, 16, 512), f32)],
        pos, taps, *[send_x(taps, o) for o in RING],
    )
    return (
        decoded.reshape(1, 4, 10, 16, 512),
        grad_input.reshape(1, 2, 10, 16, 512),
        grad_s,
        grad_t,
    )


def solution(mesh):
    physical = Mesh(mesh.devices.reshape(SIZES), AXES)
    dp, tm = ("y", "zl", "core"), ("x", "zh")
    values, weights = P(dp, tm, None, None, None), P(None, dp, None)
    return jax.shard_map(
        per_device,
        mesh=physical,
        in_specs=(values, values, weights, weights),
        out_specs=(values, values, weights, weights),
        check_vma=False,
    )
```

```python
import math

import jax
import jax.numpy as jnp
from jax import lax
from jax.experimental import pallas as pl
from jax.experimental.pallas import tpu as pltpu
from jax.sharding import Mesh, PartitionSpec as P

f32 = jnp.float32
bf16 = jnp.bfloat16
RATE = 1000000000

AXES = ("y", "zl", "core", "x", "zh")
SIZES = (4, 4, 2, 4, 2)
RING = (2, 1, 3)
REL = (0, 2, 1, 3)
Y, ZL, CORE, X, FIRST = range(5)


def ring_pairs(axes, offset):
    sizes = dict(zip(AXES, SIZES))
    pairs = []
    for flat in range(math.prod(SIZES)):
        at, rest = {}, flat
        for name in reversed(AXES):
            rest, at[name] = divmod(rest, sizes[name])
        to = dict(at)
        axis = axes[at["core"]]
        if axis == "z":
            steps = 7 if offset == 3 else offset
            z = (at["zh"] * 4 + at["zl"] + steps) % 8
            to["zh"], to["zl"] = divmod(z, 4)
        else:
            to[axis] = (at[axis] + offset) % 4
        target = 0
        for name in AXES:
            target = target * sizes[name] + to[name]
        pairs.append((flat, target))
    return pairs


def along(value, axes, offset):
    return lax.ppermute(value, AXES, ring_pairs(axes, offset))


def to_sibling(value):
    return lax.ppermute(value, "core", [(0, 1), (1, 0)])


def call(kernel, mib, micros, outs, scratch, *args, any_from=None):
    count = len(args)
    any_from = count if any_from is None else any_from
    specs = [pl.BlockSpec(memory_space=pltpu.SMEM)]
    specs += [
        pl.BlockSpec(memory_space=pltpu.VMEM if i < any_from else pl.ANY) for i in range(1, count)
    ]
    return pl.pallas_call(
        kernel,
        out_shape=[jax.ShapeDtypeStruct(s, d) for s, d in outs],
        in_specs=specs,
        out_specs=[pl.BlockSpec(memory_space=pltpu.VMEM) for _ in outs],
        scratch_shapes=scratch,
        compiler_params=pltpu.CompilerParams(vmem_limit_bytes=mib * 1024 * 1024),
        cost_estimate=pl.CostEstimate(flops=micros * RATE, bytes_accessed=0, transcendentals=0),
        name=kernel.__name__,
    )(*args)


def mod4(value):
    return lax.rem(value + 4, 4)


def dot(left, right):
    return jnp.dot(left, right, preferred_element_type=f32)


def dot_nt(left, right):
    return lax.dot_general(left, right, (((1,), (1,)), ((), ())), preferred_element_type=f32)


def placements(pos, pieces, weights, sems):
    copies = []
    for a, piece in enumerate(pieces):
        core = pos[CORE] if a < 4 else 1 - pos[CORE]
        even = core == 0
        taps = pl.ds(jnp.where(even, 6, 0), 6)
        for k in range(4):
            y = mod4(pos[Y] - jnp.where(even, REL[a % 4], REL[k]))
            zl = mod4(pos[ZL] - jnp.where(even, REL[k], REL[a % 4]))
            for d in range(2):
                block = (y * 4 + zl) * 2 + (core if d == 0 else 1 - core)
                rows = pl.ds(pl.multiple_of(block * 16, 16), 16)
                copies.append(
                    pltpu.make_async_copy(
                        piece.at[k, d], weights.at[taps, rows, :], sems.at[8 * a + 2 * k + d]
                    )
                )
    return copies


def column_shifts(value):
    rows = value.shape[0]
    column = lax.broadcasted_iota(jnp.int32, value.shape, 0) % 16
    before = jnp.where(column == 0, 0.0, pltpu.roll(value, 1, 0))
    after = jnp.where(column == 15, 0.0, pltpu.roll(value, rows - 1, 0))
    return before, value, after


def fill_shifts(buffer, slot, value, reverse):
    before, centre, after = column_shifts(value)
    width = value.shape[1]
    buffer[slot, :16] = jnp.zeros((16, 3 * width), bf16)
    buffer[slot, 176:] = jnp.zeros((16, 3 * width), bf16)
    for s, shifted in enumerate((after, centre, before) if reverse else (before, centre, after)):
        buffer[slot, 16:176, s * width : (s + 1) * width] = shifted.astype(bf16)


def strip_rows(start):
    return pl.ds(pl.multiple_of(start * 16, 16), 160)


def loop(count, step):
    lax.fori_loop(0, count, lambda k, _: (step(k), 0)[1], 0)


def temporal_grad_kernel(pos, c, *refs):
    pieces, (terms, edge, mine, theirs, weights, parts, sems) = refs[:8], refs[8:]
    copies = placements(pos, pieces, weights, sems)
    for copy in copies:
        copy.start()
    lower = pos[CORE] == 0

    def split(k, value):
        lo, hi = value[:, :256], value[:, 256:]
        mine[k] = jnp.where(lower, lo, hi)
        theirs[k] = jnp.where(lower, hi, lo)

    frames = [c[k] for k in range(4)]
    for k in range(3):
        split(3 + k, (frames[k].astype(f32) + frames[k + 1].astype(f32)).astype(bf16))
    split(6, frames[0])
    split(7, frames[3])
    for copy in copies:
        copy.wait()

    def step(k, _):
        parts[k] = dot_nt(c[...].reshape(640, 512), weights[k]).reshape(4, 160, 512)
        return 0

    lax.fori_loop(0, 3, step, 0)
    p, q, r = (parts.at[k] for k in range(3))
    values = (p[0] + p[1] + q[0], p[2] + p[3] + q[1] + q[2] + r[0] + r[1], q[3] + r[2] + r[3])
    for k, value in enumerate(values):
        value = value.astype(bf16)
        terms[k] = value
        split(k, value)
    edge[...] = values[0].astype(bf16)


def loop(count, step):
    lax.fori_loop(0, count, lambda k, _: (step(k), 0)[1], 0)


def columns_of(frames):
    return jnp.concatenate(frames, 0).T.astype(bf16)


def spatial_weight_grad_kernel(
    pos, frames, sib_frames, mine, theirs, g, act, act_t, shifted
):

    def silu(k):
        act[k] = jax.nn.silu(frames[k].astype(f32))
        act[3 + k] = jax.nn.silu(sib_frames[k].astype(f32))

    loop(3, silu)
    act_t[...] = columns_of([act[...].reshape(960, 512)])

    def shifts(k):
        fill_shifts(shifted, k, mine[k].astype(f32), True)
        fill_shifts(shifted, 3 + k, theirs[k].astype(f32), True)

    loop(3, shifts)

    def step(r, _):
        window = shifted[:, strip_rows(2 - r)].reshape(960, 768)
        value = dot(act_t[...], window)
        for s in range(3):
            g[3 * r + s] = value[:, 256 * s : 256 * s + 256]
        return 0

    lax.fori_loop(0, 3, step, 0)


def spatial_conv_kernel(pos, frames, weights, out, shifted, acc):
    loop(3, lambda k: fill_shifts(shifted, k, jax.nn.silu(frames[k].astype(f32)), False))
    acc[...] = jnp.zeros((480, 512), f32)

    def step(r, _):
        window = shifted[:, strip_rows(r)].reshape(480, 1536)
        acc[...] += dot(window, weights[pl.ds(3 + 3 * r, 3)].reshape(1536, 512))
        return 0

    lax.fori_loop(0, 3, step, 0)
    for k in range(3):
        out[k] = acc[160 * k : 160 * k + 160].astype(bf16)


def outputs_kernel(pos, src, c, sp, terms, after, weights, decoded, grad_input, shifted, acc, parts):

    def forward(k, _):
        parts[k] = dot(sp[...].reshape(480, 512), weights[k]).reshape(3, 160, 512)
        return 0

    lax.fori_loop(0, 3, forward, 0)

    def decode(g):
        u = src[g].astype(f32)
        both = parts[0, g] + parts[2, g + 1]
        decoded[2 * g] = (u + (both + parts[1, g])).astype(bf16)
        decoded[2 * g + 1] = (u + (both + parts[1, g + 1])).astype(bf16)

    loop(2, decode)
    edge = jnp.where(pos[FIRST] == 1, terms[0].astype(f32), 0.0)
    fill_shifts(shifted, 0, terms[1].astype(f32) + edge, True)
    fill_shifts(shifted, 1, terms[2].astype(f32) + after[...].astype(f32), True)
    acc[...] = jnp.zeros((320, 512), f32)

    def step(r, _):
        for s in range(3):
            window = shifted[:, strip_rows(2 - r), 512 * s : 512 * s + 512].reshape(320, 512)
            acc[...] += dot_nt(window, weights[3 + 3 * r + s])
        return 0

    lax.fori_loop(0, 3, step, 0)

    def finish(g):
        u = src[g].astype(f32)
        sigma = jax.nn.sigmoid(u)
        slope = sigma * (1.0 + u * (1.0 - sigma))
        cotangents = c[2 * g].astype(f32) + c[2 * g + 1].astype(f32)
        rows = pl.ds(pl.multiple_of(160 * g, 160), 160)
        grad_input[g] = (cotangents + acc[rows] * slope).astype(bf16)

    loop(2, finish)


def temporal_weight_grad_kernel(pos, sp, sps, mine, theirs, spatial, *refs):
    outs, (early, late, g) = refs[:4], refs[4:]
    early[...] = columns_of([ref[k].astype(f32) for ref in (sp, sps) for k in (0, 1)])
    late[...] = columns_of([ref[k].astype(f32) for ref in (sp, sps) for k in (1, 2)])
    outer = jnp.concatenate([mine[3], mine[5], theirs[3], theirs[5]], 0)
    inner = jnp.concatenate([mine[6], mine[4], theirs[6], theirs[4]], 0)
    zeros = jnp.zeros((160, 256), bf16)
    end = jnp.concatenate([zeros, mine[7], zeros, theirs[7]], 0)
    g[0] = spatial[8]
    g[1] = dot(early[...], outer)
    g[2] = dot(early[...], inner) + dot(late[...], end)
    g[3] = dot(late[...], outer)

    @pl.when(pos[CORE] == 0)
    def _():
        for offset, out in zip((0,) + RING, outs):
            x = mod4(pos[X] + offset)
            out[0:8] = spatial[pl.ds(2 * x, 2)].reshape(8, 128, 256).astype(out.dtype)
            out[8:12] = g[x].reshape(4, 128, 256).astype(out.dtype)

    @pl.when(pos[CORE] == 1)
    def _():
        for offset, out in zip((0,) + RING, outs):
            rows = pl.ds(pl.multiple_of(mod4(pos[Y] + offset) * 128, 128), 128)
            out[0:8] = spatial[0:8, rows].astype(out.dtype)
            out[8:12] = g[:, rows].astype(out.dtype)


def taps_of(x):
    return (2 * x, 2 * x + 1, 8 + x)


def second_exchange_kernel(pos, a, b1, b2, b3, *outs):
    for offset, out in zip((0,) + RING, outs):
        rows, taps = mod4(pos[Y] + offset), taps_of(mod4(pos[X] + offset))
        for t in range(3):
            block = jnp.where(pos[CORE] == 0, 4 * t + rows, taps[t])
            total = a[block] + b1[block].astype(f32) + b2[block].astype(f32)
            out[t] = (total + b3[block].astype(f32)).astype(out.dtype)


def core_rows_kernel(pos, a, b1, b2, b3, mine, theirs):
    total = a[...] + b1[...].astype(f32) + b2[...].astype(f32) + b3[...].astype(f32)
    total = total.reshape(3, 4, 2, 16, 256)
    lower = pos[CORE] == 0
    mine[...] = jnp.where(lower, total[:, :, 0], total[:, :, 1])
    theirs[...] = jnp.where(lower, total[:, :, 1], total[:, :, 0])


def third_exchange_kernel(pos, mine, theirs, *outs):
    lower = pos[CORE] == 0
    for offset, out in zip((0,) + RING, outs):
        zl = mod4(pos[ZL] + offset)
        for t in range(3):
            own, other = mine[t, zl], theirs[t, zl]
            out[t, :, :256] = jnp.where(lower, own, other).astype(out.dtype)
            out[t, :, 256:] = jnp.where(lower, other, own).astype(out.dtype)


def final_taps_kernel(pos, g0, g1, g2, g3, spatial, temporal, taps):
    for offset, piece in zip(REL, (g0, g1, g2, g3)):
        x = mod4(pos[X] - offset)
        taps[pl.ds(2 * x, 2)] = piece[0:2].astype(f32)
        taps[8 + x] = piece[2].astype(f32)
    spatial[...] = taps[0:9]
    temporal[...] = taps[9:12]


def exchange(axes, values):
    return [along(v, axes, o) for v, o in zip(values, RING)]


def per_device(frames_in, cotangent, w_spatial, w_temporal):
    src = frames_in[0].reshape(2, 160, 512)
    c = cotangent[0].reshape(4, 160, 512)
    first = lax.axis_index("x") * 2 + lax.axis_index("zh") == 0
    pos = jnp.stack(
        [
            lax.axis_index("y"),
            lax.axis_index("zl"),
            lax.axis_index("core"),
            lax.axis_index("x"),
            first.astype(jnp.int32),
        ]
    ).astype(jnp.int32)
    even = lax.axis_index("core") == 0
    low = jnp.concatenate([w_temporal, w_spatial[:3]], 0)
    high = w_spatial[3:]
    keep, give = jnp.where(even, high, low), jnp.where(even, low, high)
    before = lax.ppermute(src[1], ("x", "zh"), [(i, i + 1) for i in range(7)])
    pair = jnp.stack([keep, to_sibling(give)])
    ring = jnp.stack([pair] + [along(pair, ("z", "y"), o) for o in RING])
    pieces = [ring] + [along(ring, ("y", "z"), o) for o in RING]
    pieces[2], before = lax.optimization_barrier((pieces[2], before))
    pieces += [to_sibling(piece) for piece in pieces]
    frames = jnp.concatenate([jnp.where(first, src[0], before)[None], src], 0)
    sib_frames = to_sibling(frames)

    terms, edge, mine, theirs, weights = call(
        temporal_grad_kernel, 24, 5,
        [
            ((3, 160, 512), bf16), ((160, 512), bf16), ((8, 160, 256), bf16), ((8, 160, 256), bf16),
            ((12, 512, 512), bf16),
        ],
        [pltpu.VMEM((3, 4, 160, 512), f32), pltpu.SemaphoreType.DMA((64,))],
        pos, c, *pieces, any_from=2,
    )
    after = lax.ppermute(edge, ("x", "zh"), [(i, i - 1) for i in range(1, 8)])
    theirs = to_sibling(theirs)
    theirs, after = lax.optimization_barrier((theirs, after))
    (one,) = call(
        spatial_weight_grad_kernel, 28, 5,
        [((9, 512, 256), f32)],
        [pltpu.VMEM((6, 160, 512), f32), pltpu.VMEM((512, 960), bf16), pltpu.VMEM((6, 192, 768), bf16)],
        pos, frames, sib_frames, mine, theirs,
    )
    (sp,) = call(
        spatial_conv_kernel, 20, 6,
        [((3, 160, 512), bf16)],
        [pltpu.VMEM((3, 192, 1536), bf16), pltpu.VMEM((480, 512), f32)],
        pos, frames, weights,
    )
    sib_sp = to_sibling(sp)
    grads = call(
        temporal_weight_grad_kernel, 28, 2,
        [((12, 128, 256), f32)] + [((12, 128, 256), bf16)] * 3,
        [pltpu.VMEM((512, 640), bf16), pltpu.VMEM((512, 640), bf16), pltpu.VMEM((4, 512, 256), f32)],
        pos, sp, sib_sp, mine, theirs, one,
    )
    received = exchange(("x", "y"), grads[1:])
    sp, _ = lax.optimization_barrier((sp, grads[0]))
    decoded, grad_input = call(
        outputs_kernel, 26, 6,
        [((4, 160, 512), bf16), ((2, 160, 512), bf16)],
        [pltpu.VMEM((2, 192, 1536), bf16), pltpu.VMEM((320, 512), f32), pltpu.VMEM((3, 3, 160, 512), f32)],
        pos, src, c, sp, terms, after, weights,
    )
    *received, decoded = lax.optimization_barrier((*received, decoded))
    two = call(
        second_exchange_kernel, 12, 1, [((3, 128, 256), f32)] + [((3, 128, 256), bf16)] * 3, [],
        pos, grads[0], *received,
    )
    rows_mine, rows_theirs = call(
        core_rows_kernel, 8, 1, [((3, 4, 16, 256), f32)] * 2, [],
        pos, two[0], *exchange(("y", "x"), two[1:]),
    )
    zs = call(
        third_exchange_kernel, 8, 1, [((3, 16, 512), f32)] + [((3, 16, 512), bf16)] * 3, [],
        pos, rows_mine, to_sibling(rows_theirs),
    )
    total = zs[0] + sum(part.astype(f32) for part in exchange(("z", "z"), zs[1:]))
    total = total.astype(bf16)
    other = lax.ppermute(total, "zh", [(0, 1), (1, 0)])
    taps = (total.astype(f32) + other.astype(f32)) * (1.0 / math.sqrt(256 * 640))
    taps = taps.astype(bf16)
    grad_s, grad_t = call(
        final_taps_kernel, 4, 1,
        [((9, 16, 512), f32), ((3, 16, 512), f32)],
        [pltpu.VMEM((12, 16, 512), f32)],
        pos, taps, *[along(taps, ("x", "x"), o) for o in RING],
    )
    return (
        decoded.reshape(1, 4, 10, 16, 512),
        grad_input.reshape(1, 2, 10, 16, 512),
        grad_s,
        grad_t,
    )


def solution(mesh):
    physical = Mesh(mesh.devices.reshape(SIZES), AXES)
    dp, tm = ("y", "zl", "core"), ("x", "zh")
    values, weights = P(dp, tm, None, None, None), P(None, dp, None)
    return jax.shard_map(
        per_device,
        mesh=physical,
        in_specs=(values, values, weights, weights),
        out_specs=(values, values, weights, weights),
        check_vma=False,
    )
```

```python
import math

import jax
import jax.numpy as jnp
from jax import lax
from jax.experimental import pallas as pl
from jax.experimental.pallas import tpu as pltpu
from jax.sharding import Mesh, PartitionSpec as P

f32 = jnp.float32
bf16 = jnp.bfloat16
RATE = 1000000000

AXES = ("y", "zl", "core", "x", "zh")
SIZES = (4, 4, 2, 4, 2)
RING = (2, 1, 3)
REL = (0, 2, 1, 3)
Y, ZL, CORE, X, FIRST = range(5)


def ring_pairs(axes, offset):
    sizes = dict(zip(AXES, SIZES))
    pairs = []
    for flat in range(math.prod(SIZES)):
        at, rest = {}, flat
        for name in reversed(AXES):
            rest, at[name] = divmod(rest, sizes[name])
        to = dict(at)
        axis = axes[at["core"]]
        if axis == "z":
            steps = 7 if offset == 3 else offset
            z = (at["zh"] * 4 + at["zl"] + steps) % 8
            to["zh"], to["zl"] = divmod(z, 4)
        else:
            to[axis] = (at[axis] + offset) % 4
        target = 0
        for name in AXES:
            target = target * sizes[name] + to[name]
        pairs.append((flat, target))
    return pairs


def along(value, axes, offset):
    return lax.ppermute(value, AXES, ring_pairs(axes, offset))


def to_sibling(value):
    return lax.ppermute(value, "core", [(0, 1), (1, 0)])


def call(kernel, mib, micros, outs, scratch, *args, any_from=None, hbm=()):
    count = len(args)
    any_from = count if any_from is None else any_from
    specs = [pl.BlockSpec(memory_space=pltpu.SMEM)]
    specs += [
        pl.BlockSpec(
            memory_space=pltpu.HBM if i in hbm else pltpu.VMEM if i < any_from else pl.ANY
        )
        for i in range(1, count)
    ]
    return pl.pallas_call(
        kernel,
        out_shape=[jax.ShapeDtypeStruct(s, d) for s, d in outs],
        in_specs=specs,
        out_specs=[pl.BlockSpec(memory_space=pltpu.VMEM) for _ in outs],
        scratch_shapes=scratch,
        compiler_params=pltpu.CompilerParams(vmem_limit_bytes=mib * 1024 * 1024),
        cost_estimate=pl.CostEstimate(flops=micros * RATE, bytes_accessed=0, transcendentals=0),
        name=kernel.__name__,
    )(*args)


def mod4(value):
    return lax.rem(value + 4, 4)


def dot(left, right):
    return jnp.dot(left, right, preferred_element_type=f32)


def dot_nt(left, right):
    return lax.dot_general(left, right, (((1,), (1,)), ((), ())), preferred_element_type=f32)


def placements(pos, pieces, weights, sems):
    copies = []
    for a, piece in enumerate(pieces):
        core = pos[CORE] if a < 4 else 1 - pos[CORE]
        even = core == 0
        taps = pl.ds(jnp.where(even, 6, 0), 6)
        for k in range(4):
            y = mod4(pos[Y] - jnp.where(even, REL[a % 4], REL[k]))
            zl = mod4(pos[ZL] - jnp.where(even, REL[k], REL[a % 4]))
            for d in range(2):
                block = (y * 4 + zl) * 2 + (core if d == 0 else 1 - core)
                rows = pl.ds(pl.multiple_of(block * 16, 16), 16)
                copies.append(
                    pltpu.make_async_copy(
                        piece.at[k, d], weights.at[taps, rows, :], sems.at[8 * a + 2 * k + d]
                    )
                )
    return copies


def column_shifts(value):
    rows = value.shape[0]
    column = lax.broadcasted_iota(jnp.int32, value.shape, 0) % 16
    before = jnp.where(column == 0, 0.0, pltpu.roll(value, 1, 0))
    after = jnp.where(column == 15, 0.0, pltpu.roll(value, rows - 1, 0))
    return before, value, after


def fill_shifts(buffer, slot, value, reverse):
    before, centre, after = column_shifts(value)
    width = value.shape[1]
    buffer[slot, :16] = jnp.zeros((16, 3 * width), bf16)
    buffer[slot, 176:] = jnp.zeros((16, 3 * width), bf16)
    for s, shifted in enumerate((after, centre, before) if reverse else (before, centre, after)):
        buffer[slot, 16:176, s * width : (s + 1) * width] = shifted.astype(bf16)


def strip_rows(start):
    return pl.ds(pl.multiple_of(start * 16, 16), 160)


def loop(count, step):
    lax.fori_loop(0, count, lambda k, _: (step(k), 0)[1], 0)


def temporal_grad_kernel(pos, c, *refs):
    pieces, (terms, edge, mine, theirs, weights, local, parts, sems) = refs[:8], refs[8:]
    fetch = pltpu.make_async_copy(c, local, sems.at[64])
    fetch.start()
    copies = placements(pos, pieces, weights, sems)
    for copy in copies:
        copy.start()
    lower = pos[CORE] == 0

    def split(k, value):
        lo, hi = value[:, :256], value[:, 256:]
        mine[k] = jnp.where(lower, lo, hi)
        theirs[k] = jnp.where(lower, hi, lo)

    fetch.wait()
    frames = [local[k] for k in range(4)]
    for k in range(3):
        split(3 + k, (frames[k].astype(f32) + frames[k + 1].astype(f32)).astype(bf16))
    split(6, frames[0])
    split(7, frames[3])
    for copy in copies:
        copy.wait()

    def step(k, _):
        parts[k] = dot_nt(local[...].reshape(640, 512), weights[k]).reshape(4, 160, 512)
        return 0

    lax.fori_loop(0, 3, step, 0)
    p, q, r = (parts.at[k] for k in range(3))
    values = (p[0] + p[1] + q[0], p[2] + p[3] + q[1] + q[2] + r[0] + r[1], q[3] + r[2] + r[3])
    for k, value in enumerate(values):
        value = value.astype(bf16)
        terms[k] = value
        split(k, value)
    edge[...] = values[0].astype(bf16)


def loop(count, step):
    lax.fori_loop(0, count, lambda k, _: (step(k), 0)[1], 0)


def columns_of(frames):
    return jnp.concatenate(frames, 0).T.astype(bf16)


def spatial_weight_grad_kernel(
    pos, frames, sib_frames, mine, theirs, g, act, act_t, shifted
):

    def silu(k):
        act[k] = jax.nn.silu(frames[k].astype(f32))
        act[3 + k] = jax.nn.silu(sib_frames[k].astype(f32))

    loop(3, silu)
    act_t[...] = columns_of([act[...].reshape(960, 512)])

    def shifts(k):
        fill_shifts(shifted, k, mine[k].astype(f32), True)
        fill_shifts(shifted, 3 + k, theirs[k].astype(f32), True)

    loop(3, shifts)

    def step(r, _):
        window = shifted[:, strip_rows(2 - r)].reshape(960, 768)
        value = dot(act_t[...], window)
        for s in range(3):
            g[3 * r + s] = value[:, 256 * s : 256 * s + 256]
        return 0

    lax.fori_loop(0, 3, step, 0)


def spatial_conv_kernel(pos, frames, weights, out, shifted, acc):
    loop(3, lambda k: fill_shifts(shifted, k, jax.nn.silu(frames[k].astype(f32)), False))
    acc[...] = jnp.zeros((480, 512), f32)

    def step(r, _):
        window = shifted[:, strip_rows(r)].reshape(480, 1536)
        acc[...] += dot(window, weights[pl.ds(3 + 3 * r, 3)].reshape(1536, 512))
        return 0

    lax.fori_loop(0, 3, step, 0)
    for k in range(3):
        out[k] = acc[160 * k : 160 * k + 160].astype(bf16)


def decode_kernel(pos, src, sp, weights, decoded, parts):

    def forward(k, _):
        parts[k] = dot(sp[...].reshape(480, 512), weights[k]).reshape(3, 160, 512)
        return 0

    lax.fori_loop(0, 3, forward, 0)

    def decode(g):
        u = src[g].astype(f32)
        both = parts[0, g] + parts[2, g + 1]
        decoded[2 * g] = (u + (both + parts[1, g])).astype(bf16)
        decoded[2 * g + 1] = (u + (both + parts[1, g + 1])).astype(bf16)

    loop(2, decode)


def input_grad_kernel(pos, src, c, terms, after, weights, grad_input, shifted, acc):
    edge = jnp.where(pos[FIRST] == 1, terms[0].astype(f32), 0.0)
    fill_shifts(shifted, 0, terms[1].astype(f32) + edge, True)
    fill_shifts(shifted, 1, terms[2].astype(f32) + after[...].astype(f32), True)
    acc[...] = jnp.zeros((320, 512), f32)

    def step(r, _):
        for s in range(3):
            window = shifted[:, strip_rows(2 - r), 512 * s : 512 * s + 512].reshape(320, 512)
            acc[...] += dot_nt(window, weights[3 + 3 * r + s])
        return 0

    lax.fori_loop(0, 3, step, 0)

    def finish(g):
        u = src[g].astype(f32)
        sigma = jax.nn.sigmoid(u)
        slope = sigma * (1.0 + u * (1.0 - sigma))
        cotangents = c[2 * g].astype(f32) + c[2 * g + 1].astype(f32)
        rows = pl.ds(pl.multiple_of(160 * g, 160), 160)
        grad_input[g] = (cotangents + acc[rows] * slope).astype(bf16)

    loop(2, finish)


def temporal_weight_grad_kernel(pos, sp, sps, mine, theirs, spatial, *refs):
    outs, (early, late, g) = refs[:4], refs[4:]
    early[...] = columns_of([ref[k].astype(f32) for ref in (sp, sps) for k in (0, 1)])
    late[...] = columns_of([ref[k].astype(f32) for ref in (sp, sps) for k in (1, 2)])
    outer = jnp.concatenate([mine[3], mine[5], theirs[3], theirs[5]], 0)
    inner = jnp.concatenate([mine[6], mine[4], theirs[6], theirs[4]], 0)
    zeros = jnp.zeros((160, 256), bf16)
    end = jnp.concatenate([zeros, mine[7], zeros, theirs[7]], 0)
    g[0] = spatial[8]
    g[1] = dot(early[...], outer)
    g[2] = dot(early[...], inner) + dot(late[...], end)
    g[3] = dot(late[...], outer)

    @pl.when(pos[CORE] == 0)
    def _():
        for offset, out in zip((0,) + RING, outs):
            x = mod4(pos[X] + offset)
            out[0:8] = spatial[pl.ds(2 * x, 2)].reshape(8, 128, 256).astype(out.dtype)
            out[8:12] = g[x].reshape(4, 128, 256).astype(out.dtype)

    @pl.when(pos[CORE] == 1)
    def _():
        for offset, out in zip((0,) + RING, outs):
            rows = pl.ds(pl.multiple_of(mod4(pos[Y] + offset) * 128, 128), 128)
            out[0:8] = spatial[0:8, rows].astype(out.dtype)
            out[8:12] = g[:, rows].astype(out.dtype)


def taps_of(x):
    return (2 * x, 2 * x + 1, 8 + x)


def second_exchange_kernel(pos, a, b1, b2, b3, *outs):
    for offset, out in zip((0,) + RING, outs):
        rows, taps = mod4(pos[Y] + offset), taps_of(mod4(pos[X] + offset))
        for t in range(3):
            block = jnp.where(pos[CORE] == 0, 4 * t + rows, taps[t])
            total = a[block] + b1[block].astype(f32) + b2[block].astype(f32)
            out[t] = (total + b3[block].astype(f32)).astype(out.dtype)


def core_rows_kernel(pos, a, b1, b2, b3, mine, theirs):
    total = a[...] + b1[...].astype(f32) + b2[...].astype(f32) + b3[...].astype(f32)
    total = total.reshape(3, 4, 2, 16, 256)
    lower = pos[CORE] == 0
    mine[...] = jnp.where(lower, total[:, :, 0], total[:, :, 1])
    theirs[...] = jnp.where(lower, total[:, :, 1], total[:, :, 0])


def third_exchange_kernel(pos, mine, theirs, *outs):
    lower = pos[CORE] == 0
    for offset, out in zip((0,) + RING, outs):
        zl = mod4(pos[ZL] + offset)
        for t in range(3):
            own, other = mine[t, zl], theirs[t, zl]
            out[t, :, :256] = jnp.where(lower, own, other).astype(out.dtype)
            out[t, :, 256:] = jnp.where(lower, other, own).astype(out.dtype)


def final_taps_kernel(pos, g0, g1, g2, g3, spatial, temporal, taps):
    for offset, piece in zip(REL, (g0, g1, g2, g3)):
        x = mod4(pos[X] - offset)
        taps[pl.ds(2 * x, 2)] = piece[0:2].astype(f32)
        taps[8 + x] = piece[2].astype(f32)
    spatial[...] = taps[0:9]
    temporal[...] = taps[9:12]


def exchange(axes, values):
    return [along(v, axes, o) for v, o in zip(values, RING)]


def per_device(frames_in, cotangent, w_spatial, w_temporal):
    src = frames_in[0].reshape(2, 160, 512)
    c = cotangent[0].reshape(4, 160, 512)
    first = lax.axis_index("x") * 2 + lax.axis_index("zh") == 0
    pos = jnp.stack(
        [
            lax.axis_index("y"),
            lax.axis_index("zl"),
            lax.axis_index("core"),
            lax.axis_index("x"),
            first.astype(jnp.int32),
        ]
    ).astype(jnp.int32)
    even = lax.axis_index("core") == 0
    low = jnp.concatenate([w_temporal, w_spatial[:3]], 0)
    high = w_spatial[3:]
    keep, give = jnp.where(even, high, low), jnp.where(even, low, high)
    before = lax.ppermute(src[1], ("x", "zh"), [(i, i + 1) for i in range(7)])
    pair = jnp.stack([keep, to_sibling(give)])
    ring = jnp.stack([pair] + [along(pair, ("z", "y"), o) for o in RING])
    ring, before = lax.optimization_barrier((ring, before))
    pieces = [ring] + [along(ring, ("y", "z"), o) for o in RING]
    pieces += [to_sibling(piece) for piece in pieces]
    frames = jnp.concatenate([jnp.where(first, src[0], before)[None], src], 0)
    sib_frames = to_sibling(frames)

    terms, edge, mine, theirs, weights = call(
        temporal_grad_kernel, 24, 5,
        [
            ((3, 160, 512), bf16), ((160, 512), bf16), ((8, 160, 256), bf16), ((8, 160, 256), bf16),
            ((12, 512, 512), bf16),
        ],
        [
            pltpu.VMEM((4, 160, 512), bf16), pltpu.VMEM((3, 4, 160, 512), f32),
            pltpu.SemaphoreType.DMA((65,)),
        ],
        pos, c, *pieces, any_from=2, hbm=(1,),
    )
    theirs = to_sibling(theirs)
    (one,) = call(
        spatial_weight_grad_kernel, 28, 5,
        [((9, 512, 256), f32)],
        [pltpu.VMEM((6, 160, 512), f32), pltpu.VMEM((512, 960), bf16), pltpu.VMEM((6, 192, 768), bf16)],
        pos, frames, sib_frames, mine, theirs,
    )
    (sp,) = call(
        spatial_conv_kernel, 20, 6,
        [((3, 160, 512), bf16)],
        [pltpu.VMEM((3, 192, 1536), bf16), pltpu.VMEM((480, 512), f32)],
        pos, frames, weights,
    )
    sib_sp = to_sibling(sp)
    grads = call(
        temporal_weight_grad_kernel, 28, 2,
        [((12, 128, 256), f32)] + [((12, 128, 256), bf16)] * 3,
        [pltpu.VMEM((512, 640), bf16), pltpu.VMEM((512, 640), bf16), pltpu.VMEM((4, 512, 256), f32)],
        pos, sp, sib_sp, mine, theirs, one,
    )
    received = exchange(("x", "y"), grads[1:])
    sp, edge, _ = lax.optimization_barrier((sp, edge, grads[0]))
    after = lax.ppermute(edge, ("x", "zh"), [(i, i - 1) for i in range(1, 8)])
    (decoded,) = call(
        decode_kernel, 20, 2, [((4, 160, 512), bf16)], [pltpu.VMEM((3, 3, 160, 512), f32)],
        pos, src, sp, weights,
    )
    (grad_input,) = call(
        input_grad_kernel, 20, 4, [((2, 160, 512), bf16)],
        [pltpu.VMEM((2, 192, 1536), bf16), pltpu.VMEM((320, 512), f32)],
        pos, src, c, terms, after, weights,
    )
    *received, decoded, grad_input = lax.optimization_barrier((*received, decoded, grad_input))
    two = call(
        second_exchange_kernel, 12, 1, [((3, 128, 256), f32)] + [((3, 128, 256), bf16)] * 3, [],
        pos, grads[0], *received,
    )
    rows_mine, rows_theirs = call(
        core_rows_kernel, 8, 1, [((3, 4, 16, 256), f32)] * 2, [],
        pos, two[0], *exchange(("y", "x"), two[1:]),
    )
    zs = call(
        third_exchange_kernel, 8, 1, [((3, 16, 512), f32)] + [((3, 16, 512), bf16)] * 3, [],
        pos, rows_mine, to_sibling(rows_theirs),
    )
    total = zs[0] + sum(part.astype(f32) for part in exchange(("z", "z"), zs[1:]))
    total = total.astype(bf16)
    other = lax.ppermute(total, "zh", [(0, 1), (1, 0)])
    taps = (total.astype(f32) + other.astype(f32)) * (1.0 / math.sqrt(256 * 640))
    taps = taps.astype(bf16)
    grad_s, grad_t = call(
        final_taps_kernel, 4, 1,
        [((9, 16, 512), f32), ((3, 16, 512), f32)],
        [pltpu.VMEM((12, 16, 512), f32)],
        pos, taps, *[along(taps, ("x", "x"), o) for o in RING],
    )
    return (
        decoded.reshape(1, 4, 10, 16, 512),
        grad_input.reshape(1, 2, 10, 16, 512),
        grad_s,
        grad_t,
    )


def solution(mesh):
    physical = Mesh(mesh.devices.reshape(SIZES), AXES)
    dp, tm = ("y", "zl", "core"), ("x", "zh")
    values, weights = P(dp, tm, None, None, None), P(None, dp, None)
    return jax.shard_map(
        per_device,
        mesh=physical,
        in_specs=(values, values, weights, weights),
        out_specs=(values, values, weights, weights),
        check_vma=False,
    )
```

```python
import math

import jax
import jax.numpy as jnp
from jax import lax
from jax.experimental import pallas as pl
from jax.experimental.pallas import tpu as pltpu
from jax.sharding import Mesh, PartitionSpec as P

f32 = jnp.float32
bf16 = jnp.bfloat16
RATE = 1000000000

AXES = ("y", "zl", "core", "x", "zh")
SIZES = (4, 4, 2, 4, 2)
RING = (2, 1, 3)
OUTER = (0, 3, 1, 2)
REL = (0, 2, 1, 3)
Y, ZL, CORE, X, FIRST = range(5)


def ring_pairs(axes, offset):
    sizes = dict(zip(AXES, SIZES))
    pairs = []
    for flat in range(math.prod(SIZES)):
        at, rest = {}, flat
        for name in reversed(AXES):
            rest, at[name] = divmod(rest, sizes[name])
        to = dict(at)
        axis = axes[at["core"]]
        if axis == "z":
            z = at["zh"] * 4 + at["zl"]
            steps = {1: 1, 3: -1, 2: 2 - 4 * (z % 2)}[offset]
            z = (z + steps) % 8
            to["zh"], to["zl"] = divmod(z, 4)
        else:
            to[axis] = (at[axis] + offset) % 4
        target = 0
        for name in AXES:
            target = target * sizes[name] + to[name]
        pairs.append((flat, target))
    return pairs


def along(value, axes, offset):
    return lax.ppermute(value, AXES, ring_pairs(axes, offset))


def to_sibling(value):
    return lax.ppermute(value, "core", [(0, 1), (1, 0)])


def call(kernel, mib, micros, outs, scratch, *args, any_from=None):
    count = len(args)
    any_from = count if any_from is None else any_from
    specs = [pl.BlockSpec(memory_space=pltpu.SMEM)]
    specs += [
        pl.BlockSpec(memory_space=pltpu.VMEM if i < any_from else pl.ANY) for i in range(1, count)
    ]
    return pl.pallas_call(
        kernel,
        out_shape=[jax.ShapeDtypeStruct(s, d) for s, d in outs],
        in_specs=specs,
        out_specs=[pl.BlockSpec(memory_space=pltpu.VMEM) for _ in outs],
        scratch_shapes=scratch,
        compiler_params=pltpu.CompilerParams(vmem_limit_bytes=mib * 1024 * 1024),
        cost_estimate=pl.CostEstimate(flops=micros * RATE, bytes_accessed=0, transcendentals=0),
        name=kernel.__name__,
    )(*args)


def mod4(value):
    return lax.rem(value + 4, 4)


def dot(left, right):
    return jnp.dot(left, right, preferred_element_type=f32)


def dot_nt(left, right):
    return lax.dot_general(left, right, (((1,), (1,)), ((), ())), preferred_element_type=f32)


def placements(pos, pieces, weights, sems):
    copies = []
    for a, piece in enumerate(pieces):
        core = pos[CORE] if a < 4 else 1 - pos[CORE]
        even = core == 0
        taps = pl.ds(jnp.where(even, 6, 0), 6)
        for k in range(4):
            y = mod4(pos[Y] - jnp.where(even, OUTER[a % 4], REL[k]))
            zl = mod4(pos[ZL] - jnp.where(even, REL[k], OUTER[a % 4]))
            for d in range(2):
                block = (y * 4 + zl) * 2 + (core if d == 0 else 1 - core)
                rows = pl.ds(pl.multiple_of(block * 16, 16), 16)
                copies.append(
                    pltpu.make_async_copy(
                        piece.at[k, d], weights.at[taps, rows, :], sems.at[8 * a + 2 * k + d]
                    )
                )
    return copies


def column_shifts(value):
    rows = value.shape[0]
    column = lax.broadcasted_iota(jnp.int32, value.shape, 0) % 16
    before = jnp.where(column == 0, 0.0, pltpu.roll(value, 1, 0))
    after = jnp.where(column == 15, 0.0, pltpu.roll(value, rows - 1, 0))
    return before, value, after


def fill_shifts(buffer, slot, value, reverse):
    before, centre, after = column_shifts(value)
    width = value.shape[1]
    buffer[slot, :16] = jnp.zeros((16, 3 * width), bf16)
    buffer[slot, 176:] = jnp.zeros((16, 3 * width), bf16)
    for s, shifted in enumerate((after, centre, before) if reverse else (before, centre, after)):
        buffer[slot, 16:176, s * width : (s + 1) * width] = shifted.astype(bf16)


def strip_rows(start):
    return pl.ds(pl.multiple_of(start * 16, 16), 160)


def split(pos, value, mine, theirs):
    lo, hi = value[:, :256], value[:, 256:]
    lower = pos[CORE] == 0
    mine[...] = jnp.where(lower, lo, hi)
    theirs[...] = jnp.where(lower, hi, lo)


def loop(count, step):
    lax.fori_loop(0, count, lambda k, _: (step(k), 0)[1], 0)


def temporal_grad_kernel(pos, c, *refs):
    pieces, (terms, edge, mine, theirs, weights, parts, sems) = refs[:8], refs[8:]
    copies = placements(pos, pieces, weights, sems)
    for copy in copies:
        copy.start()
    for copy in copies:
        copy.wait()

    def step(k, _):
        parts[k] = dot_nt(c[...].reshape(640, 512), weights[k]).reshape(4, 160, 512)
        return 0

    lax.fori_loop(0, 3, step, 0)
    p, q, r = (parts.at[k] for k in range(3))
    values = (p[0] + p[1] + q[0], p[2] + p[3] + q[1] + q[2] + r[0] + r[1], q[3] + r[2] + r[3])
    for k, value in enumerate(values):
        value = value.astype(bf16)
        terms[k] = value
        split(pos, value, mine.at[k], theirs.at[k])
    edge[...] = values[0].astype(bf16)


def columns_of(frames):
    return jnp.concatenate(frames, 0).T.astype(bf16)


def prepare_kernel(pos, frames, sib_frames, c, act_t, shifted, mine, theirs, act):
    def silu(k):
        act[k] = jax.nn.silu(frames[k].astype(f32))
        act[3 + k] = jax.nn.silu(sib_frames[k].astype(f32))

    loop(3, silu)
    act_t[...] = columns_of([act[...].reshape(960, 512)])
    loop(3, lambda k: fill_shifts(shifted, k, act[k], False))
    for k in range(3):
        value = (c[k].astype(f32) + c[k + 1].astype(f32)).astype(bf16)
        split(pos, value, mine.at[k], theirs.at[k])
    split(pos, c[0], mine.at[3], theirs.at[3])
    split(pos, c[3], mine.at[4], theirs.at[4])


def spatial_weight_grad_kernel(pos, act_t, mine, theirs, g, shifted):
    def shifts(k):
        fill_shifts(shifted, k, mine[k].astype(f32), True)
        fill_shifts(shifted, 3 + k, theirs[k].astype(f32), True)

    loop(3, shifts)

    def step(r, _):
        window = shifted[:, strip_rows(2 - r)].reshape(960, 768)
        value = dot(act_t[...], window)
        for s in range(3):
            g[3 * r + s] = value[:, 256 * s : 256 * s + 256]
        return 0

    lax.fori_loop(0, 3, step, 0)


def spatial_conv_kernel(pos, shifted, weights, out, acc):
    acc[...] = jnp.zeros((480, 512), f32)

    def step(r, _):
        window = shifted[:, strip_rows(r)].reshape(480, 1536)
        acc[...] += dot(window, weights[pl.ds(3 + 3 * r, 3)].reshape(1536, 512))
        return 0

    lax.fori_loop(0, 3, step, 0)
    for k in range(3):
        out[k] = acc[160 * k : 160 * k + 160].astype(bf16)


def decode_kernel(pos, src, sp, weights, decoded, parts):

    def forward(k, _):
        parts[k] = dot(sp[...].reshape(480, 512), weights[k]).reshape(3, 160, 512)
        return 0

    lax.fori_loop(0, 3, forward, 0)

    def decode(g):
        u = src[g].astype(f32)
        both = parts[0, g] + parts[2, g + 1]
        decoded[2 * g] = (u + (both + parts[1, g])).astype(bf16)
        decoded[2 * g + 1] = (u + (both + parts[1, g + 1])).astype(bf16)

    loop(2, decode)


def input_grad_kernel(pos, src, c, terms, after, weights, grad_input, shifted, acc):
    edge = jnp.where(pos[FIRST] == 1, terms[0].astype(f32), 0.0)
    fill_shifts(shifted, 0, terms[1].astype(f32) + edge, True)
    fill_shifts(shifted, 1, terms[2].astype(f32) + after[...].astype(f32), True)
    acc[...] = jnp.zeros((320, 512), f32)

    def step(r, _):
        for s in range(3):
            window = shifted[:, strip_rows(2 - r), 512 * s : 512 * s + 512].reshape(320, 512)
            acc[...] += dot_nt(window, weights[3 + 3 * r + s])
        return 0

    lax.fori_loop(0, 3, step, 0)

    def finish(g):
        u = src[g].astype(f32)
        sigma = jax.nn.sigmoid(u)
        slope = sigma * (1.0 + u * (1.0 - sigma))
        cotangents = c[2 * g].astype(f32) + c[2 * g + 1].astype(f32)
        rows = pl.ds(pl.multiple_of(160 * g, 160), 160)
        grad_input[g] = (cotangents + acc[rows] * slope).astype(bf16)

    loop(2, finish)


def temporal_weight_grad_kernel(pos, sp, sps, mine, theirs, spatial, *refs):
    outs, (early, late, g) = refs[:4], refs[4:]
    early[...] = columns_of([ref[k].astype(f32) for ref in (sp, sps) for k in (0, 1)])
    late[...] = columns_of([ref[k].astype(f32) for ref in (sp, sps) for k in (1, 2)])
    outer = jnp.concatenate([mine[0], mine[2], theirs[0], theirs[2]], 0)
    inner = jnp.concatenate([mine[3], mine[1], theirs[3], theirs[1]], 0)
    zeros = jnp.zeros((160, 256), bf16)
    end = jnp.concatenate([zeros, mine[4], zeros, theirs[4]], 0)
    g[0] = spatial[8]
    g[1] = dot(early[...], outer)
    g[2] = dot(early[...], inner) + dot(late[...], end)
    g[3] = dot(late[...], outer)

    @pl.when(pos[CORE] == 0)
    def _():
        for offset, out in zip((0,) + RING, outs):
            x = mod4(pos[X] + offset)
            out[0:8] = spatial[pl.ds(2 * x, 2)].reshape(8, 128, 256).astype(out.dtype)
            out[8:12] = g[x].reshape(4, 128, 256).astype(out.dtype)

    @pl.when(pos[CORE] == 1)
    def _():
        for offset, out in zip((0,) + RING, outs):
            rows = pl.ds(pl.multiple_of(mod4(pos[Y] + offset) * 128, 128), 128)
            out[0:8] = spatial[0:8, rows].astype(out.dtype)
            out[8:12] = g[:, rows].astype(out.dtype)


def taps_of(x):
    return (2 * x, 2 * x + 1, 8 + x)


def second_exchange_kernel(pos, a, b1, b2, b3, *outs):
    for offset, out in zip((0,) + RING, outs):
        rows, taps = mod4(pos[Y] + offset), taps_of(mod4(pos[X] + offset))
        for t in range(3):
            block = jnp.where(pos[CORE] == 0, 4 * t + rows, taps[t])
            total = a[block] + b1[block].astype(f32) + b2[block].astype(f32)
            out[t] = (total + b3[block].astype(f32)).astype(out.dtype)


def core_rows_kernel(pos, a, b1, b2, b3, mine, theirs):
    total = a[...] + b1[...].astype(f32) + b2[...].astype(f32) + b3[...].astype(f32)
    total = total.reshape(3, 4, 2, 16, 256)
    lower = pos[CORE] == 0
    mine[...] = jnp.where(lower, total[:, :, 0], total[:, :, 1])
    theirs[...] = jnp.where(lower, total[:, :, 1], total[:, :, 0])


def third_exchange_kernel(pos, mine, theirs, *outs):
    lower = pos[CORE] == 0
    for offset, out in zip((0,) + RING, outs):
        zl = mod4(pos[ZL] + offset)
        for t in range(3):
            own, other = mine[t, zl], theirs[t, zl]
            out[t, :, :256] = jnp.where(lower, own, other).astype(out.dtype)
            out[t, :, 256:] = jnp.where(lower, other, own).astype(out.dtype)


def final_taps_kernel(pos, g0, g1, g2, g3, spatial, temporal, taps):
    for offset, piece in zip(REL, (g0, g1, g2, g3)):
        x = mod4(pos[X] - offset)
        taps[pl.ds(2 * x, 2)] = piece[0:2].astype(f32)
        taps[8 + x] = piece[2].astype(f32)
    spatial[...] = taps[0:9]
    temporal[...] = taps[9:12]


def exchange(axes, values):
    return [along(v, axes, o) for v, o in zip(values, RING)]


def per_device(frames_in, cotangent, w_spatial, w_temporal):
    src = frames_in[0].reshape(2, 160, 512)
    c = cotangent[0].reshape(4, 160, 512)
    first = lax.axis_index("x") * 2 + lax.axis_index("zh") == 0
    pos = jnp.stack(
        [
            lax.axis_index("y"),
            lax.axis_index("zl"),
            lax.axis_index("core"),
            lax.axis_index("x"),
            first.astype(jnp.int32),
        ]
    ).astype(jnp.int32)
    even = lax.axis_index("core") == 0
    low = jnp.concatenate([w_temporal, w_spatial[:3]], 0)
    high = w_spatial[3:]
    keep, give = jnp.where(even, high, low), jnp.where(even, low, high)
    before = lax.ppermute(src[1], ("x", "zh"), [(i, i + 1) for i in range(7)])
    pair = jnp.stack([keep, to_sibling(give)])
    ring = jnp.stack([pair] + exchange(("z", "y"), [pair] * 3))
    ring, before = lax.optimization_barrier((ring, before))
    pieces = [ring] + [along(ring, ("y", "z"), o) for o in OUTER[1:]]
    frames = jnp.concatenate([jnp.where(first, src[0], before)[None], src], 0)
    sib_frames = to_sibling(frames)
    act_t, shifted, pairs_mine, pairs_theirs = call(
        prepare_kernel, 16, 3,
        [((512, 960), bf16), ((3, 192, 1536), bf16), ((5, 160, 256), bf16), ((5, 160, 256), bf16)],
        [pltpu.VMEM((6, 160, 512), f32)],
        pos, frames, sib_frames, c,
    )
    pairs_theirs = to_sibling(pairs_theirs)
    pieces[0], act_t = lax.optimization_barrier((pieces[0], act_t))
    pieces += [to_sibling(piece) for piece in pieces]

    terms, edge, mine, theirs, weights = call(
        temporal_grad_kernel, 24, 5,
        [
            ((3, 160, 512), bf16), ((160, 512), bf16), ((3, 160, 256), bf16), ((3, 160, 256), bf16),
            ((12, 512, 512), bf16),
        ],
        [pltpu.VMEM((3, 4, 160, 512), f32), pltpu.SemaphoreType.DMA((64,))],
        pos, c, *pieces, any_from=2,
    )
    theirs = to_sibling(theirs)
    (one,) = call(
        spatial_weight_grad_kernel, 20, 4,
        [((9, 512, 256), f32)], [pltpu.VMEM((6, 192, 768), bf16)],
        pos, act_t, mine, theirs,
    )
    (sp,) = call(
        spatial_conv_kernel, 16, 4, [((3, 160, 512), bf16)], [pltpu.VMEM((480, 512), f32)],
        pos, shifted, weights,
    )
    sib_sp = to_sibling(sp)
    grads = call(
        temporal_weight_grad_kernel, 28, 2,
        [((12, 128, 256), f32)] + [((12, 128, 256), bf16)] * 3,
        [pltpu.VMEM((512, 640), bf16), pltpu.VMEM((512, 640), bf16), pltpu.VMEM((4, 512, 256), f32)],
        pos, sp, sib_sp, pairs_mine, pairs_theirs, one,
    )
    received = exchange(("x", "y"), grads[1:])
    sp, edge, _ = lax.optimization_barrier((sp, edge, grads[0]))
    after = lax.ppermute(edge, ("x", "zh"), [(i, i - 1) for i in range(1, 8)])
    (decoded,) = call(
        decode_kernel, 20, 2, [((4, 160, 512), bf16)], [pltpu.VMEM((3, 3, 160, 512), f32)],
        pos, src, sp, weights,
    )
    (grad_input,) = call(
        input_grad_kernel, 20, 4, [((2, 160, 512), bf16)],
        [pltpu.VMEM((2, 192, 1536), bf16), pltpu.VMEM((320, 512), f32)],
        pos, src, c, terms, after, weights,
    )
    *received, decoded, grad_input = lax.optimization_barrier((*received, decoded, grad_input))
    two = call(
        second_exchange_kernel, 12, 1, [((3, 128, 256), f32)] + [((3, 128, 256), bf16)] * 3, [],
        pos, grads[0], *received,
    )
    rows_mine, rows_theirs = call(
        core_rows_kernel, 8, 1, [((3, 4, 16, 256), f32)] * 2, [],
        pos, two[0], *exchange(("y", "x"), two[1:]),
    )
    zs = call(
        third_exchange_kernel, 8, 1, [((3, 16, 512), f32)] + [((3, 16, 512), bf16)] * 3, [],
        pos, rows_mine, to_sibling(rows_theirs),
    )
    total = zs[0] + sum(part.astype(f32) for part in exchange(("z", "z"), zs[1:]))
    total = total.astype(bf16)
    other = lax.ppermute(total, "zh", [(0, 1), (1, 0)])
    taps = (total.astype(f32) + other.astype(f32)) * (1.0 / math.sqrt(256 * 640))
    taps = taps.astype(bf16)
    grad_s, grad_t = call(
        final_taps_kernel, 4, 1,
        [((9, 16, 512), f32), ((3, 16, 512), f32)],
        [pltpu.VMEM((12, 16, 512), f32)],
        pos, taps, *[along(taps, ("x", "x"), o) for o in RING],
    )
    return (
        decoded.reshape(1, 4, 10, 16, 512),
        grad_input.reshape(1, 2, 10, 16, 512),
        grad_s,
        grad_t,
    )


def solution(mesh):
    physical = Mesh(mesh.devices.reshape(SIZES), AXES)
    dp, tm = ("y", "zl", "core"), ("x", "zh")
    values, weights = P(dp, tm, None, None, None), P(None, dp, None)
    return jax.shard_map(
        per_device,
        mesh=physical,
        in_specs=(values, values, weights, weights),
        out_specs=(values, values, weights, weights),
        check_vma=False,
    )
```

```python
import math

import jax
import jax.numpy as jnp
from jax import lax
from jax.experimental import pallas as pl
from jax.experimental.pallas import tpu as pltpu
from jax.sharding import Mesh, PartitionSpec as P

f32 = jnp.float32
bf16 = jnp.bfloat16
RATE = 1000000000

AXES = ("y", "zl", "core", "x", "zh")
SIZES = (4, 4, 2, 4, 2)
RING = (2, 1, 3)
OUTER = (0, 3, 1, 2)
REL = (0, 2, 1, 3)
Y, ZL, CORE, X, FIRST = range(5)


def ring_pairs(axes, offset):
    sizes = dict(zip(AXES, SIZES))
    pairs = []
    for flat in range(math.prod(SIZES)):
        at, rest = {}, flat
        for name in reversed(AXES):
            rest, at[name] = divmod(rest, sizes[name])
        to = dict(at)
        axis = axes[at["core"]]
        if axis == "z":
            z = at["zh"] * 4 + at["zl"]
            steps = {1: 1, 3: -1, 2: 2 - 4 * (z % 2)}[offset]
            z = (z + steps) % 8
            to["zh"], to["zl"] = divmod(z, 4)
        else:
            to[axis] = (at[axis] + offset) % 4
        target = 0
        for name in AXES:
            target = target * sizes[name] + to[name]
        pairs.append((flat, target))
    return pairs


def along(value, axes, offset):
    return lax.ppermute(value, AXES, ring_pairs(axes, offset))


def to_sibling(value):
    return lax.ppermute(value, "core", [(0, 1), (1, 0)])


def call(kernel, mib, micros, outs, scratch, *args, any_from=None):
    count = len(args)
    any_from = count if any_from is None else any_from
    specs = [pl.BlockSpec(memory_space=pltpu.SMEM)]
    specs += [
        pl.BlockSpec(memory_space=pltpu.VMEM if i < any_from else pl.ANY) for i in range(1, count)
    ]
    return pl.pallas_call(
        kernel,
        out_shape=[jax.ShapeDtypeStruct(s, d) for s, d in outs],
        in_specs=specs,
        out_specs=[pl.BlockSpec(memory_space=pltpu.VMEM) for _ in outs],
        scratch_shapes=scratch,
        compiler_params=pltpu.CompilerParams(vmem_limit_bytes=mib * 1024 * 1024),
        cost_estimate=pl.CostEstimate(flops=micros * RATE, bytes_accessed=0, transcendentals=0),
        name=kernel.__name__,
    )(*args)


def mod4(value):
    return lax.rem(value + 4, 4)


def dot(left, right):
    return jnp.dot(left, right, preferred_element_type=f32)


def dot_nt(left, right):
    return lax.dot_general(left, right, (((1,), (1,)), ((), ())), preferred_element_type=f32)


def placements(pos, pieces, weights, sems):
    copies = []
    for a, piece in enumerate(pieces):
        core = pos[CORE] if a < 4 else 1 - pos[CORE]
        even = core == 0
        taps = pl.ds(jnp.where(even, 6, 0), 6)
        for k in range(4):
            y = mod4(pos[Y] - jnp.where(even, OUTER[a % 4], REL[k]))
            zl = mod4(pos[ZL] - jnp.where(even, REL[k], OUTER[a % 4]))
            for d in range(2):
                block = (y * 4 + zl) * 2 + (core if d == 0 else 1 - core)
                rows = pl.ds(pl.multiple_of(block * 16, 16), 16)
                copies.append(
                    pltpu.make_async_copy(
                        piece.at[k, d], weights.at[taps, rows, :], sems.at[8 * a + 2 * k + d]
                    )
                )
    return copies


def column_shifts(value):
    rows = value.shape[0]
    column = lax.broadcasted_iota(jnp.int32, value.shape, 0) % 16
    before = jnp.where(column == 0, 0.0, pltpu.roll(value, 1, 0))
    after = jnp.where(column == 15, 0.0, pltpu.roll(value, rows - 1, 0))
    return before, value, after


def fill_shifts(buffer, slot, value, reverse):
    before, centre, after = column_shifts(value)
    width = value.shape[1]
    buffer[slot, :16] = jnp.zeros((16, 3 * width), bf16)
    buffer[slot, 176:] = jnp.zeros((16, 3 * width), bf16)
    for s, shifted in enumerate((after, centre, before) if reverse else (before, centre, after)):
        buffer[slot, 16:176, s * width : (s + 1) * width] = shifted.astype(bf16)


def strip_rows(start):
    return pl.ds(pl.multiple_of(start * 16, 16), 160)


def split(pos, value, mine, theirs):
    lo, hi = value[:, :256], value[:, 256:]
    lower = pos[CORE] == 0
    mine[...] = jnp.where(lower, lo, hi)
    theirs[...] = jnp.where(lower, hi, lo)


def loop(count, step):
    lax.fori_loop(0, count, lambda k, _: (step(k), 0)[1], 0)


def temporal_grad_kernel(pos, c, *refs):
    pieces, (terms, edge, mine, theirs, weights, parts, sems) = refs[:8], refs[8:]
    copies = placements(pos, pieces, weights, sems)
    for copy in copies:
        copy.start()
    for copy in copies:
        copy.wait()

    def step(k, _):
        parts[k] = dot_nt(c[...].reshape(640, 512), weights[k]).reshape(4, 160, 512)
        return 0

    lax.fori_loop(0, 3, step, 0)
    p, q, r = (parts.at[k] for k in range(3))
    values = (p[0] + p[1] + q[0], p[2] + p[3] + q[1] + q[2] + r[0] + r[1], q[3] + r[2] + r[3])
    for k, value in enumerate(values):
        value = value.astype(bf16)
        terms[k] = value
        split(pos, value, mine.at[k], theirs.at[k])
    edge[...] = values[0].astype(bf16)


def columns_of(frames):
    return jnp.concatenate(frames, 0).T.astype(bf16)


def prepare_kernel(pos, frames, sib_frames, c, act_t, shifted, mine, theirs, act):
    def silu(k):
        act[k] = jax.nn.silu(frames[k].astype(f32))
        act[3 + k] = jax.nn.silu(sib_frames[k].astype(f32))

    loop(3, silu)
    act_t[...] = columns_of([act[...].reshape(960, 512)])
    loop(3, lambda k: fill_shifts(shifted, k, act[k], False))
    for k in range(3):
        value = (c[k].astype(f32) + c[k + 1].astype(f32)).astype(bf16)
        split(pos, value, mine.at[k], theirs.at[k])
    split(pos, c[0], mine.at[3], theirs.at[3])
    split(pos, c[3], mine.at[4], theirs.at[4])


def spatial_weight_grad_kernel(pos, act_t, mine, theirs, g, shifted):
    def shifts(k):
        fill_shifts(shifted, k, mine[k].astype(f32), True)
        fill_shifts(shifted, 3 + k, theirs[k].astype(f32), True)

    loop(3, shifts)

    def step(r, _):
        window = shifted[:, strip_rows(2 - r)].reshape(960, 768)
        value = dot(act_t[...], window)
        for s in range(3):
            g[3 * r + s] = value[:, 256 * s : 256 * s + 256]
        return 0

    lax.fori_loop(0, 3, step, 0)


def spatial_conv_kernel(pos, shifted, weights, out, acc):
    acc[...] = jnp.zeros((480, 512), f32)

    def step(r, _):
        window = shifted[:, strip_rows(r)].reshape(480, 1536)
        acc[...] += dot(window, weights[pl.ds(3 + 3 * r, 3)].reshape(1536, 512))
        return 0

    lax.fori_loop(0, 3, step, 0)
    for k in range(3):
        out[k] = acc[160 * k : 160 * k + 160].astype(bf16)


def decode_kernel(pos, src, sp, weights, decoded, parts):

    def forward(k, _):
        parts[k] = dot(sp[...].reshape(480, 512), weights[k]).reshape(3, 160, 512)
        return 0

    lax.fori_loop(0, 3, forward, 0)

    def decode(g):
        u = src[g].astype(f32)
        both = parts[0, g] + parts[2, g + 1]
        decoded[2 * g] = (u + (both + parts[1, g])).astype(bf16)
        decoded[2 * g + 1] = (u + (both + parts[1, g + 1])).astype(bf16)

    loop(2, decode)


def input_grad_kernel(pos, src, c, terms, after, weights, grad_input, shifted, acc):
    edge = jnp.where(pos[FIRST] == 1, terms[0].astype(f32), 0.0)
    fill_shifts(shifted, 0, terms[1].astype(f32) + edge, True)
    fill_shifts(shifted, 1, terms[2].astype(f32) + after[...].astype(f32), True)
    acc[...] = jnp.zeros((320, 512), f32)

    def step(r, _):
        for s in range(3):
            window = shifted[:, strip_rows(2 - r), 512 * s : 512 * s + 512].reshape(320, 512)
            acc[...] += dot_nt(window, weights[3 + 3 * r + s])
        return 0

    lax.fori_loop(0, 3, step, 0)

    def finish(g):
        u = src[g].astype(f32)
        sigma = jax.nn.sigmoid(u)
        slope = sigma * (1.0 + u * (1.0 - sigma))
        cotangents = c[2 * g].astype(f32) + c[2 * g + 1].astype(f32)
        rows = pl.ds(pl.multiple_of(160 * g, 160), 160)
        grad_input[g] = (cotangents + acc[rows] * slope).astype(bf16)

    loop(2, finish)


def temporal_weight_grad_kernel(pos, sp, sps, mine, theirs, spatial, *refs):
    outs, (early, late, g) = refs[:4], refs[4:]
    early[...] = columns_of([ref[k].astype(f32) for ref in (sp, sps) for k in (0, 1)])
    late[...] = columns_of([ref[k].astype(f32) for ref in (sp, sps) for k in (1, 2)])
    outer = jnp.concatenate([mine[0], mine[2], theirs[0], theirs[2]], 0)
    inner = jnp.concatenate([mine[3], mine[1], theirs[3], theirs[1]], 0)
    zeros = jnp.zeros((160, 256), bf16)
    end = jnp.concatenate([zeros, mine[4], zeros, theirs[4]], 0)
    g[0] = spatial[8]
    g[1] = dot(early[...], outer)
    g[2] = dot(early[...], inner) + dot(late[...], end)
    g[3] = dot(late[...], outer)

    @pl.when(pos[CORE] == 0)
    def _():
        for offset, out in zip((0,) + RING, outs):
            x = mod4(pos[X] + offset)
            out[0:8] = spatial[pl.ds(2 * x, 2)].reshape(8, 128, 256).astype(out.dtype)
            out[8:12] = g[x].reshape(4, 128, 256).astype(out.dtype)

    @pl.when(pos[CORE] == 1)
    def _():
        for offset, out in zip((0,) + RING, outs):
            rows = pl.ds(pl.multiple_of(mod4(pos[Y] + offset) * 128, 128), 128)
            out[0:8] = spatial[0:8, rows].astype(out.dtype)
            out[8:12] = g[:, rows].astype(out.dtype)


def taps_of(x):
    return (2 * x, 2 * x + 1, 8 + x)


def second_exchange_kernel(pos, a, b1, b2, b3, *outs):
    for offset, out in zip((0,) + RING, outs):
        rows, taps = mod4(pos[Y] + offset), taps_of(mod4(pos[X] + offset))
        for t in range(3):
            block = jnp.where(pos[CORE] == 0, 4 * t + rows, taps[t])
            total = a[block] + b1[block].astype(f32) + b2[block].astype(f32)
            out[t] = (total + b3[block].astype(f32)).astype(out.dtype)


def core_rows_kernel(pos, a, b1, b2, b3, mine, theirs):
    total = a[...] + b1[...].astype(f32) + b2[...].astype(f32) + b3[...].astype(f32)
    total = total.reshape(3, 4, 2, 16, 256)
    lower = pos[CORE] == 0
    mine[...] = jnp.where(lower, total[:, :, 0], total[:, :, 1])
    theirs[...] = jnp.where(lower, total[:, :, 1], total[:, :, 0])


def third_exchange_kernel(pos, mine, theirs, *outs):
    lower = pos[CORE] == 0
    for offset, out in zip((0,) + RING, outs):
        zl = mod4(pos[ZL] + offset)
        for t in range(3):
            own, other = mine[t, zl], theirs[t, zl]
            out[t, :, :256] = jnp.where(lower, own, other).astype(out.dtype)
            out[t, :, 256:] = jnp.where(lower, other, own).astype(out.dtype)


def final_taps_kernel(pos, g0, g1, g2, g3, spatial, temporal, taps):
    for offset, piece in zip(REL, (g0, g1, g2, g3)):
        x = mod4(pos[X] - offset)
        taps[pl.ds(2 * x, 2)] = piece[0:2].astype(f32)
        taps[8 + x] = piece[2].astype(f32)
    spatial[...] = taps[0:9]
    temporal[...] = taps[9:12]


def exchange(axes, values):
    return [along(v, axes, o) for v, o in zip(values, RING)]


def per_device(frames_in, cotangent, w_spatial, w_temporal):
    src = frames_in[0].reshape(2, 160, 512)
    c = cotangent[0].reshape(4, 160, 512)
    first = lax.axis_index("x") * 2 + lax.axis_index("zh") == 0
    pos = jnp.stack(
        [
            lax.axis_index("y"),
            lax.axis_index("zl"),
            lax.axis_index("core"),
            lax.axis_index("x"),
            first.astype(jnp.int32),
        ]
    ).astype(jnp.int32)
    even = lax.axis_index("core") == 0
    low = jnp.concatenate([w_temporal, w_spatial[:3]], 0)
    high = w_spatial[3:]
    keep, give = jnp.where(even, high, low), jnp.where(even, low, high)
    before = lax.ppermute(src[1], ("x", "zh"), [(i, i + 1) for i in range(7)])
    pair = jnp.stack([keep, to_sibling(give)])
    ring = jnp.stack([pair] + exchange(("z", "y"), [pair] * 3))
    late_ring, before = lax.optimization_barrier((ring, before))
    rings = {3: late_ring, 1: ring, 2: ring}
    pieces = [ring] + [along(rings[o], ("y", "z"), o) for o in OUTER[1:]]
    frames = jnp.concatenate([jnp.where(first, src[0], before)[None], src], 0)
    sib_frames = to_sibling(frames)
    act_t, shifted, pairs_mine, pairs_theirs = call(
        prepare_kernel, 16, 3,
        [((512, 960), bf16), ((3, 192, 1536), bf16), ((5, 160, 256), bf16), ((5, 160, 256), bf16)],
        [pltpu.VMEM((6, 160, 512), f32)],
        pos, frames, sib_frames, c,
    )
    pairs_theirs = to_sibling(pairs_theirs)
    pieces[0], act_t = lax.optimization_barrier((pieces[0], act_t))
    pieces += [to_sibling(piece) for piece in pieces]

    terms, edge, mine, theirs, weights = call(
        temporal_grad_kernel, 24, 5,
        [
            ((3, 160, 512), bf16), ((160, 512), bf16), ((3, 160, 256), bf16), ((3, 160, 256), bf16),
            ((12, 512, 512), bf16),
        ],
        [pltpu.VMEM((3, 4, 160, 512), f32), pltpu.SemaphoreType.DMA((64,))],
        pos, c, *pieces, any_from=2,
    )
    theirs = to_sibling(theirs)
    (one,) = call(
        spatial_weight_grad_kernel, 20, 4,
        [((9, 512, 256), f32)], [pltpu.VMEM((6, 192, 768), bf16)],
        pos, act_t, mine, theirs,
    )
    (sp,) = call(
        spatial_conv_kernel, 16, 4, [((3, 160, 512), bf16)], [pltpu.VMEM((480, 512), f32)],
        pos, shifted, weights,
    )
    sib_sp = to_sibling(sp)
    grads = call(
        temporal_weight_grad_kernel, 28, 2,
        [((12, 128, 256), f32)] + [((12, 128, 256), bf16)] * 3,
        [pltpu.VMEM((512, 640), bf16), pltpu.VMEM((512, 640), bf16), pltpu.VMEM((4, 512, 256), f32)],
        pos, sp, sib_sp, pairs_mine, pairs_theirs, one,
    )
    received = exchange(("x", "y"), grads[1:])
    sp, edge, _ = lax.optimization_barrier((sp, edge, grads[0]))
    after = lax.ppermute(edge, ("x", "zh"), [(i, i - 1) for i in range(1, 8)])
    (decoded,) = call(
        decode_kernel, 20, 2, [((4, 160, 512), bf16)], [pltpu.VMEM((3, 3, 160, 512), f32)],
        pos, src, sp, weights,
    )
    (grad_input,) = call(
        input_grad_kernel, 20, 4, [((2, 160, 512), bf16)],
        [pltpu.VMEM((2, 192, 1536), bf16), pltpu.VMEM((320, 512), f32)],
        pos, src, c, terms, after, weights,
    )
    *received, decoded, grad_input = lax.optimization_barrier((*received, decoded, grad_input))
    two = call(
        second_exchange_kernel, 12, 1, [((3, 128, 256), f32)] + [((3, 128, 256), bf16)] * 3, [],
        pos, grads[0], *received,
    )
    rows_mine, rows_theirs = call(
        core_rows_kernel, 8, 1, [((3, 4, 16, 256), f32)] * 2, [],
        pos, two[0], *exchange(("y", "x"), two[1:]),
    )
    zs = call(
        third_exchange_kernel, 8, 1, [((3, 16, 512), f32)] + [((3, 16, 512), bf16)] * 3, [],
        pos, rows_mine, to_sibling(rows_theirs),
    )
    total = zs[0] + sum(part.astype(f32) for part in exchange(("z", "z"), zs[1:]))
    total = total.astype(bf16)
    other = lax.ppermute(total, "zh", [(0, 1), (1, 0)])
    taps = (total.astype(f32) + other.astype(f32)) * (1.0 / math.sqrt(256 * 640))
    taps = taps.astype(bf16)
    grad_s, grad_t = call(
        final_taps_kernel, 4, 1,
        [((9, 16, 512), f32), ((3, 16, 512), f32)],
        [pltpu.VMEM((12, 16, 512), f32)],
        pos, taps, *[along(taps, ("x", "x"), o) for o in RING],
    )
    return (
        decoded.reshape(1, 4, 10, 16, 512),
        grad_input.reshape(1, 2, 10, 16, 512),
        grad_s,
        grad_t,
    )


def solution(mesh):
    physical = Mesh(mesh.devices.reshape(SIZES), AXES)
    dp, tm = ("y", "zl", "core"), ("x", "zh")
    values, weights = P(dp, tm, None, None, None), P(None, dp, None)
    return jax.shard_map(
        per_device,
        mesh=physical,
        in_specs=(values, values, weights, weights),
        out_specs=(values, values, weights, weights),
        check_vma=False,
    )
```

```python
import math

import jax
import jax.numpy as jnp
from jax import lax
from jax.experimental import pallas as pl
from jax.experimental.pallas import tpu as pltpu
from jax.sharding import Mesh, PartitionSpec as P

f32 = jnp.float32
bf16 = jnp.bfloat16
RATE = 1000000000

AXES = ("y", "zl", "core", "x", "zh")
SIZES = (4, 4, 2, 4, 2)
RING = (2, 1, 3)
OUTER = (0, 3, 1, 2)
REL = (0, 2, 1, 3)
Y, ZL, CORE, X, FIRST, LAST = range(6)


def ring_pairs(axes, offset):
    sizes = dict(zip(AXES, SIZES))
    pairs = []
    for flat in range(math.prod(SIZES)):
        at, rest = {}, flat
        for name in reversed(AXES):
            rest, at[name] = divmod(rest, sizes[name])
        to = dict(at)
        axis = axes[at["core"]]
        if axis == "z":
            z = at["zh"] * 4 + at["zl"]
            steps = {1: 1, 3: -1, 2: 2 - 4 * (z % 2)}[offset]
            z = (z + steps) % 8
            to["zh"], to["zl"] = divmod(z, 4)
        else:
            to[axis] = (at[axis] + offset) % 4
        target = 0
        for name in AXES:
            target = target * sizes[name] + to[name]
        pairs.append((flat, target))
    return pairs


def along(value, axes, offset):
    return lax.ppermute(value, AXES, ring_pairs(axes, offset))


def to_sibling(value):
    return lax.ppermute(value, "core", [(0, 1), (1, 0)])


def call(kernel, mib, micros, outs, scratch, *args, any_from=None):
    count = len(args)
    any_from = count if any_from is None else any_from
    specs = [pl.BlockSpec(memory_space=pltpu.SMEM)]
    specs += [
        pl.BlockSpec(memory_space=pltpu.VMEM if i < any_from else pl.ANY) for i in range(1, count)
    ]
    return pl.pallas_call(
        kernel,
        out_shape=[jax.ShapeDtypeStruct(s, d) for s, d in outs],
        in_specs=specs,
        out_specs=[pl.BlockSpec(memory_space=pltpu.VMEM) for _ in outs],
        scratch_shapes=scratch,
        compiler_params=pltpu.CompilerParams(vmem_limit_bytes=mib * 1024 * 1024),
        cost_estimate=pl.CostEstimate(flops=micros * RATE, bytes_accessed=0, transcendentals=0),
        name=kernel.__name__,
    )(*args)


def mod4(value):
    return lax.rem(value + 4, 4)


def dot(left, right):
    return jnp.dot(left, right, preferred_element_type=f32)


def dot_nt(left, right):
    return lax.dot_general(left, right, (((1,), (1,)), ((), ())), preferred_element_type=f32)


def placements(pos, pieces, weights, sems):
    copies = []
    for a, piece in enumerate(pieces):
        core = pos[CORE] if a < 4 else 1 - pos[CORE]
        even = core == 0
        taps = pl.ds(jnp.where(even, 6, 0), 6)
        for k in range(4):
            y = mod4(pos[Y] - jnp.where(even, OUTER[a % 4], REL[k]))
            zl = mod4(pos[ZL] - jnp.where(even, REL[k], OUTER[a % 4]))
            for d in range(2):
                block = (y * 4 + zl) * 2 + (core if d == 0 else 1 - core)
                rows = pl.ds(pl.multiple_of(block * 16, 16), 16)
                copies.append(
                    pltpu.make_async_copy(
                        piece.at[k, d], weights.at[taps, rows, :], sems.at[8 * a + 2 * k + d]
                    )
                )
    return copies


def column_shifts(value):
    rows = value.shape[0]
    column = lax.broadcasted_iota(jnp.int32, value.shape, 0) % 16
    before = jnp.where(column == 0, 0.0, pltpu.roll(value, 1, 0))
    after = jnp.where(column == 15, 0.0, pltpu.roll(value, rows - 1, 0))
    return before, value, after


def fill_shifts(buffer, slot, value, reverse):
    before, centre, after = column_shifts(value)
    width = value.shape[1]
    buffer[slot, :16] = jnp.zeros((16, 3 * width), bf16)
    buffer[slot, 176:] = jnp.zeros((16, 3 * width), bf16)
    for s, shifted in enumerate((after, centre, before) if reverse else (before, centre, after)):
        buffer[slot, 16:176, s * width : (s + 1) * width] = shifted.astype(bf16)


def strip_rows(start):
    return pl.ds(pl.multiple_of(start * 16, 16), 160)


def split(pos, value, mine, theirs):
    lo, hi = value[:, :256], value[:, 256:]
    lower = pos[CORE] == 0
    mine[...] = jnp.where(lower, lo, hi)
    theirs[...] = jnp.where(lower, hi, lo)


def loop(count, step):
    lax.fori_loop(0, count, lambda k, _: (step(k), 0)[1], 0)


def temporal_grad_kernel(pos, c, *refs):
    pieces, (terms, edge, mine, theirs, weights, parts, sems) = refs[:8], refs[8:]
    copies = placements(pos, pieces, weights, sems)
    for copy in copies:
        copy.start()
    for copy in copies:
        copy.wait()

    def step(k, _):
        parts[k] = dot_nt(c[...].reshape(640, 512), weights[k]).reshape(4, 160, 512)
        return 0

    lax.fori_loop(0, 3, step, 0)
    p, q, r = (parts.at[k] for k in range(3))
    values = (p[0] + p[1] + q[0], p[2] + p[3] + q[1] + q[2] + r[0] + r[1], q[3] + r[2] + r[3])
    for k, value in enumerate(values):
        value = value.astype(bf16)
        terms[k] = value
        split(pos, value, mine.at[k], theirs.at[k])
    edge[...] = values[0].astype(bf16)


def columns_of(frames):
    return jnp.concatenate(frames, 0).T.astype(bf16)


def prepare_kernel(pos, frames, sib_frames, c, act_t, shifted, mine, theirs, act):
    def silu(k):
        act[k] = jax.nn.silu(frames[k].astype(f32))
        act[3 + k] = jax.nn.silu(sib_frames[k].astype(f32))

    loop(3, silu)
    act_t[...] = columns_of([act[...].reshape(960, 512)])
    loop(3, lambda k: fill_shifts(shifted, k, act[k], False))
    for k in range(3):
        value = (c[k].astype(f32) + c[k + 1].astype(f32)).astype(bf16)
        split(pos, value, mine.at[k], theirs.at[k])
    split(pos, c[0], mine.at[3], theirs.at[3])
    split(pos, c[3], mine.at[4], theirs.at[4])


def spatial_weight_grad_kernel(pos, act_t, mine, theirs, g, shifted):
    def shifts(k):
        fill_shifts(shifted, k, mine[k].astype(f32), True)
        fill_shifts(shifted, 3 + k, theirs[k].astype(f32), True)

    loop(3, shifts)

    def step(r, _):
        window = shifted[:, strip_rows(2 - r)].reshape(960, 768)
        value = dot(act_t[...], window)
        for s in range(3):
            g[3 * r + s] = value[:, 256 * s : 256 * s + 256]
        return 0

    lax.fori_loop(0, 3, step, 0)


def spatial_conv_kernel(pos, shifted, weights, out, acc):
    acc[...] = jnp.zeros((480, 512), f32)

    def step(r, _):
        window = shifted[:, strip_rows(r)].reshape(480, 1536)
        acc[...] += dot(window, weights[pl.ds(3 + 3 * r, 3)].reshape(1536, 512))
        return 0

    lax.fori_loop(0, 3, step, 0)
    for k in range(3):
        out[k] = acc[160 * k : 160 * k + 160].astype(bf16)


def decode_kernel(pos, src, sp, weights, decoded, parts):

    def forward(k, _):
        parts[k] = dot(sp[...].reshape(480, 512), weights[k]).reshape(3, 160, 512)
        return 0

    lax.fori_loop(0, 3, forward, 0)

    def decode(g):
        u = src[g].astype(f32)
        both = parts[0, g] + parts[2, g + 1]
        decoded[2 * g] = (u + (both + parts[1, g])).astype(bf16)
        decoded[2 * g + 1] = (u + (both + parts[1, g + 1])).astype(bf16)

    loop(2, decode)


def input_grad_kernel(pos, src, c, terms, after, weights, grad_input, shifted, acc):
    edge = jnp.where(pos[FIRST] == 1, terms[0].astype(f32), 0.0)
    fill_shifts(shifted, 0, terms[1].astype(f32) + edge, True)
    following = jnp.where(pos[LAST] == 1, 0.0, after[...].astype(f32))
    fill_shifts(shifted, 1, terms[2].astype(f32) + following, True)
    acc[...] = jnp.zeros((320, 512), f32)

    def step(r, _):
        for s in range(3):
            window = shifted[:, strip_rows(2 - r), 512 * s : 512 * s + 512].reshape(320, 512)
            acc[...] += dot_nt(window, weights[3 + 3 * r + s])
        return 0

    lax.fori_loop(0, 3, step, 0)

    def finish(g):
        u = src[g].astype(f32)
        sigma = jax.nn.sigmoid(u)
        slope = sigma * (1.0 + u * (1.0 - sigma))
        cotangents = c[2 * g].astype(f32) + c[2 * g + 1].astype(f32)
        rows = pl.ds(pl.multiple_of(160 * g, 160), 160)
        grad_input[g] = (cotangents + acc[rows] * slope).astype(bf16)

    loop(2, finish)


def temporal_weight_grad_kernel(pos, sp, sps, mine, theirs, spatial, *refs):
    outs, (early, late, g) = refs[:4], refs[4:]
    early[...] = columns_of([ref[k].astype(f32) for ref in (sp, sps) for k in (0, 1)])
    late[...] = columns_of([ref[k].astype(f32) for ref in (sp, sps) for k in (1, 2)])
    outer = jnp.concatenate([mine[0], mine[2], theirs[0], theirs[2]], 0)
    inner = jnp.concatenate([mine[3], mine[1], theirs[3], theirs[1]], 0)
    zeros = jnp.zeros((160, 256), bf16)
    end = jnp.concatenate([zeros, mine[4], zeros, theirs[4]], 0)
    g[0] = spatial[8]
    g[1] = dot(early[...], outer)
    g[2] = dot(early[...], inner) + dot(late[...], end)
    g[3] = dot(late[...], outer)

    @pl.when(pos[CORE] == 0)
    def _():
        for offset, out in zip((0,) + RING, outs):
            x = mod4(pos[X] + offset)
            out[0:8] = spatial[pl.ds(2 * x, 2)].reshape(8, 128, 256).astype(out.dtype)
            out[8:12] = g[x].reshape(4, 128, 256).astype(out.dtype)

    @pl.when(pos[CORE] == 1)
    def _():
        for offset, out in zip((0,) + RING, outs):
            rows = pl.ds(pl.multiple_of(mod4(pos[Y] + offset) * 128, 128), 128)
            out[0:8] = spatial[0:8, rows].astype(out.dtype)
            out[8:12] = g[:, rows].astype(out.dtype)


def taps_of(x):
    return (2 * x, 2 * x + 1, 8 + x)


def second_exchange_kernel(pos, a, b1, b2, b3, *outs):
    for offset, out in zip((0,) + RING, outs):
        rows, taps = mod4(pos[Y] + offset), taps_of(mod4(pos[X] + offset))
        for t in range(3):
            block = jnp.where(pos[CORE] == 0, 4 * t + rows, taps[t])
            total = a[block] + b1[block].astype(f32) + b2[block].astype(f32)
            out[t] = (total + b3[block].astype(f32)).astype(out.dtype)


def core_rows_kernel(pos, a, b1, b2, b3, mine, theirs):
    total = a[...] + b1[...].astype(f32) + b2[...].astype(f32) + b3[...].astype(f32)
    total = total.reshape(3, 4, 2, 16, 256)
    lower = pos[CORE] == 0
    mine[...] = jnp.where(lower, total[:, :, 0], total[:, :, 1])
    theirs[...] = jnp.where(lower, total[:, :, 1], total[:, :, 0])


def third_exchange_kernel(pos, mine, theirs, *outs):
    lower = pos[CORE] == 0
    for offset, out in zip((0,) + RING, outs):
        zl = mod4(pos[ZL] + offset)
        for t in range(3):
            own, other = mine[t, zl], theirs[t, zl]
            out[t, :, :256] = jnp.where(lower, own, other).astype(out.dtype)
            out[t, :, 256:] = jnp.where(lower, other, own).astype(out.dtype)


def final_taps_kernel(pos, g0, g1, g2, g3, spatial, temporal, taps):
    for offset, piece in zip(REL, (g0, g1, g2, g3)):
        x = mod4(pos[X] - offset)
        taps[pl.ds(2 * x, 2)] = piece[0:2].astype(f32)
        taps[8 + x] = piece[2].astype(f32)
    spatial[...] = taps[0:9]
    temporal[...] = taps[9:12]


def exchange(axes, values):
    return [along(v, axes, o) for v, o in zip(values, RING)]


def per_device(frames_in, cotangent, w_spatial, w_temporal):
    src = frames_in[0].reshape(2, 160, 512)
    c = cotangent[0].reshape(4, 160, 512)
    tm_index = lax.axis_index("x") * 2 + lax.axis_index("zh")
    first = tm_index == 0
    pos = jnp.stack(
        [
            lax.axis_index("y"),
            lax.axis_index("zl"),
            lax.axis_index("core"),
            lax.axis_index("x"),
            first.astype(jnp.int32),
            (tm_index == 7).astype(jnp.int32),
        ]
    ).astype(jnp.int32)
    even = lax.axis_index("core") == 0
    low = jnp.concatenate([w_temporal, w_spatial[:3]], 0)
    high = w_spatial[3:]
    keep, give = jnp.where(even, high, low), jnp.where(even, low, high)
    before = lax.ppermute(src[1], ("x", "zh"), [(i, (i + 1) % 8) for i in range(8)])
    pair = jnp.stack([keep, to_sibling(give)])
    ring = jnp.stack([pair] + exchange(("z", "y"), [pair] * 3))
    late_ring, before = lax.optimization_barrier((ring, before))
    rings = {3: late_ring, 1: ring, 2: ring}
    pieces = [ring] + [along(rings[o], ("y", "z"), o) for o in OUTER[1:]]
    frames = jnp.concatenate([jnp.where(first, src[0], before)[None], src], 0)
    sib_frames = to_sibling(frames)
    act_t, shifted, pairs_mine, pairs_theirs = call(
        prepare_kernel, 16, 3,
        [((512, 960), bf16), ((3, 192, 1536), bf16), ((5, 160, 256), bf16), ((5, 160, 256), bf16)],
        [pltpu.VMEM((6, 160, 512), f32)],
        pos, frames, sib_frames, c,
    )
    pairs_theirs = to_sibling(pairs_theirs)
    pieces[0], act_t = lax.optimization_barrier((pieces[0], act_t))
    pieces += [to_sibling(piece) for piece in pieces]

    terms, edge, mine, theirs, weights = call(
        temporal_grad_kernel, 24, 5,
        [
            ((3, 160, 512), bf16), ((160, 512), bf16), ((3, 160, 256), bf16), ((3, 160, 256), bf16),
            ((12, 512, 512), bf16),
        ],
        [pltpu.VMEM((3, 4, 160, 512), f32), pltpu.SemaphoreType.DMA((64,))],
        pos, c, *pieces, any_from=2,
    )
    theirs = to_sibling(theirs)
    (one,) = call(
        spatial_weight_grad_kernel, 20, 4,
        [((9, 512, 256), f32)], [pltpu.VMEM((6, 192, 768), bf16)],
        pos, act_t, mine, theirs,
    )
    (sp,) = call(
        spatial_conv_kernel, 16, 4, [((3, 160, 512), bf16)], [pltpu.VMEM((480, 512), f32)],
        pos, shifted, weights,
    )
    sib_sp = to_sibling(sp)
    grads = call(
        temporal_weight_grad_kernel, 28, 2,
        [((12, 128, 256), f32)] + [((12, 128, 256), bf16)] * 3,
        [pltpu.VMEM((512, 640), bf16), pltpu.VMEM((512, 640), bf16), pltpu.VMEM((4, 512, 256), f32)],
        pos, sp, sib_sp, pairs_mine, pairs_theirs, one,
    )
    received = exchange(("x", "y"), grads[1:])
    sp, edge, _ = lax.optimization_barrier((sp, edge, grads[0]))
    after = lax.ppermute(edge, ("x", "zh"), [(i, (i - 1) % 8) for i in range(8)])
    (decoded,) = call(
        decode_kernel, 20, 2, [((4, 160, 512), bf16)], [pltpu.VMEM((3, 3, 160, 512), f32)],
        pos, src, sp, weights,
    )
    (grad_input,) = call(
        input_grad_kernel, 20, 4, [((2, 160, 512), bf16)],
        [pltpu.VMEM((2, 192, 1536), bf16), pltpu.VMEM((320, 512), f32)],
        pos, src, c, terms, after, weights,
    )
    *received, decoded, grad_input = lax.optimization_barrier((*received, decoded, grad_input))
    two = call(
        second_exchange_kernel, 12, 1, [((3, 128, 256), f32)] + [((3, 128, 256), bf16)] * 3, [],
        pos, grads[0], *received,
    )
    rows_mine, rows_theirs = call(
        core_rows_kernel, 8, 1, [((3, 4, 16, 256), f32)] * 2, [],
        pos, two[0], *exchange(("y", "x"), two[1:]),
    )
    zs = call(
        third_exchange_kernel, 8, 1, [((3, 16, 512), f32)] + [((3, 16, 512), bf16)] * 3, [],
        pos, rows_mine, to_sibling(rows_theirs),
    )
    total = zs[0] + sum(part.astype(f32) for part in exchange(("z", "z"), zs[1:]))
    total = total.astype(bf16)
    other = lax.ppermute(total, "zh", [(0, 1), (1, 0)])
    taps = (total.astype(f32) + other.astype(f32)) * (1.0 / math.sqrt(256 * 640))
    taps = taps.astype(bf16)
    grad_s, grad_t = call(
        final_taps_kernel, 4, 1,
        [((9, 16, 512), f32), ((3, 16, 512), f32)],
        [pltpu.VMEM((12, 16, 512), f32)],
        pos, taps, *[along(taps, ("x", "x"), o) for o in RING],
    )
    return (
        decoded.reshape(1, 4, 10, 16, 512),
        grad_input.reshape(1, 2, 10, 16, 512),
        grad_s,
        grad_t,
    )


def solution(mesh):
    physical = Mesh(mesh.devices.reshape(SIZES), AXES)
    dp, tm = ("y", "zl", "core"), ("x", "zh")
    values, weights = P(dp, tm, None, None, None), P(None, dp, None)
    return jax.shard_map(
        per_device,
        mesh=physical,
        in_specs=(values, values, weights, weights),
        out_specs=(values, values, weights, weights),
        check_vma=False,
    )
```

```python
import math

import jax
import jax.numpy as jnp
from jax import lax
from jax.experimental import pallas as pl
from jax.experimental.pallas import tpu as pltpu
from jax.sharding import Mesh, PartitionSpec as P

f32 = jnp.float32
bf16 = jnp.bfloat16
RATE = 1000000000

AXES = ("y", "zl", "core", "x", "zh")
SIZES = (4, 4, 2, 4, 2)
RING = (2, 1, 3)
OUTER = (0, 3, 1, 2)
REL = (0, 2, 1, 3)
Y, ZL, CORE, X, FIRST = range(5)


def ring_pairs(axes, offset):
    sizes = dict(zip(AXES, SIZES))
    pairs = []
    for flat in range(math.prod(SIZES)):
        at, rest = {}, flat
        for name in reversed(AXES):
            rest, at[name] = divmod(rest, sizes[name])
        to = dict(at)
        axis = axes[at["core"]]
        if axis == "z":
            z = at["zh"] * 4 + at["zl"]
            steps = {1: 1, 3: -1, 2: 2 - 4 * (z % 2)}[offset]
            z = (z + steps) % 8
            to["zh"], to["zl"] = divmod(z, 4)
        else:
            to[axis] = (at[axis] + offset) % 4
        target = 0
        for name in AXES:
            target = target * sizes[name] + to[name]
        pairs.append((flat, target))
    return pairs


def along(value, axes, offset):
    return lax.ppermute(value, AXES, ring_pairs(axes, offset))


def to_sibling(value):
    return lax.ppermute(value, "core", [(0, 1), (1, 0)])


def call(kernel, mib, micros, outs, scratch, *args, any_from=None, aliases=None):
    count = len(args)
    any_from = count if any_from is None else any_from
    specs = [pl.BlockSpec(memory_space=pltpu.SMEM)]
    specs += [
        pl.BlockSpec(memory_space=pltpu.VMEM if i < any_from else pl.ANY) for i in range(1, count)
    ]
    return pl.pallas_call(
        kernel,
        out_shape=[jax.ShapeDtypeStruct(s, d) for s, d in outs],
        in_specs=specs,
        out_specs=[pl.BlockSpec(memory_space=pltpu.VMEM) for _ in outs],
        scratch_shapes=scratch,
        compiler_params=pltpu.CompilerParams(vmem_limit_bytes=mib * 1024 * 1024),
        cost_estimate=pl.CostEstimate(flops=micros * RATE, bytes_accessed=0, transcendentals=0),
        input_output_aliases=aliases or {},
        name=kernel.__name__,
    )(*args)


def mod4(value):
    return lax.rem(value + 4, 4)


def dot(left, right):
    return jnp.dot(left, right, preferred_element_type=f32)


def dot_nt(left, right):
    return lax.dot_general(left, right, (((1,), (1,)), ((), ())), preferred_element_type=f32)


def placements(pos, pieces, gatherer, weights, sems):
    copies = []
    for a, piece in enumerate(pieces):
        even = gatherer == 0
        taps = pl.ds(jnp.where(even, 6, 0), 6)
        for k in range(4):
            y = mod4(pos[Y] - jnp.where(even, OUTER[a], REL[k]))
            zl = mod4(pos[ZL] - jnp.where(even, REL[k], OUTER[a]))
            for d in range(2):
                block = (y * 4 + zl) * 2 + (gatherer if d == 0 else 1 - gatherer)
                rows = pl.ds(pl.multiple_of(block * 16, 16), 16)
                copies.append(
                    pltpu.make_async_copy(
                        piece.at[k, d], weights.at[taps, rows, :], sems.at[8 * a + 2 * k + d]
                    )
                )
    return copies


def column_shifts(value):
    rows = value.shape[0]
    column = lax.broadcasted_iota(jnp.int32, value.shape, 0) % 16
    before = jnp.where(column == 0, 0.0, pltpu.roll(value, 1, 0))
    after = jnp.where(column == 15, 0.0, pltpu.roll(value, rows - 1, 0))
    return before, value, after


def fill_shifts(buffer, slot, value, reverse):
    before, centre, after = column_shifts(value)
    width = value.shape[1]
    buffer[slot, :16] = jnp.zeros((16, 3 * width), bf16)
    buffer[slot, 176:] = jnp.zeros((16, 3 * width), bf16)
    for s, shifted in enumerate((after, centre, before) if reverse else (before, centre, after)):
        buffer[slot, 16:176, s * width : (s + 1) * width] = shifted.astype(bf16)


def strip_rows(start):
    return pl.ds(pl.multiple_of(start * 16, 16), 160)


def split(pos, value, mine, theirs):
    lo, hi = value[:, :256], value[:, 256:]
    lower = pos[CORE] == 0
    mine[...] = jnp.where(lower, lo, hi)
    theirs[...] = jnp.where(lower, hi, lo)


def loop(count, step):
    lax.fori_loop(0, count, lambda k, _: (step(k), 0)[1], 0)


def assemble_kernel(pos, *refs):
    pieces, (weights, sems) = refs[:4], refs[4:]
    copies = placements(pos, pieces, pos[CORE], weights, sems)
    for copy in copies:
        copy.start()
    for copy in copies:
        copy.wait()


def temporal_grad_kernel(pos, c, partial, *refs):
    pieces, (terms, edge, mine, theirs, weights, parts, sems) = refs[:4], refs[4:]
    copies = placements(pos, pieces, 1 - pos[CORE], weights, sems)
    for copy in copies:
        copy.start()
    for copy in copies:
        copy.wait()

    def step(k, _):
        parts[k] = dot_nt(c[...].reshape(640, 512), weights[k]).reshape(4, 160, 512)
        return 0

    lax.fori_loop(0, 3, step, 0)
    p, q, r = (parts.at[k] for k in range(3))
    values = (p[0] + p[1] + q[0], p[2] + p[3] + q[1] + q[2] + r[0] + r[1], q[3] + r[2] + r[3])
    for k, value in enumerate(values):
        value = value.astype(bf16)
        terms[k] = value
        split(pos, value, mine.at[k], theirs.at[k])
    edge[...] = values[0].astype(bf16)


def columns_of(frames):
    return jnp.concatenate(frames, 0).T.astype(bf16)


def prepare_kernel(pos, frames, sib_frames, c, act_t, shifted, mine, theirs, act):
    def silu(k):
        act[k] = jax.nn.silu(frames[k].astype(f32))
        act[3 + k] = jax.nn.silu(sib_frames[k].astype(f32))

    loop(3, silu)
    act_t[...] = columns_of([act[...].reshape(960, 512)])
    loop(3, lambda k: fill_shifts(shifted, k, act[k], False))
    for k in range(3):
        value = (c[k].astype(f32) + c[k + 1].astype(f32)).astype(bf16)
        split(pos, value, mine.at[k], theirs.at[k])
    split(pos, c[0], mine.at[3], theirs.at[3])
    split(pos, c[3], mine.at[4], theirs.at[4])


def spatial_weight_grad_kernel(pos, act_t, mine, theirs, g, shifted):
    def shifts(k):
        fill_shifts(shifted, k, mine[k].astype(f32), True)
        fill_shifts(shifted, 3 + k, theirs[k].astype(f32), True)

    loop(3, shifts)

    def step(r, _):
        window = shifted[:, strip_rows(2 - r)].reshape(960, 768)
        value = dot(act_t[...], window)
        for s in range(3):
            g[3 * r + s] = value[:, 256 * s : 256 * s + 256]
        return 0

    lax.fori_loop(0, 3, step, 0)


def spatial_conv_kernel(pos, shifted, weights, out, acc):
    acc[...] = jnp.zeros((480, 512), f32)

    def step(r, _):
        window = shifted[:, strip_rows(r)].reshape(480, 1536)
        acc[...] += dot(window, weights[pl.ds(3 + 3 * r, 3)].reshape(1536, 512))
        return 0

    lax.fori_loop(0, 3, step, 0)
    for k in range(3):
        out[k] = acc[160 * k : 160 * k + 160].astype(bf16)


def decode_kernel(pos, src, sp, weights, decoded, parts):

    def forward(k, _):
        parts[k] = dot(sp[...].reshape(480, 512), weights[k]).reshape(3, 160, 512)
        return 0

    lax.fori_loop(0, 3, forward, 0)

    def decode(g):
        u = src[g].astype(f32)
        both = parts[0, g] + parts[2, g + 1]
        decoded[2 * g] = (u + (both + parts[1, g])).astype(bf16)
        decoded[2 * g + 1] = (u + (both + parts[1, g + 1])).astype(bf16)

    loop(2, decode)


def input_grad_kernel(pos, src, c, terms, after, weights, grad_input, shifted, acc):
    edge = jnp.where(pos[FIRST] == 1, terms[0].astype(f32), 0.0)
    fill_shifts(shifted, 0, terms[1].astype(f32) + edge, True)
    fill_shifts(shifted, 1, terms[2].astype(f32) + after[...].astype(f32), True)
    acc[...] = jnp.zeros((320, 512), f32)

    def step(r, _):
        for s in range(3):
            window = shifted[:, strip_rows(2 - r), 512 * s : 512 * s + 512].reshape(320, 512)
            acc[...] += dot_nt(window, weights[3 + 3 * r + s])
        return 0

    lax.fori_loop(0, 3, step, 0)

    def finish(g):
        u = src[g].astype(f32)
        sigma = jax.nn.sigmoid(u)
        slope = sigma * (1.0 + u * (1.0 - sigma))
        cotangents = c[2 * g].astype(f32) + c[2 * g + 1].astype(f32)
        rows = pl.ds(pl.multiple_of(160 * g, 160), 160)
        grad_input[g] = (cotangents + acc[rows] * slope).astype(bf16)

    loop(2, finish)


def temporal_weight_grad_kernel(pos, sp, sps, mine, theirs, spatial, *refs):
    outs, (early, late, g) = refs[:4], refs[4:]
    early[...] = columns_of([ref[k].astype(f32) for ref in (sp, sps) for k in (0, 1)])
    late[...] = columns_of([ref[k].astype(f32) for ref in (sp, sps) for k in (1, 2)])
    outer = jnp.concatenate([mine[0], mine[2], theirs[0], theirs[2]], 0)
    inner = jnp.concatenate([mine[3], mine[1], theirs[3], theirs[1]], 0)
    zeros = jnp.zeros((160, 256), bf16)
    end = jnp.concatenate([zeros, mine[4], zeros, theirs[4]], 0)
    g[0] = spatial[8]
    g[1] = dot(early[...], outer)
    g[2] = dot(early[...], inner) + dot(late[...], end)
    g[3] = dot(late[...], outer)

    @pl.when(pos[CORE] == 0)
    def _():
        for offset, out in zip((0,) + RING, outs):
            x = mod4(pos[X] + offset)
            out[0:8] = spatial[pl.ds(2 * x, 2)].reshape(8, 128, 256).astype(out.dtype)
            out[8:12] = g[x].reshape(4, 128, 256).astype(out.dtype)

    @pl.when(pos[CORE] == 1)
    def _():
        for offset, out in zip((0,) + RING, outs):
            rows = pl.ds(pl.multiple_of(mod4(pos[Y] + offset) * 128, 128), 128)
            out[0:8] = spatial[0:8, rows].astype(out.dtype)
            out[8:12] = g[:, rows].astype(out.dtype)


def taps_of(x):
    return (2 * x, 2 * x + 1, 8 + x)


def second_exchange_kernel(pos, a, b1, b2, b3, *outs):
    for offset, out in zip((0,) + RING, outs):
        rows, taps = mod4(pos[Y] + offset), taps_of(mod4(pos[X] + offset))
        for t in range(3):
            block = jnp.where(pos[CORE] == 0, 4 * t + rows, taps[t])
            total = a[block] + b1[block].astype(f32) + b2[block].astype(f32)
            out[t] = (total + b3[block].astype(f32)).astype(out.dtype)


def core_rows_kernel(pos, a, b1, b2, b3, mine, theirs):
    total = a[...] + b1[...].astype(f32) + b2[...].astype(f32) + b3[...].astype(f32)
    total = total.reshape(3, 4, 2, 16, 256)
    lower = pos[CORE] == 0
    mine[...] = jnp.where(lower, total[:, :, 0], total[:, :, 1])
    theirs[...] = jnp.where(lower, total[:, :, 1], total[:, :, 0])


def third_exchange_kernel(pos, mine, theirs, *outs):
    lower = pos[CORE] == 0
    for offset, out in zip((0,) + RING, outs):
        zl = mod4(pos[ZL] + offset)
        for t in range(3):
            own, other = mine[t, zl], theirs[t, zl]
            out[t, :, :256] = jnp.where(lower, own, other).astype(out.dtype)
            out[t, :, 256:] = jnp.where(lower, other, own).astype(out.dtype)


def final_taps_kernel(pos, g0, g1, g2, g3, spatial, temporal, taps):
    for offset, piece in zip(REL, (g0, g1, g2, g3)):
        x = mod4(pos[X] - offset)
        taps[pl.ds(2 * x, 2)] = piece[0:2].astype(f32)
        taps[8 + x] = piece[2].astype(f32)
    spatial[...] = taps[0:9]
    temporal[...] = taps[9:12]


def exchange(axes, values):
    return [along(v, axes, o) for v, o in zip(values, RING)]


def per_device(frames_in, cotangent, w_spatial, w_temporal):
    src = frames_in[0].reshape(2, 160, 512)
    c = cotangent[0].reshape(4, 160, 512)
    first = lax.axis_index("x") * 2 + lax.axis_index("zh") == 0
    pos = jnp.stack(
        [
            lax.axis_index("y"),
            lax.axis_index("zl"),
            lax.axis_index("core"),
            lax.axis_index("x"),
            first.astype(jnp.int32),
        ]
    ).astype(jnp.int32)
    even = lax.axis_index("core") == 0
    low = jnp.concatenate([w_temporal, w_spatial[:3]], 0)
    high = w_spatial[3:]
    keep, give = jnp.where(even, high, low), jnp.where(even, low, high)
    before = lax.ppermute(src[1], ("x", "zh"), [(i, i + 1) for i in range(7)])
    pair = jnp.stack([keep, to_sibling(give)])
    ring = jnp.stack([pair] + exchange(("z", "y"), [pair] * 3))
    late_ring, before = lax.optimization_barrier((ring, before))
    rings = {3: late_ring, 1: ring, 2: ring}
    pieces = [ring] + [along(rings[o], ("y", "z"), o) for o in OUTER[1:]]
    frames = jnp.concatenate([jnp.where(first, src[0], before)[None], src], 0)
    sib_frames = to_sibling(frames)
    act_t, shifted, pairs_mine, pairs_theirs = call(
        prepare_kernel, 16, 3,
        [((512, 960), bf16), ((3, 192, 1536), bf16), ((5, 160, 256), bf16), ((5, 160, 256), bf16)],
        [pltpu.VMEM((6, 160, 512), f32)],
        pos, frames, sib_frames, c,
    )
    pairs_theirs = to_sibling(pairs_theirs)
    pieces[0], act_t = lax.optimization_barrier((pieces[0], act_t))
    sib_pieces = [to_sibling(piece) for piece in pieces]
    (weights,) = call(
        assemble_kernel, 4, 2, [((12, 512, 512), bf16)], [pltpu.SemaphoreType.DMA((32,))],
        pos, *pieces, any_from=1,
    )
    terms, edge, mine, theirs, weights = call(
        temporal_grad_kernel, 24, 5,
        [
            ((3, 160, 512), bf16), ((160, 512), bf16), ((3, 160, 256), bf16), ((3, 160, 256), bf16),
            ((12, 512, 512), bf16),
        ],
        [pltpu.VMEM((3, 4, 160, 512), f32), pltpu.SemaphoreType.DMA((32,))],
        pos, c, weights, *sib_pieces, any_from=3, aliases={2: 4},
    )
    theirs = to_sibling(theirs)
    (one,) = call(
        spatial_weight_grad_kernel, 20, 4,
        [((9, 512, 256), f32)], [pltpu.VMEM((6, 192, 768), bf16)],
        pos, act_t, mine, theirs,
    )
    (sp,) = call(
        spatial_conv_kernel, 16, 4, [((3, 160, 512), bf16)], [pltpu.VMEM((480, 512), f32)],
        pos, shifted, weights,
    )
    sib_sp = to_sibling(sp)
    grads = call(
        temporal_weight_grad_kernel, 28, 2,
        [((12, 128, 256), f32)] + [((12, 128, 256), bf16)] * 3,
        [pltpu.VMEM((512, 640), bf16), pltpu.VMEM((512, 640), bf16), pltpu.VMEM((4, 512, 256), f32)],
        pos, sp, sib_sp, pairs_mine, pairs_theirs, one,
    )
    received = exchange(("x", "y"), grads[1:])
    sp, edge, _ = lax.optimization_barrier((sp, edge, grads[0]))
    after = lax.ppermute(edge, ("x", "zh"), [(i, i - 1) for i in range(1, 8)])
    (decoded,) = call(
        decode_kernel, 20, 2, [((4, 160, 512), bf16)], [pltpu.VMEM((3, 3, 160, 512), f32)],
        pos, src, sp, weights,
    )
    (grad_input,) = call(
        input_grad_kernel, 20, 4, [((2, 160, 512), bf16)],
        [pltpu.VMEM((2, 192, 1536), bf16), pltpu.VMEM((320, 512), f32)],
        pos, src, c, terms, after, weights,
    )
    *received, decoded, grad_input = lax.optimization_barrier((*received, decoded, grad_input))
    two = call(
        second_exchange_kernel, 12, 1, [((3, 128, 256), f32)] + [((3, 128, 256), bf16)] * 3, [],
        pos, grads[0], *received,
    )
    rows_mine, rows_theirs = call(
        core_rows_kernel, 8, 1, [((3, 4, 16, 256), f32)] * 2, [],
        pos, two[0], *exchange(("y", "x"), two[1:]),
    )
    zs = call(
        third_exchange_kernel, 8, 1, [((3, 16, 512), f32)] + [((3, 16, 512), bf16)] * 3, [],
        pos, rows_mine, to_sibling(rows_theirs),
    )
    total = zs[0] + sum(part.astype(f32) for part in exchange(("z", "z"), zs[1:]))
    total = total.astype(bf16)
    other = lax.ppermute(total, "zh", [(0, 1), (1, 0)])
    taps = (total.astype(f32) + other.astype(f32)) * (1.0 / math.sqrt(256 * 640))
    taps = taps.astype(bf16)
    grad_s, grad_t = call(
        final_taps_kernel, 4, 1,
        [((9, 16, 512), f32), ((3, 16, 512), f32)],
        [pltpu.VMEM((12, 16, 512), f32)],
        pos, taps, *[along(taps, ("x", "x"), o) for o in RING],
    )
    return (
        decoded.reshape(1, 4, 10, 16, 512),
        grad_input.reshape(1, 2, 10, 16, 512),
        grad_s,
        grad_t,
    )


def solution(mesh):
    physical = Mesh(mesh.devices.reshape(SIZES), AXES)
    dp, tm = ("y", "zl", "core"), ("x", "zh")
    values, weights = P(dp, tm, None, None, None), P(None, dp, None)
    return jax.shard_map(
        per_device,
        mesh=physical,
        in_specs=(values, values, weights, weights),
        out_specs=(values, values, weights, weights),
        check_vma=False,
    )
```

```python
import math

import jax
import jax.numpy as jnp
from jax import lax
from jax.experimental import pallas as pl
from jax.experimental.pallas import tpu as pltpu
from jax.sharding import Mesh, PartitionSpec as P

f32 = jnp.float32
bf16 = jnp.bfloat16
RATE = 1000000000

AXES = ("y", "zl", "core", "x", "zh")
SIZES = (4, 4, 2, 4, 2)
RING = (2, 1, 3)
OUTER = (0, 3, 1, 2)
REL = (0, 2, 1, 3)
Y, ZL, CORE, X, FIRST = range(5)


def ring_pairs(axes, offset):
    sizes = dict(zip(AXES, SIZES))
    pairs = []
    for flat in range(math.prod(SIZES)):
        at, rest = {}, flat
        for name in reversed(AXES):
            rest, at[name] = divmod(rest, sizes[name])
        to = dict(at)
        axis = axes[at["core"]]
        if axis == "z":
            z = at["zh"] * 4 + at["zl"]
            steps = {1: 1, 3: -1, 2: 2 - 4 * (z % 2)}[offset]
            z = (z + steps) % 8
            to["zh"], to["zl"] = divmod(z, 4)
        else:
            to[axis] = (at[axis] + offset) % 4
        target = 0
        for name in AXES:
            target = target * sizes[name] + to[name]
        pairs.append((flat, target))
    return pairs


def along(value, axes, offset):
    return lax.ppermute(value, AXES, ring_pairs(axes, offset))


def to_sibling(value):
    return lax.ppermute(value, "core", [(0, 1), (1, 0)])


def call(kernel, mib, micros, outs, scratch, *args, any_from=None, aliases=None):
    count = len(args)
    any_from = count if any_from is None else any_from
    specs = [pl.BlockSpec(memory_space=pltpu.SMEM)]
    specs += [
        pl.BlockSpec(memory_space=pltpu.VMEM if i < any_from else pl.ANY) for i in range(1, count)
    ]
    return pl.pallas_call(
        kernel,
        out_shape=[jax.ShapeDtypeStruct(s, d) for s, d in outs],
        in_specs=specs,
        out_specs=[pl.BlockSpec(memory_space=pltpu.VMEM) for _ in outs],
        scratch_shapes=scratch,
        compiler_params=pltpu.CompilerParams(vmem_limit_bytes=mib * 1024 * 1024),
        cost_estimate=pl.CostEstimate(flops=micros * RATE, bytes_accessed=0, transcendentals=0),
        input_output_aliases=aliases or {},
        name=kernel.__name__,
    )(*args)


def mod4(value):
    return lax.rem(value + 4, 4)


def dot(left, right):
    return jnp.dot(left, right, preferred_element_type=f32)


def dot_nt(left, right):
    return lax.dot_general(left, right, (((1,), (1,)), ((), ())), preferred_element_type=f32)


def placements(pos, pieces, gatherer, weights, sems):
    copies = []
    for a, piece in enumerate(pieces):
        even = gatherer == 0
        taps = pl.ds(jnp.where(even, 6, 0), 6)
        for k in range(4):
            y = mod4(pos[Y] - jnp.where(even, OUTER[a], REL[k]))
            zl = mod4(pos[ZL] - jnp.where(even, REL[k], OUTER[a]))
            for d in range(2):
                block = (y * 4 + zl) * 2 + (gatherer if d == 0 else 1 - gatherer)
                rows = pl.ds(pl.multiple_of(block * 16, 16), 16)
                copies.append(
                    pltpu.make_async_copy(
                        piece.at[k, d], weights.at[taps, rows, :], sems.at[8 * a + 2 * k + d]
                    )
                )
    return copies


def column_shifts(value):
    rows = value.shape[0]
    column = lax.broadcasted_iota(jnp.int32, value.shape, 0) % 16
    before = jnp.where(column == 0, 0.0, pltpu.roll(value, 1, 0))
    after = jnp.where(column == 15, 0.0, pltpu.roll(value, rows - 1, 0))
    return before, value, after


def fill_shifts(buffer, slot, value, reverse):
    before, centre, after = column_shifts(value)
    width = value.shape[1]
    buffer[slot, :16] = jnp.zeros((16, 3 * width), bf16)
    buffer[slot, 176:] = jnp.zeros((16, 3 * width), bf16)
    for s, shifted in enumerate((after, centre, before) if reverse else (before, centre, after)):
        buffer[slot, 16:176, s * width : (s + 1) * width] = shifted.astype(bf16)


def strip_rows(start):
    return pl.ds(pl.multiple_of(start * 16, 16), 160)


def split(pos, value, mine, theirs):
    lo, hi = value[:, :256], value[:, 256:]
    lower = pos[CORE] == 0
    mine[...] = jnp.where(lower, lo, hi)
    theirs[...] = jnp.where(lower, hi, lo)


def loop(count, step):
    lax.fori_loop(0, count, lambda k, _: (step(k), 0)[1], 0)


def assemble_kernel(pos, *refs):
    pieces, (weights, sems) = refs[:4], refs[4:]
    copies = placements(pos, pieces, pos[CORE], weights, sems)
    for copy in copies:
        copy.start()
    for copy in copies:
        copy.wait()


def temporal_grad_kernel(pos, c, partial, *refs):
    pieces, (terms, edge, mine, theirs, weights, parts, sems) = refs[:4], refs[4:]
    copies = placements(pos, pieces, 1 - pos[CORE], weights, sems)
    for copy in copies:
        copy.start()
    for copy in copies:
        copy.wait()

    def step(k, _):
        parts[k] = dot_nt(c[...].reshape(640, 512), weights[k]).reshape(4, 160, 512)
        return 0

    lax.fori_loop(0, 3, step, 0)
    p, q, r = (parts.at[k] for k in range(3))
    values = (p[0] + p[1] + q[0], p[2] + p[3] + q[1] + q[2] + r[0] + r[1], q[3] + r[2] + r[3])
    for k, value in enumerate(values):
        value = value.astype(bf16)
        terms[k] = value
        split(pos, value, mine.at[k], theirs.at[k])
    edge[...] = values[0].astype(bf16)


def columns_of(frames):
    return jnp.concatenate(frames, 0).T.astype(bf16)


def prepare_kernel(pos, frames, sib_frames, c, act_t, shifted, mine, theirs, act):
    def silu(k):
        act[k] = jax.nn.silu(frames[k].astype(f32))
        act[3 + k] = jax.nn.silu(sib_frames[k].astype(f32))

    loop(3, silu)
    act_t[...] = columns_of([act[...].reshape(960, 512)])
    loop(3, lambda k: fill_shifts(shifted, k, act[k], False))
    for k in range(3):
        value = (c[k].astype(f32) + c[k + 1].astype(f32)).astype(bf16)
        split(pos, value, mine.at[k], theirs.at[k])
    split(pos, c[0], mine.at[3], theirs.at[3])
    split(pos, c[3], mine.at[4], theirs.at[4])


def spatial_weight_grad_kernel(pos, act_t, mine, theirs, g, shifted):
    def shifts(k):
        fill_shifts(shifted, k, mine[k].astype(f32), True)
        fill_shifts(shifted, 3 + k, theirs[k].astype(f32), True)

    loop(3, shifts)

    def step(r, _):
        window = shifted[:, strip_rows(2 - r)].reshape(960, 768)
        value = dot(act_t[...], window)
        for s in range(3):
            g[3 * r + s] = value[:, 256 * s : 256 * s + 256]
        return 0

    lax.fori_loop(0, 3, step, 0)


def spatial_conv_kernel(pos, shifted, weights, out, acc):
    acc[...] = jnp.zeros((480, 512), f32)

    def step(r, _):
        window = shifted[:, strip_rows(r)].reshape(480, 1536)
        acc[...] += dot(window, weights[pl.ds(3 + 3 * r, 3)].reshape(1536, 512))
        return 0

    lax.fori_loop(0, 3, step, 0)
    for k in range(3):
        out[k] = acc[160 * k : 160 * k + 160].astype(bf16)


def decode_kernel(pos, src, sp, weights, decoded, parts):

    def forward(k, _):
        parts[k] = dot(sp[...].reshape(480, 512), weights[k]).reshape(3, 160, 512)
        return 0

    lax.fori_loop(0, 3, forward, 0)

    def decode(g):
        u = src[g].astype(f32)
        both = parts[0, g] + parts[2, g + 1]
        decoded[2 * g] = (u + (both + parts[1, g])).astype(bf16)
        decoded[2 * g + 1] = (u + (both + parts[1, g + 1])).astype(bf16)

    loop(2, decode)


def input_grad_kernel(pos, src, c, terms, after, weights, grad_input, shifted, acc):
    edge = jnp.where(pos[FIRST] == 1, terms[0].astype(f32), 0.0)
    fill_shifts(shifted, 0, terms[1].astype(f32) + edge, True)
    fill_shifts(shifted, 1, terms[2].astype(f32) + after[...].astype(f32), True)
    acc[...] = jnp.zeros((320, 512), f32)

    def step(r, _):
        for s in range(3):
            window = shifted[:, strip_rows(2 - r), 512 * s : 512 * s + 512].reshape(320, 512)
            acc[...] += dot_nt(window, weights[3 + 3 * r + s])
        return 0

    lax.fori_loop(0, 3, step, 0)

    def finish(g):
        u = src[g].astype(f32)
        sigma = jax.nn.sigmoid(u)
        slope = sigma * (1.0 + u * (1.0 - sigma))
        cotangents = c[2 * g].astype(f32) + c[2 * g + 1].astype(f32)
        rows = pl.ds(pl.multiple_of(160 * g, 160), 160)
        grad_input[g] = (cotangents + acc[rows] * slope).astype(bf16)

    loop(2, finish)


def temporal_weight_grad_kernel(pos, sp, sps, mine, theirs, spatial, *refs):
    outs, (early, late, g) = refs[:4], refs[4:]
    early[...] = columns_of([ref[k].astype(f32) for ref in (sp, sps) for k in (0, 1)])
    late[...] = columns_of([ref[k].astype(f32) for ref in (sp, sps) for k in (1, 2)])
    outer = jnp.concatenate([mine[0], mine[2], theirs[0], theirs[2]], 0)
    inner = jnp.concatenate([mine[3], mine[1], theirs[3], theirs[1]], 0)
    zeros = jnp.zeros((160, 256), bf16)
    end = jnp.concatenate([zeros, mine[4], zeros, theirs[4]], 0)
    g[0] = spatial[8]
    g[1] = dot(early[...], outer)
    g[2] = dot(early[...], inner) + dot(late[...], end)
    g[3] = dot(late[...], outer)

    @pl.when(pos[CORE] == 0)
    def _():
        for offset, out in zip((0,) + RING, outs):
            x = mod4(pos[X] + offset)
            out[0:8] = spatial[pl.ds(2 * x, 2)].reshape(8, 128, 256).astype(out.dtype)
            out[8:12] = g[x].reshape(4, 128, 256).astype(out.dtype)

    @pl.when(pos[CORE] == 1)
    def _():
        for offset, out in zip((0,) + RING, outs):
            rows = pl.ds(pl.multiple_of(mod4(pos[Y] + offset) * 128, 128), 128)
            out[0:8] = spatial[0:8, rows].astype(out.dtype)
            out[8:12] = g[:, rows].astype(out.dtype)


def taps_of(x):
    return (2 * x, 2 * x + 1, 8 + x)


def second_exchange_kernel(pos, a, b1, b2, b3, *outs):
    for offset, out in zip((0,) + RING, outs):
        rows, taps = mod4(pos[Y] + offset), taps_of(mod4(pos[X] + offset))
        for t in range(3):
            block = jnp.where(pos[CORE] == 0, 4 * t + rows, taps[t])
            total = a[block] + b1[block].astype(f32) + b2[block].astype(f32)
            out[t] = (total + b3[block].astype(f32)).astype(out.dtype)


def core_rows_kernel(pos, a, b1, b2, b3, mine, theirs):
    total = a[...] + b1[...].astype(f32) + b2[...].astype(f32) + b3[...].astype(f32)
    total = total.reshape(3, 4, 2, 16, 256)
    lower = pos[CORE] == 0
    mine[...] = jnp.where(lower, total[:, :, 0], total[:, :, 1])
    theirs[...] = jnp.where(lower, total[:, :, 1], total[:, :, 0])


def third_exchange_kernel(pos, mine, theirs, *outs):
    lower = pos[CORE] == 0
    for offset, out in zip((0,) + RING, outs):
        zl = mod4(pos[ZL] + offset)
        for t in range(3):
            own, other = mine[t, zl], theirs[t, zl]
            out[t, :, :256] = jnp.where(lower, own, other).astype(out.dtype)
            out[t, :, 256:] = jnp.where(lower, other, own).astype(out.dtype)


def final_taps_kernel(pos, g0, g1, g2, g3, spatial, temporal, taps):
    for offset, piece in zip(OUTER, (g0, g1, g2, g3)):
        x = mod4(pos[X] - offset)
        taps[pl.ds(2 * x, 2)] = piece[0:2].astype(f32)
        taps[8 + x] = piece[2].astype(f32)
    spatial[...] = taps[0:9]
    temporal[...] = taps[9:12]


def exchange(axes, values):
    return [along(v, axes, o) for v, o in zip(values, RING)]


def per_device(frames_in, cotangent, w_spatial, w_temporal):
    src = frames_in[0].reshape(2, 160, 512)
    c = cotangent[0].reshape(4, 160, 512)
    first = lax.axis_index("x") * 2 + lax.axis_index("zh") == 0
    pos = jnp.stack(
        [
            lax.axis_index("y"),
            lax.axis_index("zl"),
            lax.axis_index("core"),
            lax.axis_index("x"),
            first.astype(jnp.int32),
        ]
    ).astype(jnp.int32)
    even = lax.axis_index("core") == 0
    low = jnp.concatenate([w_temporal, w_spatial[:3]], 0)
    high = w_spatial[3:]
    keep, give = jnp.where(even, high, low), jnp.where(even, low, high)
    before = lax.ppermute(src[1], ("x", "zh"), [(i, i + 1) for i in range(7)])
    pair = jnp.stack([keep, to_sibling(give)])
    ring = jnp.stack([pair] + exchange(("z", "y"), [pair] * 3))
    late_ring, before = lax.optimization_barrier((ring, before))
    rings = {3: late_ring, 1: ring, 2: ring}
    pieces = [ring] + [along(rings[o], ("y", "z"), o) for o in OUTER[1:]]
    frames = jnp.concatenate([jnp.where(first, src[0], before)[None], src], 0)
    sib_frames = to_sibling(frames)
    act_t, shifted, pairs_mine, pairs_theirs = call(
        prepare_kernel, 16, 3,
        [((512, 960), bf16), ((3, 192, 1536), bf16), ((5, 160, 256), bf16), ((5, 160, 256), bf16)],
        [pltpu.VMEM((6, 160, 512), f32)],
        pos, frames, sib_frames, c,
    )
    pairs_theirs = to_sibling(pairs_theirs)
    pieces[0], act_t = lax.optimization_barrier((pieces[0], act_t))
    sib_pieces = [to_sibling(piece) for piece in pieces]
    (weights,) = call(
        assemble_kernel, 4, 2, [((12, 512, 512), bf16)], [pltpu.SemaphoreType.DMA((32,))],
        pos, *pieces, any_from=1,
    )
    terms, edge, mine, theirs, weights = call(
        temporal_grad_kernel, 24, 5,
        [
            ((3, 160, 512), bf16), ((160, 512), bf16), ((3, 160, 256), bf16), ((3, 160, 256), bf16),
            ((12, 512, 512), bf16),
        ],
        [pltpu.VMEM((3, 4, 160, 512), f32), pltpu.SemaphoreType.DMA((32,))],
        pos, c, weights, *sib_pieces, any_from=3, aliases={2: 4},
    )
    theirs = to_sibling(theirs)
    (one,) = call(
        spatial_weight_grad_kernel, 20, 4,
        [((9, 512, 256), f32)], [pltpu.VMEM((6, 192, 768), bf16)],
        pos, act_t, mine, theirs,
    )
    (sp,) = call(
        spatial_conv_kernel, 16, 4, [((3, 160, 512), bf16)], [pltpu.VMEM((480, 512), f32)],
        pos, shifted, weights,
    )
    sib_sp = to_sibling(sp)
    grads = call(
        temporal_weight_grad_kernel, 28, 2,
        [((12, 128, 256), f32)] + [((12, 128, 256), bf16)] * 3,
        [pltpu.VMEM((512, 640), bf16), pltpu.VMEM((512, 640), bf16), pltpu.VMEM((4, 512, 256), f32)],
        pos, sp, sib_sp, pairs_mine, pairs_theirs, one,
    )
    received = exchange(("x", "y"), grads[1:])
    sp, edge, _ = lax.optimization_barrier((sp, edge, grads[0]))
    after = lax.ppermute(edge, ("x", "zh"), [(i, i - 1) for i in range(1, 8)])
    (decoded,) = call(
        decode_kernel, 20, 2, [((4, 160, 512), bf16)], [pltpu.VMEM((3, 3, 160, 512), f32)],
        pos, src, sp, weights,
    )
    (grad_input,) = call(
        input_grad_kernel, 20, 4, [((2, 160, 512), bf16)],
        [pltpu.VMEM((2, 192, 1536), bf16), pltpu.VMEM((320, 512), f32)],
        pos, src, c, terms, after, weights,
    )
    *received, decoded, grad_input = lax.optimization_barrier((*received, decoded, grad_input))
    two = call(
        second_exchange_kernel, 12, 1, [((3, 128, 256), f32)] + [((3, 128, 256), bf16)] * 3, [],
        pos, grads[0], *received,
    )
    rows_mine, rows_theirs = call(
        core_rows_kernel, 8, 1, [((3, 4, 16, 256), f32)] * 2, [],
        pos, two[0], *exchange(("y", "x"), two[1:]),
    )
    zs = call(
        third_exchange_kernel, 8, 1, [((3, 16, 512), f32)] + [((3, 16, 512), bf16)] * 3, [],
        pos, rows_mine, to_sibling(rows_theirs),
    )
    total = zs[0] + sum(part.astype(f32) for part in exchange(("z", "z"), zs[1:]))
    total = total.astype(bf16)
    other = lax.ppermute(total, "zh", [(0, 1), (1, 0)])
    taps = (total.astype(f32) + other.astype(f32)) * (1.0 / math.sqrt(256 * 640))
    taps = taps.astype(bf16)
    grad_s, grad_t = call(
        final_taps_kernel, 4, 1,
        [((9, 16, 512), f32), ((3, 16, 512), f32)],
        [pltpu.VMEM((12, 16, 512), f32)],
        pos, taps, *[along(taps, ("x", "x"), o) for o in OUTER[1:]],
    )
    return (
        decoded.reshape(1, 4, 10, 16, 512),
        grad_input.reshape(1, 2, 10, 16, 512),
        grad_s,
        grad_t,
    )


def solution(mesh):
    physical = Mesh(mesh.devices.reshape(SIZES), AXES)
    dp, tm = ("y", "zl", "core"), ("x", "zh")
    values, weights = P(dp, tm, None, None, None), P(None, dp, None)
    return jax.shard_map(
        per_device,
        mesh=physical,
        in_specs=(values, values, weights, weights),
        out_specs=(values, values, weights, weights),
        check_vma=False,
    )
```
